32 devices in a mesh: dp: 8 (over z, y), row: 2 (over core), col: 2 (over x).
Axes of the slice: x: 2, y: 2, z: 4, core: 2. Of those that a mesh axis runs over, the one named last changes fastest.
Arguments:
- tokens: bfloat16 [32768, 1024], P('dp', ('row', 'col')), may hold values from -6 to 6
- first_gain: float32 [1024], P(('row', 'col')), may hold values from 0.5 to 1.5
- first_shift: float32 [1024], P(('row', 'col')), may hold values from -3 to 3
- joined_weight: bfloat16 [1024, 3072], P('row', 'col'), may hold values from -0.1875 to 0.1875
- query_value_bias: float32 [16, 128], P(('col', 'row')), may hold values from -3 to 3
- output_weight: bfloat16 [1024, 1024], P('col', 'row'), may hold values from -0.375 to 0.375
- output_bias: float32 [1024], P(('row', 'col')), may hold values from -3 to 3
- second_gain: float32 [1024], P(('row', 'col')), may hold values from 0.5 to 1.5
- second_shift: float32 [1024], P(('row', 'col')), may hold values from -3 to 3
- up_weight: bfloat16 [1024, 4096], P('row', 'col'), may hold values from -0.1875 to 0.1875
- up_bias: float32 [4096], P(('col', 'row')), may hold values from -3 to 3
- down_weight: bfloat16 [4096, 1024], P('col', 'row'), may hold values from -0.09375 to 0.09375
- down_bias: float32 [1024], P(('row', 'col')), may hold values from -3 to 3
- out_grad: bfloat16 [32768, 1024], P('dp', ('row', 'col')), may hold values from -6 to 6
Outputs:
- result: bfloat16 [32768, 1024], P('dp', ('row', 'col'))
- tokens_grad: float32 [32768, 1024], P('dp', ('row', 'col'))
- first_gain_grad: float32 [1024], P(('row', 'col'))
- first_shift_grad: float32 [1024], P(('row', 'col'))
- joined_weight_grad: float32 [1024, 3072], P('row', 'col')
- query_value_bias_grad: float32 [16, 128], P(('col', 'row'))
- output_weight_grad: float32 [1024, 1024], P('col', 'row')
- output_bias_grad: float32 [1024], P(('row', 'col'))
- second_gain_grad: float32 [1024], P(('row', 'col'))
- second_shift_grad: float32 [1024], P(('row', 'col'))
- up_weight_grad: float32 [1024, 4096], P('row', 'col')
- up_bias_grad: float32 [4096], P(('col', 'row'))
- down_weight_grad: float32 [4096, 1024], P('col', 'row')
- down_bias_grad: float32 [1024], P(('row', 'col'))
The draws below stay inside these ranges and needn't reach their ends.
All inputs are finite; a program needn't handle non-finite values.
Results may differ from the reference program's by a relative error of at most 0.009.
Values may be sent and summed in bfloat16 or wider, within the bound.
A program may use at most 320 MiB of HBM per device.

```python
import math
import jax
import jax.numpy as jnp
from jax import lax

D = 1024
H = 16
HD = 64
FF = 4096
SEQ_LEN = 1024
TOKENS = 32768


def levels(stream_key, extent, cuts, least, high):
    factor_of = 1.0
    for dim, parts in cuts:
        draws = jax.random.uniform(jax.random.fold_in(jax.random.fold_in(stream_key, 6), dim), (parts,), jnp.float32, least / len(cuts), high / len(cuts))
        factor_of = factor_of * jnp.repeat(jnp.exp(draws), extent[dim] // parts).reshape((-1,) + (1,) * (len(extent) - 1 - dim))
    return factor_of


def centred(stream_key, extent, spread, most, shards=(), kind=jnp.bfloat16):
    array = spread * jax.random.normal(stream_key, extent, jnp.float32)
    if shards:
        array = array * levels(stream_key, extent, shards, -0.22, 0.18)
    return jnp.clip(array, -most, most).astype(kind)


def setup_inputs(seed: int = 0) -> dict:
    key_of = jax.random.split(jax.random.key(seed), 15)
    tokens = centred(key_of[0], (TOKENS, D), 1.0, 6.0, ((0, 8), (1, 4)))
    first_gain = jnp.clip(1.0 + 0.1 * jax.random.normal(key_of[1], (D,), jnp.float32), 0.5, 1.5)
    first_shift = centred(key_of[2], (D,), 0.3, 3.0, ((0, 4),), jnp.float32)
    joined_weight = centred(key_of[3], (D, 3 * D), D ** -0.5, 0.1875, ((0, 2), (1, 2)))
    query_value_bias = centred(key_of[4], (H, 2 * HD), 0.3, 3.0, ((0, 4),), jnp.float32)
    output_weight = centred(key_of[5], (D, D), (D // 4) ** -0.5, 0.375, ((0, 2), (1, 2)))
    output_bias = centred(key_of[6], (D,), 0.3, 3.0, ((0, 4),), jnp.float32)
    second_gain = jnp.clip(1.0 + 0.1 * jax.random.normal(key_of[7], (D,), jnp.float32), 0.5, 1.5)
    second_shift = centred(key_of[8], (D,), 0.3, 3.0, ((0, 4),), jnp.float32)
    up_weight = centred(key_of[9], (D, FF), D ** -0.5, 0.1875, ((0, 2), (1, 2)))
    up_bias = centred(key_of[10], (FF,), 0.3, 3.0, ((0, 4),), jnp.float32)
    down_weight = centred(key_of[11], (FF, D), FF ** -0.5, 0.09375, ((0, 2), (1, 2)))
    down_bias = centred(key_of[12], (D,), 0.3, 3.0, ((0, 4),), jnp.float32)
    out_grad = centred(key_of[13], (TOKENS, D), 1.0, 6.0, ((0, 8), (1, 4)))
    return dict(tokens=tokens, first_gain=first_gain, first_shift=first_shift, joined_weight=joined_weight, query_value_bias=query_value_bias, output_weight=output_weight, output_bias=output_bias, second_gain=second_gain, second_shift=second_shift, up_weight=up_weight, up_bias=up_bias, down_weight=down_weight, down_bias=down_bias, out_grad=out_grad)


@jax.custom_vjp
def low(v):
    return lax.optimization_barrier(v.astype(jnp.bfloat16)).astype(jnp.float32)

@jax.custom_vjp
def low_back(v):
    return v

def low_keep(v):
    return (low(v), None)

def low_pass(kept, grad):
    return (grad,)

def back_keep(v):
    return (v, None)

def back_low(kept, grad):
    return (low(grad),)
low.defvjp(low_keep, low_pass)
low_back.defvjp(back_keep, back_low)
EPSILON = 1e-05

def matmul(left, right):
    return jnp.dot(left, right, precision=lax.Precision.HIGHEST, preferred_element_type=jnp.float32)

def layer_norm(inputs, norm_gain, norm_shift):
    average = lax.optimization_barrier(jnp.mean(inputs, axis=-1, keepdims=True))
    variance = lax.optimization_barrier(jnp.mean(jnp.square(inputs - average), axis=-1, keepdims=True))
    return (inputs - average) * lax.rsqrt(variance + EPSILON) * norm_gain + norm_shift

def attend_one(triple):
    queries, key_rows, value_rows = triple
    raw_scores = jnp.einsum('qhd,khd->hqk', queries, key_rows, precision=lax.Precision.HIGHEST)
    positions = jnp.arange(SEQ_LEN)
    distance = (positions[:, None] - positions[None, :]).astype(jnp.float32)
    slopes = jnp.exp2(-8.0 * (jnp.arange(H).astype(jnp.float32) + 1.0) / H)
    scores = low_back(raw_scores * HD ** (-0.5) - slopes[:, None, None] * distance)
    scores = jnp.where(distance >= 0, scores, -1e+30)
    soft_weights = low(jax.nn.softmax(scores, axis=-1))
    return jnp.einsum('hqk,khd->qhd', soft_weights, value_rows, precision=lax.Precision.HIGHEST)

def forward(inputs, first_gain, first_shift, joined_weight, query_value_bias, output_weight, output_bias, second_gain, second_shift, up_weight, up_bias, down_weight, down_bias):
    seq_count = inputs.shape[0] // SEQ_LEN
    normed_first = low(layer_norm(inputs, first_gain, first_shift))
    pair_bias = query_value_bias.reshape(H, 2, HD)
    zero_block = jnp.zeros((H, 1, HD), inputs.dtype)
    full_bias = jnp.concatenate([pair_bias[:, :1], zero_block, pair_bias[:, 1:]], axis=1).reshape(3 * D)
    joined_rows = low(low_back(matmul(normed_first, joined_weight) + full_bias))
    joined_rows = joined_rows.reshape(seq_count, SEQ_LEN, H, 3, HD)
    attended = lax.map(jax.checkpoint(attend_one), (joined_rows[:, :, :, 0], joined_rows[:, :, :, 1], joined_rows[:, :, :, 2]))
    attended = low(low_back(attended.reshape(-1, D)))
    hidden = inputs + low_back(matmul(attended, output_weight)) + output_bias
    normed_second = low(layer_norm(hidden, second_gain, second_shift))
    preact = low_back(matmul(normed_second, up_weight) + up_bias)
    activated = low(jax.nn.gelu(preact, approximate=True))
    return hidden + low_back(matmul(activated, down_weight)) + down_bias

def reference(tokens, first_gain, first_shift, joined_weight, query_value_bias, output_weight, output_bias, second_gain, second_shift, up_weight, up_bias, down_weight, down_bias, out_grad):
    params = tuple((member.astype(jnp.float32) for member in (first_gain, first_shift, joined_weight, query_value_bias, output_weight, output_bias, second_gain, second_shift, up_weight, up_bias, down_weight, down_bias)))
    seqs_all = tokens.shape[0] // SEQ_LEN
    group_size = math.gcd(seqs_all, max(1, 4096 // SEQ_LEN))
    turns = seqs_all // group_size
    inputs_all = tokens.astype(jnp.float32).reshape(turns, group_size * SEQ_LEN, D)
    grads_all = out_grad.astype(jnp.float32).reshape(turns, group_size * SEQ_LEN, D)

    def advance(totals, pair):
        inputs_part, grads_part = pair
        output_part, pullback = jax.vjp(forward, inputs_part, *params)
        grads = pullback(grads_part)
        updated = tuple((running + added for running, added in zip(totals, grads[1:])))
        return (updated, (output_part, grads[0]))
    initial = tuple((jnp.zeros_like(member) for member in params))
    totals, (outputs, input_grads) = lax.scan(advance, initial, (inputs_all, grads_all))
    return (outputs.reshape(-1, D).astype(jnp.bfloat16), input_grads.reshape(-1, D), totals[0], totals[1], totals[2], totals[3], totals[4], totals[5], totals[6], totals[7], totals[8], totals[9], totals[10], totals[11])
```

```python
import math
from functools import partial

import jax
import jax.numpy as jnp
from jax import lax
from jax.experimental import pallas as pl
from jax.experimental.pallas import tpu as pltpu
from jax.sharding import PartitionSpec as P

D = 1024
H = 16
HD = 64
FF = 4096
SEQ_LEN = 1024
QB = 256
EPSILON = 1e-05
L2E = math.log2(math.e)
BF = jnp.bfloat16
F32 = jnp.float32


def bdot(a, b, ca, cb):
    return lax.dot_general(a, b, (((ca,), (cb,)), ((), ())), preferred_element_type=F32)


def bias_cols(slope, n):
    j = lax.broadcasted_iota(jnp.int32, (n, HD), 0).astype(F32)
    lane = lax.broadcasted_iota(jnp.int32, (n, HD), 1)
    full = j * (slope * 8.0)
    hi = full.astype(BF)
    rest = full - hi.astype(F32)
    mid = rest.astype(BF)
    low = (rest - mid.astype(F32)).astype(BF)
    return jnp.where(lane == 0, hi, jnp.where(lane == 1, mid, jnp.where(lane == 2, low, jnp.zeros_like(hi))))


def block_scores(keys, queries, stop, i):
    z = bdot(keys[:stop], queries[i * QB : (i + 1) * QB], 1, 1) * (HD ** (-0.5) * L2E)
    row = lax.broadcasted_iota(jnp.int32, (QB, QB), 0)
    col = lax.broadcasted_iota(jnp.int32, (QB, QB), 1)
    last = jnp.where(row <= col, z[stop - QB :], -1e30)
    return last if stop == QB else jnp.concatenate([z[: stop - QB], last], 0)


def attend_kernel(slopes, x_ref, o_ref, lse_ref):
    n = x_ref.shape[0]
    pair = pl.program_id(0)
    ones = jnp.ones((n, HD), BF)
    heads = []
    for t in range(2):
        base = 3 * HD * t
        q, k, v = (x_ref[:, base + HD * s : base + HD * (s + 1)] for s in range(3))
        keys = jnp.concatenate([k, bias_cols(slopes[2 * pair + t], n)], 1)
        queries = jnp.concatenate([q, ones], 1)
        pieces = []
        for i in range(n // QB):
            stop = QB * (i + 1)
            z = block_scores(keys, queries, stop, i)
            top = jnp.max(z, 0, keepdims=True)
            p = jnp.exp2(z - top)
            total = jnp.sum(p, 0, keepdims=True)
            pieces.append((bdot(v[:stop], p.astype(BF), 0, 0) / total).T)
            lse_ref[0, t : t + 1, i * QB : stop] = top + jnp.log2(total)
        heads.append(jnp.concatenate(pieces, 0))
    o_ref[...] = jnp.concatenate(heads, 1).astype(BF)


def attend(slopes, joined):
    n, width = joined.shape
    pairs = width // (6 * HD)
    return pl.pallas_call(
        attend_kernel,
        grid_spec=pltpu.PrefetchScalarGridSpec(
            num_scalar_prefetch=1,
            grid=(pairs,),
            in_specs=[pl.BlockSpec((n, 6 * HD), lambda h, s: (0, h))],
            out_specs=[
                pl.BlockSpec((n, 2 * HD), lambda h, s: (0, h)),
                pl.BlockSpec((1, 2, n), lambda h, s: (h, 0, 0)),
            ],
        ),
        out_shape=[
            jax.ShapeDtypeStruct((n, pairs * 2 * HD), BF),
            jax.ShapeDtypeStruct((pairs, 2, n), F32),
        ],
        compiler_params=pltpu.CompilerParams(vmem_limit_bytes=40 << 20),
        cost_estimate=pl.CostEstimate(
            flops=32 * n * n * HD * pairs, bytes_accessed=n * 512 * pairs * 2, transcendentals=n * n * pairs
        ),
        name="attend",
    )(slopes, joined)


def attend_back_kernel(slopes, x_ref, do_ref, lse_ref, dx_ref, dk_ref, dv_ref):
    n = x_ref.shape[0]
    pair = pl.program_id(0)
    ones = jnp.ones((n, HD), BF)
    parts = []
    for t in range(2):
        base = 3 * HD * t
        q, k, v = (x_ref[:, base + HD * s : base + HD * (s + 1)] for s in range(3))
        do = do_ref[:, HD * t : HD * (t + 1)]
        keys = jnp.concatenate([k, bias_cols(slopes[2 * pair + t], n)], 1)
        queries = jnp.concatenate([q, ones], 1)
        dq = []
        for i in reversed(range(n // QB)):
            stop = QB * (i + 1)
            rows = slice(i * QB, stop)
            z = block_scores(keys, queries, stop, i)
            p = jnp.exp2(z - lse_ref[0, t : t + 1, rows])
            dp = bdot(v[:stop], do[rows], 1, 1)
            total = jnp.sum(p * dp, 0, keepdims=True)
            ds = (p * (dp - total)).astype(BF)
            dq.append(bdot(k[:stop], ds, 0, 0).T)
            dk = bdot(ds, q[rows], 1, 0)
            dv = bdot(p.astype(BF), do[rows], 1, 0)
            if stop == n:
                dk_ref[...] = dk
                dv_ref[...] = dv
            else:
                dk_ref[:stop] += dk
                dv_ref[:stop] += dv
        scale = HD ** (-0.5)
        parts += [jnp.concatenate(dq[::-1], 0) * scale, dk_ref[...] * scale, dv_ref[...]]
    dx_ref[...] = jnp.concatenate(parts, 1).astype(BF)


def attend_back(slopes, joined, out_grads, lse):
    n, width = joined.shape
    pairs = width // (6 * HD)
    return pl.pallas_call(
        attend_back_kernel,
        grid_spec=pltpu.PrefetchScalarGridSpec(
            num_scalar_prefetch=1,
            grid=(pairs,),
            in_specs=[
                pl.BlockSpec((n, 6 * HD), lambda h, s: (0, h)),
                pl.BlockSpec((n, 2 * HD), lambda h, s: (0, h)),
                pl.BlockSpec((1, 2, n), lambda h, s: (h, 0, 0)),
            ],
            out_specs=pl.BlockSpec((n, 6 * HD), lambda h, s: (0, h)),
            scratch_shapes=[pltpu.VMEM((n, HD), F32)] * 2,
        ),
        out_shape=jax.ShapeDtypeStruct(joined.shape, BF),
        compiler_params=pltpu.CompilerParams(vmem_limit_bytes=40 << 20),
        cost_estimate=pl.CostEstimate(
            flops=80 * n * n * HD * pairs, bytes_accessed=n * 1024 * pairs * 2, transcendentals=n * n * pairs
        ),
        name="attend_back",
    )(slopes, joined, out_grads, lse)


def swap(values, axis):
    return lax.ppermute(values, axis, [(0, 1), (1, 0)])


def mesh_bits(count):
    return [1 << b for b in range(count.bit_length() - 1)]


def side_by_side(flag, mine, other, axis):
    return jnp.where(
        flag, jnp.concatenate([other, mine], axis), jnp.concatenate([mine, other], axis)
    )


def to_sequence(block, row, col):
    n, width = block.shape
    parts = block.reshape(2, 2, n // 4, width)
    own = lax.dynamic_index_in_dim(parts, col, 1, False)
    got = swap(lax.dynamic_index_in_dim(parts, 1 - col, 1, False), "col")
    half = side_by_side(col == 1, own, got, 2)
    mine = lax.dynamic_index_in_dim(half, row, 0, False)
    other = swap(lax.dynamic_index_in_dim(half, 1 - row, 0, False), "row")
    return jnp.concatenate([mine, other], 1)


def from_sequence(values, row, col):
    n, width = values.shape
    mine, send = values[:, : width // 2], values[:, width // 2 :]
    got = swap(send, "row")
    half = jnp.where(row == 1, jnp.stack([got, mine]), jnp.stack([mine, got]))
    parts = half.reshape(2, n, 2, width // 4)
    own = lax.dynamic_index_in_dim(parts, col, 2, False)
    got = swap(lax.dynamic_index_in_dim(parts, 1 - col, 2, False), "col")
    return side_by_side(col == 1, own[:, None], got[:, None], 1).reshape(4 * n, width // 4)


def whole_weight(block):
    across = swap(block, "col")
    return block, across, swap(block, "row"), swap(across, "row")


def put(quarters, row_dim):
    own, across, below, both = quarters
    if row_dim == 0:
        return jnp.concatenate([jnp.concatenate([own, across], 1), jnp.concatenate([below, both], 1)], 0)
    return jnp.concatenate([jnp.concatenate([own, below], 1), jnp.concatenate([across, both], 1)], 0)


def halves(values, dim):
    n = values.shape[dim] // 2
    return lax.slice_in_dim(values, 0, n, axis=dim), lax.slice_in_dim(values, n, 2 * n, axis=dim)


def reduce_weight(grad, row_dim, dp_size):
    mine, send = halves(grad, row_dim)
    mine = mine.astype(F32) + swap(send.astype(BF), "row").astype(F32)
    mine, send = halves(mine, 1 - row_dim)
    mine = mine + swap(send.astype(BF), "col").astype(F32)
    place = lax.axis_index("dp")
    bits = mesh_bits(dp_size)
    for bit in bits:
        upper = (place // bit) % 2 == 1
        low, high = halves(mine, 0)
        send = jnp.where(upper, low, high).astype(BF)
        mine = jnp.where(upper, high, low) + lax.ppermute(
            send, "dp", [(i, i ^ bit) for i in range(dp_size)]
        ).astype(F32)
    mine = mine.astype(BF)
    for bit in bits[::-1]:
        upper = (place // bit) % 2 == 1
        got = lax.ppermute(mine, "dp", [(i, i ^ bit) for i in range(dp_size)])
        mine = side_by_side(upper, mine, got, 0)
    return mine.astype(F32)


def normed(values, gain, shift):
    average = jnp.mean(values, axis=1, keepdims=True)
    away = values - average
    scale = lax.rsqrt(jnp.mean(away * away, axis=1, keepdims=True) + EPSILON)
    centered = away * scale
    return centered, scale, (centered * gain + shift).astype(BF)


def norm_backward(upstream, centered, scale, gain):
    scaled = upstream * gain
    back = scale * (
        scaled
        - jnp.mean(scaled, axis=1, keepdims=True)
        - centered * jnp.mean(scaled * centered, axis=1, keepdims=True)
    )
    return back, jnp.sum(upstream * centered, axis=0), jnp.sum(upstream, axis=0)


def local(
    dp_size,
    tokens,
    first_gain,
    first_shift,
    joined_weight,
    query_value_bias,
    output_weight,
    output_bias,
    second_gain,
    second_shift,
    up_weight,
    up_bias,
    down_weight,
    down_bias,
    out_grad,
):
    row, col = lax.axis_index("row"), lax.axis_index("col")
    heads = query_value_bias.shape[0] * 4
    small = jnp.concatenate(
        [
            first_gain,
            first_shift,
            output_bias,
            second_gain,
            second_shift,
            down_bias,
            up_bias,
            query_value_bias.reshape(-1),
        ]
    )
    by_row = jnp.stack([small, swap(small, "row")])
    small = jnp.stack([by_row, swap(by_row, "col")], 1)

    def feature_vector(k):
        part = small[:, :, 256 * k : 256 * (k + 1)]
        part = jnp.where(col == 1, part[:, ::-1], part)
        return part.reshape(-1)

    def hidden_vector(start, size):
        part = small[:, :, start : start + size]
        part = jnp.where(row == 1, part[::-1], part)
        return part.transpose(1, 0, 2).reshape(-1)

    g1, s1, ob, g2, s2, db = (feature_vector(k) for k in range(6))
    ub = hidden_vector(6 * 256, up_bias.shape[0])
    pair_bias = hidden_vector(6 * 256 + up_bias.shape[0], query_value_bias.size).reshape(heads, 2, HD)
    qv_bias = jnp.concatenate(
        [pair_bias[:, :1], jnp.zeros((heads, 1, HD), F32), pair_bias[:, 1:]], axis=1
    ).reshape(-1)
    head_ids = (jnp.arange(heads) + col * (heads // 2)) % heads
    slopes = jnp.exp2(-8.0 * (head_ids.astype(F32) + 1.0) / heads)

    inputs = to_sequence(tokens, row, col).astype(F32)
    wj = put(whole_weight(joined_weight), 0)
    wo = put(whole_weight(output_weight), 1)
    wu = put(whole_weight(up_weight), 0)
    og = to_sequence(out_grad, row, col)
    wd = put(whole_weight(down_weight), 1)

    centered_first, scale_first, normed_first = normed(inputs, g1, s1)
    joined = (jnp.dot(normed_first, wj, preferred_element_type=F32) + qv_bias).astype(BF)
    attended, lse = attend(slopes, joined)
    hidden = inputs + jnp.dot(attended, wo, preferred_element_type=F32) + ob
    centered_second, scale_second, normed_second = normed(hidden, g2, s2)
    preact = jnp.dot(normed_second, wu, preferred_element_type=F32) + ub
    activated = jax.nn.gelu(preact, approximate=True).astype(BF)
    outcome = hidden + jnp.dot(activated, wd, preferred_element_type=F32) + db
    result = from_sequence(outcome.astype(BF), row, col)

    upstream = og.astype(F32)
    down_bias_grad = jnp.sum(upstream, axis=0)
    down_weight_grad = reduce_weight(bdot(activated, og, 0, 0).astype(BF), 1, dp_size)
    activated_grad = bdot(og, wd, 1, 1)
    _, gelu_pull = jax.vjp(partial(jax.nn.gelu, approximate=True), preact)
    preact_grad = gelu_pull(activated_grad)[0].astype(BF)
    up_bias_grad = jnp.sum(preact_grad.astype(F32), axis=0)
    up_weight_grad = reduce_weight(bdot(normed_second, preact_grad, 0, 0).astype(BF), 0, dp_size)
    normed_second_grad = bdot(preact_grad, wu, 1, 1)
    back_second, second_gain_grad, second_shift_grad = norm_backward(
        normed_second_grad, centered_second, scale_second, g2
    )
    hidden_grad = upstream + back_second
    output_bias_grad = jnp.sum(hidden_grad, axis=0)
    branch = hidden_grad.astype(BF)
    output_weight_grad = reduce_weight(bdot(attended, branch, 0, 0).astype(BF), 1, dp_size)
    attended_grad = bdot(branch, wo, 1, 1).astype(BF)
    joined_grad = attend_back(slopes, joined, attended_grad, lse)
    column_sums = jnp.sum(joined_grad.astype(F32), axis=0).reshape(heads, 3, HD)
    query_value_bias_grad = jnp.stack([column_sums[:, 0], column_sums[:, 2]], axis=1).reshape(-1)
    joined_weight_grad = reduce_weight(bdot(normed_first, joined_grad, 0, 0).astype(BF), 0, dp_size)
    normed_first_grad = bdot(joined_grad, wj, 1, 1)
    back_first, first_gain_grad, first_shift_grad = norm_backward(
        normed_first_grad, centered_first, scale_first, g1
    )
    tokens_grad = from_sequence((hidden_grad + back_first).astype(BF), row, col).astype(F32)

    features = jnp.stack(
        [
            first_gain_grad,
            first_shift_grad,
            output_bias_grad,
            second_gain_grad,
            second_shift_grad,
            down_bias_grad,
        ]
    ).reshape(6, 2, 2, D // 4)
    features = jnp.where(col == 1, features[:, :, ::-1], features)
    features = features.transpose(1, 2, 0, 3).reshape(2, 2, -1)

    def hidden_parts(values):
        values = values.reshape(2, 2, -1)
        values = jnp.where(row == 1, values[:, ::-1], values)
        return values.transpose(1, 0, 2)

    totals = jnp.concatenate(
        [features, hidden_parts(up_bias_grad), hidden_parts(query_value_bias_grad)], 2
    )
    totals = totals[0] + swap(totals[1], "row")
    totals = totals[0] + swap(totals[1], "col")
    for bit in mesh_bits(dp_size):
        totals = totals + lax.ppermute(totals, "dp", [(i, i ^ bit) for i in range(dp_size)])
    w = D // 4
    fg, fs, obg, sg, ss, dbg = (totals[w * k : w * (k + 1)] for k in range(6))
    ubg = totals[6 * w : 6 * w + up_bias.shape[0]]
    qvg = totals[6 * w + up_bias.shape[0] :].reshape(query_value_bias.shape)
    return (
        result,
        tokens_grad,
        fg,
        fs,
        joined_weight_grad,
        qvg,
        output_weight_grad,
        obg,
        sg,
        ss,
        up_weight_grad,
        ubg,
        down_weight_grad,
        dbg,
    )


def solution(mesh):
    feature = P(("row", "col"))
    in_specs = (
        P("dp", ("row", "col")),
        feature,
        feature,
        P("row", "col"),
        P(("col", "row"), None),
        P("col", "row"),
        feature,
        feature,
        feature,
        P("row", "col"),
        P(("col", "row")),
        P("col", "row"),
        feature,
        P("dp", ("row", "col")),
    )
    out_specs = (
        P("dp", ("row", "col")),
        P("dp", ("row", "col")),
        feature,
        feature,
        P("row", "col"),
        P(("col", "row"), None),
        P("col", "row"),
        feature,
        feature,
        feature,
        P("row", "col"),
        P(("col", "row")),
        P("col", "row"),
        feature,
    )
    return jax.shard_map(
        partial(local, mesh.shape["dp"]),
        mesh=mesh,
        in_specs=in_specs,
        out_specs=out_specs,
        check_vma=False,
    )
```

```python
import math
from functools import partial

import jax
import jax.numpy as jnp
from jax import lax
from jax.experimental import pallas as pl
from jax.experimental.pallas import tpu as pltpu
from jax.sharding import PartitionSpec as P

D = 1024
H = 16
HD = 64
FF = 4096
SEQ_LEN = 1024
QB = 256
EPSILON = 1e-05
L2E = math.log2(math.e)
BF = jnp.bfloat16
F32 = jnp.float32
MESH = pl.DeviceIdType.MESH


def bdot(a, b, ca, cb):
    return lax.dot_general(a, b, (((ca,), (cb,)), ((), ())), preferred_element_type=F32)


def bias_cols(slope, n):
    j = lax.broadcasted_iota(jnp.int32, (n, HD), 0).astype(F32)
    lane = lax.broadcasted_iota(jnp.int32, (n, HD), 1)
    full = j * (slope * 8.0)
    hi = full.astype(BF)
    rest = full - hi.astype(F32)
    mid = rest.astype(BF)
    low = (rest - mid.astype(F32)).astype(BF)
    return jnp.where(lane == 0, hi, jnp.where(lane == 1, mid, jnp.where(lane == 2, low, jnp.zeros_like(hi))))


def block_scores(keys, queries, stop, i):
    z = bdot(keys[:stop], queries[i * QB : (i + 1) * QB], 1, 1) * (HD ** (-0.5) * L2E)
    row = lax.broadcasted_iota(jnp.int32, (QB, QB), 0)
    col = lax.broadcasted_iota(jnp.int32, (QB, QB), 1)
    last = jnp.where(row <= col, z[stop - QB :], -1e30)
    return last if stop == QB else jnp.concatenate([z[: stop - QB], last], 0)


def attend_step(slopes, x_ref, o_ref, lse_ref):
    n = x_ref.shape[0]
    pair = pl.program_id(0)
    ones = jnp.ones((n, HD), BF)
    heads = []
    for t in range(2):
        base = 3 * HD * t
        q, k, v = (x_ref[:, base + HD * s : base + HD * (s + 1)] for s in range(3))
        keys = jnp.concatenate([k, bias_cols(slopes[2 * pair + t], n)], 1)
        queries = jnp.concatenate([q, ones], 1)
        pieces = []
        for i in range(n // QB):
            stop = QB * (i + 1)
            z = block_scores(keys, queries, stop, i)
            top = jnp.max(z, 0, keepdims=True)
            p = jnp.exp2(z - top)
            total = jnp.sum(p, 0, keepdims=True)
            pieces.append((bdot(v[:stop], p.astype(BF), 0, 0) / total).T)
            lse_ref[0, t : t + 1, i * QB : stop] = top + jnp.log2(total)
        heads.append(jnp.concatenate(pieces, 0))
    o_ref[...] = jnp.concatenate(heads, 1).astype(BF)


def attend_back_step(slopes, x_ref, do_ref, lse_ref, dx_ref, dk_ref, dv_ref):
    n = x_ref.shape[0]
    pair = pl.program_id(0)
    ones = jnp.ones((n, HD), BF)
    parts = []
    for t in range(2):
        base = 3 * HD * t
        q, k, v = (x_ref[:, base + HD * s : base + HD * (s + 1)] for s in range(3))
        do = do_ref[:, HD * t : HD * (t + 1)]
        keys = jnp.concatenate([k, bias_cols(slopes[2 * pair + t], n)], 1)
        queries = jnp.concatenate([q, ones], 1)
        dq = []
        for i in reversed(range(n // QB)):
            stop = QB * (i + 1)
            rows = slice(i * QB, stop)
            z = block_scores(keys, queries, stop, i)
            p = jnp.exp2(z - lse_ref[0, t : t + 1, rows])
            dp = bdot(v[:stop], do[rows], 1, 1)
            total = jnp.sum(p * dp, 0, keepdims=True)
            ds = (p * (dp - total)).astype(BF)
            dq.append(bdot(k[:stop], ds, 0, 0).T)
            dk = bdot(ds, q[rows], 1, 0)
            dv = bdot(p.astype(BF), do[rows], 1, 0)
            if stop == n:
                dk_ref[...] = dk
                dv_ref[...] = dv
            else:
                dk_ref[:stop] += dk
                dv_ref[:stop] += dv
        scale = HD ** (-0.5)
        parts += [jnp.concatenate(dq[::-1], 0) * scale, dk_ref[...] * scale, dv_ref[...]]
    dx_ref[...] = jnp.concatenate(parts, 1).astype(BF)


class Place:
    def __init__(self, dp_size):
        self.row = lax.axis_index("row")
        self.col = lax.axis_index("col")
        self.dp = lax.axis_index("dp")
        self.bits = [1 << b for b in range(dp_size.bit_length() - 1)]
        self.across = {"col": 1 - self.col}
        self.beside = {"row": 1 - self.row}
        self.diagonal = {"row": 1 - self.row, "col": 1 - self.col}
        self.flags = [lax.rem(self.dp // bit, 2) for bit in self.bits]
        self.peers = [
            {"dp": self.dp + bit - 2 * bit * flag} for bit, flag in zip(self.bits, self.flags)
        ]

    def meet(self, partners):
        barrier = pltpu.get_barrier_semaphore()
        for partner in partners:
            pl.semaphore_signal(barrier, inc=1, device_id=partner, device_id_type=MESH)
        pl.semaphore_wait(barrier, len(partners))


def send(src, dst, sems, k, device):
    return pltpu.make_async_remote_copy(
        src_ref=src,
        dst_ref=dst,
        send_sem=sems.at[0, k],
        recv_sem=sems.at[1, k],
        device_id=device,
        device_id_type=MESH,
    )


class Gather:
    def __init__(self, place, block, full, row_dim, chunks, sems, copy_sem):
        self.p, self.block, self.full, self.row_dim = place, block, full, row_dim
        self.n, self.sems, self.copy_sem = chunks, sems, copy_sem
        self.rows, self.cols = block.shape
        self.half = self.rows // 2
        self.step = self.half // chunks

    @staticmethod
    def count(chunks):
        return 1 + 4 * chunks

    def region(self, row, col, half=None, k=0):
        first, second = (row, col) if self.row_dim == 0 else (col, row)
        start = pl.multiple_of(first * self.rows, 16)
        size = self.rows
        if half is not None:
            start = pl.multiple_of(start + half * self.half + k * self.step, 16)
            size = self.step
        return self.full.at[pl.ds(start, size), pl.ds(pl.multiple_of(second * self.cols, 128), self.cols)]

    def own(self):
        return pltpu.make_async_copy(self.block, self.region(self.p.row, self.p.col), self.copy_sem)

    def beside(self, incoming):
        row = 1 - self.p.row if incoming else self.p.row
        return send(self.block, self.region(row, self.p.col), self.sems, 0, self.p.beside)

    def over(self, k, incoming):
        flag = self.p.flags[0]
        src = self.block.at[pl.ds(pl.multiple_of(flag * self.half + k * self.step, 16), self.step)]
        col = 1 - self.p.col if incoming else self.p.col
        return send(src, self.region(self.p.row, col, flag, k), self.sems, 1 + k, self.p.across)

    def relay(self, k, incoming):
        flag = self.p.flags[0]
        half = 1 - flag if incoming else flag
        src = self.region(self.p.row, 1 - self.p.col, flag, k)
        dst = self.region(self.p.row, 1 - self.p.col, half, k)
        return send(src, dst, self.sems, 1 + self.n + k, self.p.peers[0])

    def hand(self, k, second, incoming):
        flag = self.p.flags[0]
        half = 1 - flag if second else flag
        row = 1 - self.p.row if incoming else self.p.row
        src = self.region(self.p.row, 1 - self.p.col, half, k)
        dst = self.region(row, 1 - self.p.col, half, k)
        return send(src, dst, self.sems, 1 + (3 if second else 2) * self.n + k, self.p.beside)

    def start(self):
        for k in range(self.n):
            self.over(k, False).start()
        self.beside(False).start()
        self.own().start()

    def arrived(self, k):
        self.over(k, True).wait_recv()
        self.relay(k, False).start()
        self.hand(k, False, False).start()

    def relayed(self, k):
        self.relay(k, True).wait_recv()
        self.hand(k, True, False).start()

    def finish(self):
        self.own().wait()
        self.beside(False).wait_send()
        self.beside(True).wait_recv()
        for k in range(self.n):
            self.over(k, False).wait_send()
            self.relay(k, False).wait_send()
            for second in (False, True):
                self.hand(k, second, False).wait_send()
                self.hand(k, second, True).wait_recv()


class Reduce:
    AHEAD = 3

    def __init__(self, place, part, out, row_dim, chunks, refs):
        self.p, self.part, self.out, self.row_dim, self.n = place, part, out, row_dim, chunks
        self.got, self.own, self.over, self.full, *rest = refs
        levels = len(place.bits)
        self.landing, (self.load_sem, self.core_sem, self.over_sem, self.half_sem, self.back_sem, self.out_sem) = (
            rest[:levels],
            rest[levels:],
        )
        self.rows, self.cols = out.shape
        self.step = self.rows // chunks
        self.levels = levels
        self.ticks = chunks + 2 * levels

    @staticmethod
    def scratch(rows, cols, chunks, levels):
        step = rows // chunks
        return (
            [
                pltpu.VMEM((2, rows, cols), BF),
                pltpu.VMEM((2, rows, cols), BF),
                pltpu.VMEM((rows, cols), BF),
                pltpu.VMEM((rows, cols), BF),
            ]
            + [pltpu.VMEM((chunks, step >> (b + 1), cols), BF) for b in range(levels)]
            + [
                pltpu.SemaphoreType.DMA((2,)),
                pltpu.SemaphoreType.DMA((2, 2)),
                pltpu.SemaphoreType.DMA((2, chunks)),
                pltpu.SemaphoreType.DMA((2, levels * chunks)),
                pltpu.SemaphoreType.DMA((2, levels * chunks)),
                pltpu.SemaphoreType.DMA,
            ]
        )

    def quarter(self, row, col):
        first, second = (row, col) if self.row_dim == 0 else (col, row)
        return self.part.at[
            pl.ds(pl.multiple_of(first * self.rows, 16), self.rows),
            pl.ds(pl.multiple_of(second * self.cols, 128), self.cols),
        ]

    def load(self, i):
        col = self.p.col if i else 1 - self.p.col
        return pltpu.make_async_copy(self.quarter(self.p.row, col), self.own.at[col], self.load_sem.at[i])

    def beside(self, i):
        col = self.p.col if i else 1 - self.p.col
        return send(self.quarter(1 - self.p.row, col), self.got.at[col], self.core_sem, i, self.p.beside)

    def begin(self):
        for i in range(2):
            self.beside(i).start()
            self.load(i).start()

    def add_pair(self, i):
        col = self.p.col if i else 1 - self.p.col
        self.load(i).wait()
        self.beside(i).wait_recv()

        def body(k, carry):
            at = pl.ds(pl.multiple_of(k * 64, 64), 64)
            self.own[col, at] = self.own[col, at] + self.got[col, at]
            return carry

        lax.fori_loop(0, self.rows // 64, body, 0)

    def chunk(self, k):
        return pl.ds(pl.multiple_of(k * self.step, 16), self.step)

    def crossing(self, k):
        at = self.chunk(k)
        return send(self.own.at[1 - self.p.col, at], self.over.at[at], self.over_sem, k, self.p.across)

    def offset(self, level):
        return sum((self.p.flags[b] * (self.step >> (b + 1)) for b in range(level)), 0)

    def rows_at(self, k, start, size):
        return pl.ds(pl.multiple_of(k * self.step + start, 8), size)

    def halving(self, b, k):
        size = self.step >> (b + 1)
        start = self.offset(b) + (1 - self.p.flags[b]) * size
        return send(
            self.own.at[self.p.col, self.rows_at(k, start, size)],
            self.landing[b].at[k],
            self.half_sem,
            b * self.n + k,
            self.p.peers[b],
        )

    def doubling(self, b, k, incoming):
        size = self.step >> (b + 1)
        start = self.offset(b) + self.p.flags[b] * size
        other = self.offset(b) + (1 - self.p.flags[b]) * size
        at = self.full.at[self.rows_at(k, start, size)]
        to = self.full.at[self.rows_at(k, other if incoming else start, size)]
        return send(at, to, self.back_sem, b * self.n + k, self.p.peers[b])

    def first_half(self):
        self.add_pair(0)
        for k in range(min(self.AHEAD, self.n)):
            self.crossing(k).start()

    def second_half(self):
        self.add_pair(1)

    def stage(self, j, k):
        col, levels = self.p.col, self.levels
        if j == 0:
            self.crossing(k).wait_recv()
            at = self.chunk(k)
            self.own[col, at] = self.own[col, at] + self.over[at]
            self.halving(0, k).start()
        elif j <= levels:
            b = j - 1
            self.halving(b, k).wait_recv()
            size = self.step >> (b + 1)
            at = self.rows_at(k, self.offset(b + 1), size)
            total = self.own[col, at] + self.landing[b][k]
            if b + 1 < levels:
                self.own[col, at] = total
                self.halving(b + 1, k).start()
            else:
                self.full[at] = total
                self.doubling(b, k, False).start()
        else:
            b = 2 * levels - j
            self.doubling(b, k, True).wait_recv()
            if b:
                self.doubling(b - 1, k, False).start()

    def tick(self, t):
        for j in reversed(range(1 + 2 * self.levels)):

            @pl.when((t - j >= 0) & (t - j < self.n))
            def _(j=j):
                self.stage(j, t - j)

        @pl.when((t >= 0) & (t + self.AHEAD < self.n))
        def _():
            self.crossing(t + self.AHEAD).start()

    def finish(self):
        copy = pltpu.make_async_copy(self.full, self.out, self.out_sem)
        copy.start()
        for i in range(2):
            self.beside(i).wait_send()

        def body(k, carry):
            self.crossing(k).wait_send()
            for b in range(self.levels):
                self.halving(b, k).wait_send()
                self.doubling(b, k, False).wait_send()
            return carry

        lax.fori_loop(0, self.n, body, 0)
        copy.wait()


class Pipeline:
    def __init__(self, reductions):
        self.items, start = [], 2
        for item in reductions:
            self.items.append((start, item))
            start += item.n
        self.ticks = max(s + item.ticks for s, item in self.items)

    def begin(self):
        for _, item in self.items:
            item.begin()

    def advance(self, t):
        for start, item in self.items:

            @pl.when(t == start - 2)
            def _(item=item):
                item.first_half()

            @pl.when(t == start - 1)
            def _(item=item):
                item.second_half()

            item.tick(t - start)

    def drain(self, t):
        def body(i, carry):
            self.advance(i)
            return carry

        lax.fori_loop(t, self.ticks, body, 0)
        for _, item in self.items:
            item.finish()


def chunk_count(rows, dp_size, most=8):
    return max(1, min(most, rows // (16 * dp_size)))


class Spread:
    def __init__(self, place, block, whole, to_sequences, sems, copy_sem):
        self.p, self.block, self.whole, self.forward = place, block, whole, to_sequences
        self.sems, self.copy_sem = sems, copy_sem
        self.rows = whole.shape[0]
        self.cols = block.shape[1]

    def ends(self, to_row, to_col, row, col):
        if self.forward:
            seq, part = 2 * to_row + to_col, 2 * row + col
        else:
            seq, part = 2 * row + col, 2 * to_row + to_col
        narrow = self.block.at[pl.ds(pl.multiple_of(seq * self.rows, 16), self.rows)]
        wide = self.whole.at[:, pl.ds(pl.multiple_of(part * self.cols, 128), self.cols)]
        return (narrow, wide) if self.forward else (wide, narrow)

    def copy(self, k, incoming):
        p = self.p
        row, col = ((p.row, 1 - p.col), (1 - p.row, p.col), (1 - p.row, 1 - p.col))[k]
        device = (p.across, p.beside, p.diagonal)[k]
        src, dst = self.ends(row, col, p.row, p.col)
        if incoming:
            dst = self.ends(p.row, p.col, row, col)[1]
        return send(src, dst, self.sems, k, device)

    def own(self):
        p = self.p
        return pltpu.make_async_copy(*self.ends(p.row, p.col, p.row, p.col), self.copy_sem)

    def start(self):
        for k in range(3):
            self.copy(k, False).start()
        self.own().start()

    def finish(self):
        self.own().wait()
        for k in range(3):
            self.copy(k, False).wait_send()
            self.copy(k, True).wait_recv()


ANY = pl.BlockSpec(memory_space=pl.ANY)


def front_kernel(dp_size, tokens, weight, small, x, full, smalls, sems, spread_sems, small_sems, copy_sems):
    p = Place(dp_size)
    p.meet([p.across, p.beside, p.diagonal, p.peers[0]])
    gather = Gather(p, weight, full, 0, CHUNKS, sems, copy_sems.at[0])
    spread = Spread(p, tokens, x, True, spread_sems, copy_sems.at[1])
    mine = 2 * p.row + p.col
    others = (
        (2 * p.row + 1 - p.col, p.across),
        (2 * (1 - p.row) + p.col, p.beside),
        (2 * (1 - p.row) + 1 - p.col, p.diagonal),
    )
    gather.start()
    keep = pltpu.make_async_copy(small, smalls.at[mine], copy_sems.at[2])
    keep.start()
    for k, (_, device) in enumerate(others):
        send(small, smalls.at[mine], small_sems, k, device).start()
    spread.start()
    for k in range(CHUNKS):
        gather.arrived(k)
        if k:
            gather.relayed(k - 1)
    gather.relayed(CHUNKS - 1)
    keep.wait()
    for k, (index, device) in enumerate(others):
        send(small, smalls.at[mine], small_sems, k, device).wait_send()
        send(small, smalls.at[index], small_sems, k, device).wait_recv()
    gather.finish()
    spread.finish()


CHUNKS = 4


def front(dp_size, tokens, weight, small):
    rows, width = tokens.shape
    return pl.pallas_call(
        partial(front_kernel, dp_size),
        in_specs=[ANY] * 3,
        out_specs=[ANY] * 3,
        out_shape=[
            jax.ShapeDtypeStruct((rows // 4, width * 4), BF),
            jax.ShapeDtypeStruct((2 * weight.shape[0], 2 * weight.shape[1]), BF),
            jax.ShapeDtypeStruct((4,) + small.shape, F32),
        ],
        scratch_shapes=[
            pltpu.SemaphoreType.DMA((2, Gather.count(CHUNKS))),
            pltpu.SemaphoreType.DMA((2, 3)),
            pltpu.SemaphoreType.DMA((2, 3)),
            pltpu.SemaphoreType.DMA((3,)),
        ],
        compiler_params=pltpu.CompilerParams(collective_id=0, has_side_effects=True),
        name="front",
    )(tokens, weight, small)


def tail_kernel(dp_size, spec, part, grads, small, out, spread_out, small_out, *refs):
    p = Place(dp_size)
    p.meet([p.across, p.beside, p.diagonal] + p.peers)
    count = len(refs) - 8
    reduction = Reduce(p, part, out, spec[0], spec[1], refs[:count])
    spread_sems, copy_sem, four_sem, bit_sem, four, lots, mine_ref, own_sem = refs[count:]
    pipe = Pipeline([reduction])
    pipe.begin()
    others = (
        (2 * p.row + 1 - p.col, p.across),
        (2 * (1 - p.row) + p.col, p.beside),
        (2 * (1 - p.row) + 1 - p.col, p.diagonal),
    )
    load = pltpu.make_async_copy(small.at[2 * p.row + p.col], mine_ref.at[0], own_sem.at[0])
    load.start()
    for k, (index, device) in enumerate(others):
        send(small.at[index], four.at[k], four_sem, k, device).start()
    spread = Spread(p, spread_out, grads, False, spread_sems, copy_sem)
    pipe.advance(0)
    spread.start()
    load.wait()
    for k, (index, device) in enumerate(others):
        send(small.at[index], four.at[k], four_sem, k, device).wait_recv()
    mine_ref[0] = mine_ref[0] + four[0] + (four[1] + four[2])
    for b, peer in enumerate(p.peers):
        copy = send(mine_ref.at[b], lots.at[b], bit_sem, b, peer)
        copy.start()
        pipe.advance(1 + b)
        copy.wait_recv()
        mine_ref[b + 1] = mine_ref[b] + lots[b]
    small_out[...] = mine_ref[len(p.peers)]
    pipe.drain(1 + len(p.peers))
    for k, (index, device) in enumerate(others):
        send(small.at[index], four.at[k], four_sem, k, device).wait_send()
    for b, peer in enumerate(p.peers):
        send(mine_ref.at[b], lots.at[b], bit_sem, b, peer).wait_send()
    spread.finish()


def tail(dp_size, part, grads, small):
    levels = dp_size.bit_length() - 1
    rows, cols = part.shape[0] // 2, part.shape[1] // 2
    chunks = chunk_count(rows, dp_size)
    shape = small.shape[1:]
    return pl.pallas_call(
        partial(tail_kernel, dp_size, (0, chunks)),
        in_specs=[ANY] * 3,
        out_specs=[ANY, ANY, pl.BlockSpec(memory_space=pltpu.VMEM)],
        out_shape=[
            jax.ShapeDtypeStruct((rows, cols), BF),
            jax.ShapeDtypeStruct((4 * grads.shape[0], grads.shape[1] // 4), BF),
            jax.ShapeDtypeStruct(shape, F32),
        ],
        scratch_shapes=Reduce.scratch(rows, cols, chunks, levels)
        + [
            pltpu.SemaphoreType.DMA((2, 3)),
            pltpu.SemaphoreType.DMA,
            pltpu.SemaphoreType.DMA((2, 3)),
            pltpu.SemaphoreType.DMA((2, levels)),
            pltpu.VMEM((3,) + shape, F32),
            pltpu.VMEM((levels,) + shape, F32),
            pltpu.VMEM((levels + 1,) + shape, F32),
            pltpu.SemaphoreType.DMA((1,)),
        ],
        compiler_params=pltpu.CompilerParams(
            collective_id=3, has_side_effects=True, vmem_limit_bytes=48 << 20
        ),
        name="tail",
    )(part, grads, small)


GATHERED = ((1, 1), (0, 4), (1, 4))


def attend_kernel(dp_size, slopes, x_ref, *refs):
    blocks, (o_ref, lse_ref), wholes, sems = refs[:3], refs[3:5], refs[5:8], refs[8:11]
    copy_sems = refs[11]
    step = pl.program_id(0)
    p = Place(dp_size)
    gathers = [
        Gather(p, block, whole, dim, chunks, sem, copy_sems.at[i])
        for i, (block, whole, (dim, chunks), sem) in enumerate(zip(blocks, wholes, GATHERED, sems))
    ]
    items = [(g, k) for g in gathers for k in range(g.n)]

    @pl.when(step == 0)
    def _():
        p.meet([p.across, p.beside, p.peers[0]])
        for g in gathers:
            g.start()

    attend_step(slopes, x_ref, o_ref, lse_ref)
    last = pl.num_programs(0) - 1

    def move(i):
        if i < len(items):
            g, k = items[i]
            g.arrived(k)
        if 0 < i <= len(items):
            g, k = items[i - 1]
            g.relayed(k)

    for i in range(5):

        @pl.when(step == i + 2)
        def _(i=i):
            move(i)

    @pl.when(step == last)
    def _():
        for i in range(5, len(items) + 1):
            move(i)
        for g in gathers:
            g.finish()


def attend(dp_size, slopes, joined, weights):
    n, width = joined.shape
    pairs = width // (6 * HD)
    return pl.pallas_call(
        partial(attend_kernel, dp_size),
        grid_spec=pltpu.PrefetchScalarGridSpec(
            num_scalar_prefetch=1,
            grid=(pairs,),
            in_specs=[pl.BlockSpec((n, 6 * HD), lambda h, s: (0, h))] + [ANY] * 3,
            out_specs=[
                pl.BlockSpec((n, 2 * HD), lambda h, s: (0, h)),
                pl.BlockSpec((1, 2, n), lambda h, s: (h, 0, 0)),
            ]
            + [ANY] * 3,
            scratch_shapes=[pltpu.SemaphoreType.DMA((2, Gather.count(chunks))) for _, chunks in GATHERED]
            + [pltpu.SemaphoreType.DMA((3,))],
        ),
        out_shape=[
            jax.ShapeDtypeStruct((n, pairs * 2 * HD), BF),
            jax.ShapeDtypeStruct((pairs, 2, n), F32),
        ]
        + [jax.ShapeDtypeStruct((2 * w.shape[0], 2 * w.shape[1]), BF) for w in weights],
        compiler_params=pltpu.CompilerParams(
            vmem_limit_bytes=40 << 20, collective_id=1, has_side_effects=True
        ),
        cost_estimate=pl.CostEstimate(
            flops=32 * n * n * HD * pairs, bytes_accessed=n * 512 * pairs * 2, transcendentals=n * n * pairs
        ),
        name="attend",
    )(slopes, joined, *weights)


def attend_back_kernel(dp_size, specs, counts, slopes, x_ref, do_ref, lse_ref, *refs):
    k = len(specs)
    parts, dx_ref, outs, refs = refs[:k], refs[k], refs[k + 1 : 2 * k + 1], refs[2 * k + 1 :]
    dk_ref, dv_ref = refs[:2]
    refs = refs[2:]
    step, last = pl.program_id(0), pl.num_programs(0) - 1
    p = Place(dp_size)
    items = []
    for part, out, (dim, chunks), count in zip(parts, outs, specs, counts):
        items.append(Reduce(p, part, out, dim, chunks, refs[:count]))
        refs = refs[count:]
    pipe = Pipeline(items)

    @pl.when(step == 0)
    def _():
        p.meet([p.across, p.beside] + p.peers)
        pipe.begin()

    attend_back_step(slopes, x_ref, do_ref, lse_ref, dx_ref, dk_ref, dv_ref)

    @pl.when(step < last)
    def _():
        pipe.advance(step)

    @pl.when(step == last)
    def _():
        pipe.drain(last)


def attend_back(dp_size, slopes, joined, out_grads, lse, parts, dims):
    n, width = joined.shape
    pairs = width // (6 * HD)
    levels = dp_size.bit_length() - 1
    blocks = [(g.shape[0] // 2, g.shape[1] // 2) for g in parts]
    specs = tuple((dim, chunk_count(b[0], dp_size)) for dim, b in zip(dims, blocks))
    scratch = [Reduce.scratch(*b, chunks, levels) for b, (_, chunks) in zip(blocks, specs)]
    return pl.pallas_call(
        partial(attend_back_kernel, dp_size, specs, [len(s) for s in scratch]),
        grid_spec=pltpu.PrefetchScalarGridSpec(
            num_scalar_prefetch=1,
            grid=(pairs,),
            in_specs=[
                pl.BlockSpec((n, 6 * HD), lambda h, s: (0, h)),
                pl.BlockSpec((n, 2 * HD), lambda h, s: (0, h)),
                pl.BlockSpec((1, 2, n), lambda h, s: (h, 0, 0)),
            ]
            + [ANY] * len(parts),
            out_specs=[pl.BlockSpec((n, 6 * HD), lambda h, s: (0, h))] + [ANY] * len(parts),
            scratch_shapes=[pltpu.VMEM((n, HD), F32)] * 2 + sum(scratch, []),
        ),
        out_shape=[jax.ShapeDtypeStruct(joined.shape, BF)] + [jax.ShapeDtypeStruct(b, BF) for b in blocks],
        compiler_params=pltpu.CompilerParams(
            vmem_limit_bytes=60 << 20, collective_id=2, has_side_effects=True
        ),
        cost_estimate=pl.CostEstimate(
            flops=80 * n * n * HD * pairs, bytes_accessed=n * 1024 * pairs * 2, transcendentals=n * n * pairs
        ),
        name="attend_back",
    )(slopes, joined, out_grads, lse, *parts)


def swap(values, axis):
    return lax.ppermute(values, axis, [(0, 1), (1, 0)])


def side_by_side(flag, mine, other, axis):
    return jnp.where(
        flag, jnp.concatenate([other, mine], axis), jnp.concatenate([mine, other], axis)
    )


def to_sequence(block, row, col):
    n, width = block.shape
    parts = block.reshape(2, 2, n // 4, width)
    own = lax.dynamic_index_in_dim(parts, col, 1, False)
    got = swap(lax.dynamic_index_in_dim(parts, 1 - col, 1, False), "col")
    half = side_by_side(col == 1, own, got, 2)
    mine = lax.dynamic_index_in_dim(half, row, 0, False)
    other = swap(lax.dynamic_index_in_dim(half, 1 - row, 0, False), "row")
    return side_by_side(row == 1, mine, other, 1)


def from_sequence(values, row, col):
    n, width = values.shape
    parts = values.reshape(n, 2, width // 2)
    mine = lax.dynamic_index_in_dim(parts, row, 1, False)
    got = swap(lax.dynamic_index_in_dim(parts, 1 - row, 1, False), "row")
    half = side_by_side(row == 1, mine[None], got[None], 0)
    parts = half.reshape(2, n, 2, width // 4)
    own = lax.dynamic_index_in_dim(parts, col, 2, False)
    got = swap(lax.dynamic_index_in_dim(parts, 1 - col, 2, False), "col")
    return side_by_side(col == 1, own[:, None], got[:, None], 1).reshape(4 * n, width // 4)


def normed(values, gain, shift):
    average = jnp.mean(values, axis=1, keepdims=True)
    away = values - average
    scale = lax.rsqrt(jnp.mean(away * away, axis=1, keepdims=True) + EPSILON)
    centered = away * scale
    return centered, scale, (centered * gain + shift).astype(BF)


def norm_backward(upstream, centered, scale, gain):
    scaled = upstream * gain
    back = scale * (
        scaled
        - jnp.mean(scaled, axis=1, keepdims=True)
        - centered * jnp.mean(scaled * centered, axis=1, keepdims=True)
    )
    return back, jnp.sum(upstream * centered, axis=0), jnp.sum(upstream, axis=0)


def local(
    dp_size,
    tokens,
    first_gain,
    first_shift,
    joined_weight,
    query_value_bias,
    output_weight,
    output_bias,
    second_gain,
    second_shift,
    up_weight,
    up_bias,
    down_weight,
    down_bias,
    out_grad,
):
    row, col = lax.axis_index("row"), lax.axis_index("col")
    heads = query_value_bias.shape[0] * 4
    w = D // 4
    small = jnp.concatenate(
        [
            first_gain,
            first_shift,
            output_bias,
            second_gain,
            second_shift,
            down_bias,
            up_bias,
            query_value_bias.reshape(-1),
        ]
    ).reshape(-1, 128)
    x, wj, small = front(dp_size, tokens, joined_weight, small)
    small = small.reshape(2, 2, -1)
    g1, s1, ob, g2, s2, db = (small[:, :, w * k : w * (k + 1)].reshape(-1) for k in range(6))

    def hidden_vector(start, size):
        return small[:, :, start : start + size].transpose(1, 0, 2).reshape(-1)

    ub = hidden_vector(6 * w, up_bias.shape[0])
    pair_bias = hidden_vector(6 * w + up_bias.shape[0], query_value_bias.size).reshape(heads, 2, HD)
    qv_bias = jnp.concatenate(
        [pair_bias[:, :1], jnp.zeros((heads, 1, HD), F32), pair_bias[:, 1:]], axis=1
    ).reshape(-1)
    slopes = jnp.exp2(-8.0 * (jnp.arange(heads).astype(F32) + 1.0) / heads)

    inputs = x.astype(F32)
    centered_first, scale_first, normed_first = normed(inputs, g1, s1)
    joined = (jnp.dot(normed_first, wj, preferred_element_type=F32) + qv_bias).astype(BF)
    attended, lse, wo, wu, wd = attend(dp_size, slopes, joined, (output_weight, up_weight, down_weight))
    out_grad, attended = lax.optimization_barrier((out_grad, attended))
    og = to_sequence(out_grad, row, col)
    hidden = inputs + jnp.dot(attended, wo, preferred_element_type=F32) + ob
    centered_second, scale_second, normed_second = normed(hidden, g2, s2)
    preact = jnp.dot(normed_second, wu, preferred_element_type=F32) + ub
    activated = jax.nn.gelu(preact, approximate=True).astype(BF)
    outcome = hidden + jnp.dot(activated, wd, preferred_element_type=F32) + db
    result = from_sequence(outcome.astype(BF), row, col)

    upstream = og.astype(F32)
    down_bias_grad = jnp.sum(upstream, axis=0)
    down_part = bdot(activated, og, 0, 0).astype(BF)
    activated_grad = bdot(og, wd, 1, 1)
    _, gelu_pull = jax.vjp(partial(jax.nn.gelu, approximate=True), preact)
    preact_grad = gelu_pull(activated_grad)[0].astype(BF)
    up_bias_grad = jnp.sum(preact_grad.astype(F32), axis=0)
    up_part = bdot(normed_second, preact_grad, 0, 0).astype(BF)
    normed_second_grad = bdot(preact_grad, wu, 1, 1)
    back_second, second_gain_grad, second_shift_grad = norm_backward(
        normed_second_grad, centered_second, scale_second, g2
    )
    hidden_grad = upstream + back_second
    output_bias_grad = jnp.sum(hidden_grad, axis=0)
    branch = hidden_grad.astype(BF)
    output_part = bdot(attended, branch, 0, 0).astype(BF)
    attended_grad = bdot(branch, wo, 1, 1).astype(BF)
    joined_grad, down_weight_grad, up_weight_grad, output_weight_grad = attend_back(
        dp_size, slopes, joined, attended_grad, lse, (down_part, up_part, output_part), (1, 0, 1)
    )
    column_sums = jnp.sum(joined_grad.astype(F32), axis=0).reshape(heads, 3, HD)
    query_value_bias_grad = jnp.stack([column_sums[:, 0], column_sums[:, 2]], axis=1).reshape(-1)
    joined_part = bdot(normed_first, joined_grad, 0, 0).astype(BF)
    normed_first_grad = bdot(joined_grad, wj, 1, 1)
    back_first, first_gain_grad, first_shift_grad = norm_backward(
        normed_first_grad, centered_first, scale_first, g1
    )
    tokens_grad = (hidden_grad + back_first).astype(BF)

    features = jnp.stack(
        [
            first_gain_grad,
            first_shift_grad,
            output_bias_grad,
            second_gain_grad,
            second_shift_grad,
            down_bias_grad,
        ]
    ).reshape(6, 4, w)
    features = features.transpose(1, 0, 2).reshape(4, -1)

    def hidden_parts(values):
        return values.reshape(2, 2, -1).transpose(1, 0, 2).reshape(4, -1)

    totals = jnp.concatenate([features, hidden_parts(up_bias_grad), hidden_parts(query_value_bias_grad)], 1)
    joined_weight_grad, tokens_grad, totals = tail(
        dp_size, joined_part, tokens_grad, totals.reshape(4, -1, 128)
    )
    totals = totals.reshape(-1)
    fg, fs, obg, sg, ss, dbg = (totals[w * k : w * (k + 1)] for k in range(6))
    ubg = totals[6 * w : 6 * w + up_bias.shape[0]]
    qvg = totals[6 * w + up_bias.shape[0] :].reshape(query_value_bias.shape)
    return (
        result,
        tokens_grad.astype(F32),
        fg,
        fs,
        joined_weight_grad.astype(F32),
        qvg,
        output_weight_grad.astype(F32),
        obg,
        sg,
        ss,
        up_weight_grad.astype(F32),
        ubg,
        down_weight_grad.astype(F32),
        dbg,
    )


def solution(mesh):
    feature = P(("row", "col"))
    in_specs = (
        P("dp", ("row", "col")),
        feature,
        feature,
        P("row", "col"),
        P(("col", "row"), None),
        P("col", "row"),
        feature,
        feature,
        feature,
        P("row", "col"),
        P(("col", "row")),
        P("col", "row"),
        feature,
        P("dp", ("row", "col")),
    )
    out_specs = (
        P("dp", ("row", "col")),
        P("dp", ("row", "col")),
        feature,
        feature,
        P("row", "col"),
        P(("col", "row"), None),
        P("col", "row"),
        feature,
        feature,
        feature,
        P("row", "col"),
        P(("col", "row")),
        P("col", "row"),
        feature,
    )
    return jax.shard_map(
        partial(local, mesh.shape["dp"]),
        mesh=mesh,
        in_specs=in_specs,
        out_specs=out_specs,
        check_vma=False,
    )
```

```python
import math
from functools import partial

import jax
import jax.numpy as jnp
from jax import lax
from jax.experimental import pallas as pl
from jax.experimental.pallas import tpu as pltpu
from jax.sharding import PartitionSpec as P

D = 1024
H = 16
HD = 64
FF = 4096
SEQ_LEN = 1024
QB = 256
EPSILON = 1e-05
L2E = math.log2(math.e)
BF = jnp.bfloat16
F32 = jnp.float32
MESH = pl.DeviceIdType.MESH


def bdot(a, b, ca, cb):
    return lax.dot_general(a, b, (((ca,), (cb,)), ((), ())), preferred_element_type=F32)


def bias_cols(slope, n):
    j = lax.broadcasted_iota(jnp.int32, (n, HD), 0).astype(F32)
    lane = lax.broadcasted_iota(jnp.int32, (n, HD), 1)
    full = j * (slope * 8.0)
    hi = full.astype(BF)
    rest = full - hi.astype(F32)
    mid = rest.astype(BF)
    low = (rest - mid.astype(F32)).astype(BF)
    return jnp.where(lane == 0, hi, jnp.where(lane == 1, mid, jnp.where(lane == 2, low, jnp.zeros_like(hi))))


def block_scores(keys, queries, stop, i):
    z = bdot(keys[:stop], queries[i * QB : (i + 1) * QB], 1, 1) * (HD ** (-0.5) * L2E)
    row = lax.broadcasted_iota(jnp.int32, (QB, QB), 0)
    col = lax.broadcasted_iota(jnp.int32, (QB, QB), 1)
    last = jnp.where(row <= col, z[stop - QB :], -1e30)
    return last if stop == QB else jnp.concatenate([z[: stop - QB], last], 0)


def attend_step(slopes, x_ref, o_ref, lse_ref):
    n = x_ref.shape[0]
    pair = pl.program_id(0)
    ones = jnp.ones((n, HD), BF)
    heads = []
    for t in range(2):
        base = 3 * HD * t
        q, k, v = (x_ref[:, base + HD * s : base + HD * (s + 1)] for s in range(3))
        keys = jnp.concatenate([k, bias_cols(slopes[2 * pair + t], n)], 1)
        queries = jnp.concatenate([q, ones], 1)
        pieces = []
        for i in range(n // QB):
            stop = QB * (i + 1)
            z = block_scores(keys, queries, stop, i)
            top = jnp.max(z, 0, keepdims=True)
            p = jnp.exp2(z - top)
            total = jnp.sum(p, 0, keepdims=True)
            pieces.append((bdot(v[:stop], p.astype(BF), 0, 0) / total).T)
            lse_ref[0, t : t + 1, i * QB : stop] = top + jnp.log2(total)
        heads.append(jnp.concatenate(pieces, 0))
    o_ref[...] = jnp.concatenate(heads, 1).astype(BF)


def attend_back_step(slopes, x_ref, do_ref, lse_ref, dx_ref, dk_ref, dv_ref):
    n = x_ref.shape[0]
    pair = pl.program_id(0)
    ones = jnp.ones((n, HD), BF)
    parts = []
    for t in range(2):
        base = 3 * HD * t
        q, k, v = (x_ref[:, base + HD * s : base + HD * (s + 1)] for s in range(3))
        do = do_ref[:, HD * t : HD * (t + 1)]
        keys = jnp.concatenate([k, bias_cols(slopes[2 * pair + t], n)], 1)
        queries = jnp.concatenate([q, ones], 1)
        dq = []
        for i in reversed(range(n // QB)):
            stop = QB * (i + 1)
            rows = slice(i * QB, stop)
            z = block_scores(keys, queries, stop, i)
            p = jnp.exp2(z - lse_ref[0, t : t + 1, rows])
            dp = bdot(v[:stop], do[rows], 1, 1)
            total = jnp.sum(p * dp, 0, keepdims=True)
            ds = (p * (dp - total)).astype(BF)
            dq.append(bdot(k[:stop], ds, 0, 0).T)
            dk = bdot(ds, q[rows], 1, 0)
            dv = bdot(p.astype(BF), do[rows], 1, 0)
            if stop == n:
                dk_ref[...] = dk
                dv_ref[...] = dv
            else:
                dk_ref[:stop] += dk
                dv_ref[:stop] += dv
        scale = HD ** (-0.5)
        parts += [jnp.concatenate(dq[::-1], 0) * scale, dk_ref[...] * scale, dv_ref[...]]
    dx_ref[...] = jnp.concatenate(parts, 1).astype(BF)


class Place:
    def __init__(self, dp_size):
        self.row = lax.axis_index("row")
        self.col = lax.axis_index("col")
        self.dp = lax.axis_index("dp")
        self.bits = [1 << b for b in range(dp_size.bit_length() - 1)]
        self.across = {"col": 1 - self.col}
        self.beside = {"row": 1 - self.row}
        self.diagonal = {"row": 1 - self.row, "col": 1 - self.col}
        self.flags = [lax.rem(self.dp // bit, 2) for bit in self.bits]
        self.peers = [
            {"dp": self.dp + bit - 2 * bit * flag} for bit, flag in zip(self.bits, self.flags)
        ]

    def meet(self, partners):
        barrier = pltpu.get_barrier_semaphore()
        for partner in partners:
            pl.semaphore_signal(barrier, inc=1, device_id=partner, device_id_type=MESH)
        pl.semaphore_wait(barrier, len(partners))


def send(src, dst, sems, k, device):
    return pltpu.make_async_remote_copy(
        src_ref=src,
        dst_ref=dst,
        send_sem=sems.at[0, k],
        recv_sem=sems.at[1, k],
        device_id=device,
        device_id_type=MESH,
    )


class Gather:
    def __init__(self, place, block, full, row_dim, chunks, refs):
        self.p, self.block, self.full, self.row_dim, self.n = place, block, full, row_dim, chunks
        self.keep, self.sems, self.copy_sems = refs
        self.rows, self.cols = block.shape
        self.part = self.rows // 4
        self.step = self.part // chunks

    @staticmethod
    def scratch(shape, chunks):
        return [
            pltpu.VMEM(shape, BF),
            pltpu.SemaphoreType.DMA((2, 1 + 8 * chunks)),
            pltpu.SemaphoreType.DMA((2,)),
        ]

    def region(self, row, col, part=None, k=0):
        first, second = (row, col) if self.row_dim == 0 else (col, row)
        start = pl.multiple_of(first * self.rows, 16)
        size = self.rows
        if part is not None:
            start = pl.multiple_of(start + part * self.part + k * self.step, 16)
            size = self.step
        return self.full.at[pl.ds(start, size), pl.ds(pl.multiple_of(second * self.cols, 128), self.cols)]

    def quarter(self, first=False, second=False):
        a, b = self.p.flags[0], self.p.flags[1]
        return 2 * (1 - b if second else b) + (1 - a if first else a)

    def load(self):
        return pltpu.make_async_copy(self.block, self.keep, self.copy_sems.at[0])

    def store(self):
        return pltpu.make_async_copy(self.keep, self.region(self.p.row, self.p.col), self.copy_sems.at[1])

    def beside(self, incoming):
        row = 1 - self.p.row if incoming else self.p.row
        return send(self.block, self.region(row, self.p.col), self.sems, 0, self.p.beside)

    def over(self, k, incoming):
        part = self.quarter()
        src = self.block.at[pl.ds(pl.multiple_of(part * self.part + k * self.step, 16), self.step)]
        col = 1 - self.p.col if incoming else self.p.col
        return send(src, self.region(self.p.row, col, part, k), self.sems, 1 + k, self.p.across)

    def relay(self, bit, k, incoming):
        src = self.region(self.p.row, 1 - self.p.col, self.quarter(), k)
        part = self.quarter(bit == 0, bit == 1) if incoming else self.quarter()
        dst = self.region(self.p.row, 1 - self.p.col, part, k)
        return send(src, dst, self.sems, 1 + (1 + bit) * self.n + k, self.p.peers[bit])

    def second(self, k, incoming):
        bit = k % 2
        src = self.region(self.p.row, 1 - self.p.col, self.quarter(bit == 1, bit == 0), k)
        part = self.quarter(True, True) if incoming else self.quarter(bit == 1, bit == 0)
        dst = self.region(self.p.row, 1 - self.p.col, part, k)
        return send(src, dst, self.sems, 1 + 3 * self.n + k, self.p.peers[bit])

    def hand(self, which, k, incoming):
        part = self.quarter(which in (1, 3), which in (2, 3))
        row = 1 - self.p.row if incoming else self.p.row
        src = self.region(self.p.row, 1 - self.p.col, part, k)
        dst = self.region(row, 1 - self.p.col, part, k)
        return send(src, dst, self.sems, 1 + (4 + which) * self.n + k, self.p.beside)

    def start(self):
        self.beside(False).start()
        self.load().start()

    def issue(self, k):
        self.over(k, False).start()

    def arrived(self, k):
        self.over(k, True).wait_recv()
        for bit in range(2):
            self.relay(bit, k, False).start()
        self.hand(0, k, False).start()

    def relayed(self, k):
        for bit in range(2):
            self.relay(bit, k, True).wait_recv()
            self.hand(1 + bit, k, False).start()
        self.second(k, False).start()

    def ended(self, k):
        self.second(k, True).wait_recv()
        self.hand(3, k, False).start()

    def settle(self):
        self.load().wait()
        self.store().start()

    def finish(self):
        self.store().wait()
        self.beside(False).wait_send()
        self.beside(True).wait_recv()
        for k in range(self.n):
            self.over(k, False).wait_send()
            self.second(k, False).wait_send()
            for bit in range(2):
                self.relay(bit, k, False).wait_send()
            for which in range(4):
                self.hand(which, k, False).wait_send()
                self.hand(which, k, True).wait_recv()


AHEAD = 3
LAG = 3


def move_on(items, t):
    for lag, name in ((2 * LAG, "ended"), (LAG, "relayed"), (0, "arrived"), (-AHEAD, "issue")):
        if 0 <= t - lag < len(items):
            item, k = items[t - lag]
            getattr(item, name)(k)


def first_moves(items):
    for item, k in items[:AHEAD]:
        item.issue(k)


WIDE = 256
CROSSING = 3


class Reduce:
    def __init__(self, place, parts, outs, refs, held=None):
        self.p, self.parts, self.outs, self.held = place, parts, outs, held
        levels = self.levels = len(place.bits)
        if held is None:
            self.own, *refs = refs
        self.got, self.over, self.full, *refs = refs
        self.landing = refs[:levels]
        self.load_sem, self.core_sem, self.over_sem, self.half_sem, self.back_sem, self.out_sem = refs[levels:]
        self.n, self.rows = self.over.shape[:2]
        self.chunks = [(i, k) for i, out in enumerate(outs) for k in range(out.shape[1] // WIDE)]

    @staticmethod
    def scratch(n, rows, levels, held=False):
        own = [] if held else [pltpu.VMEM((2, n, rows, WIDE), BF)]
        return (
            own
            + [
                pltpu.VMEM((2, n, rows, WIDE), BF),
                pltpu.VMEM((n, rows, WIDE), BF),
                pltpu.VMEM((n, rows, WIDE), BF),
            ]
            + [pltpu.VMEM((n, rows >> (b + 1), WIDE), BF) for b in range(levels)]
            + [
                pltpu.SemaphoreType.DMA((2 * n,)),
                pltpu.SemaphoreType.DMA((2, 2 * n)),
                pltpu.SemaphoreType.DMA((2, n)),
                pltpu.SemaphoreType.DMA((2, levels * n)),
                pltpu.SemaphoreType.DMA((2, levels * n)),
                pltpu.SemaphoreType.DMA((n,)),
            ]
        )

    def half(self, mine):
        return self.p.col if mine else 1 - self.p.col

    def mine(self, col, k, start=0, size=None):
        size = self.rows if size is None else size
        if self.held is None:
            return self.own.at[col, k, pl.ds(pl.multiple_of(start, 16), size)]
        return self.held.at[col, k, pl.ds(pl.multiple_of(self.p.row * self.rows + start, 16), size)]

    def part(self, row, col, g):
        i, k = self.chunks[g]
        part = self.parts[i]
        start = pl.multiple_of(col * (part.shape[1] // 2) + k * WIDE, WIDE)
        return part.at[pl.ds(pl.multiple_of(row * self.rows, 16), self.rows), pl.ds(start, WIDE)]

    def load(self, mine, g):
        col = self.half(mine)
        return pltpu.make_async_copy(
            self.part(self.p.row, col, g), self.own.at[col, g], self.load_sem.at[self.n * mine + g]
        )

    def beside(self, mine, g):
        col = self.half(mine)
        if self.held is None:
            src = self.part(1 - self.p.row, col, g)
        else:
            src = self.held.at[col, g, pl.ds(pl.multiple_of((1 - self.p.row) * self.rows, 16), self.rows)]
        return send(src, self.got.at[col, g], self.core_sem, self.n * mine + g, self.p.beside)

    def landed(self, mine, g):
        col = self.half(mine)
        ref = self.got.at[col, g]
        return send(ref, ref, self.core_sem, self.n * mine + g, self.p.beside)

    def begin(self):
        for mine in range(2):
            for g in range(self.n):
                self.beside(mine, g).start()
                self.load(mine, g).start()

    def pair(self, mine, g):
        col = self.half(mine)
        if self.held is None:
            ref = self.own.at[col, g]
            pltpu.make_async_copy(ref, ref, self.load_sem.at[self.n * mine + g]).wait()
        self.landed(mine, g).wait_recv()
        ref = self.mine(col, g)
        ref[...] = ref[...] + self.got[col, g]

    def crossing(self, k):
        return send(self.mine(1 - self.p.col, k), self.over.at[k], self.over_sem, k, self.p.across)

    def offset(self, level):
        return sum((self.p.flags[b] * (self.rows >> (b + 1)) for b in range(level)), 0)

    def halving(self, b, k):
        size = self.rows >> (b + 1)
        start = self.offset(b) + (1 - self.p.flags[b]) * size
        return send(
            self.mine(self.p.col, k, start, size),
            self.landing[b].at[k],
            self.half_sem,
            b * self.n + k,
            self.p.peers[b],
        )

    def doubling(self, b, k, incoming):
        size = self.rows >> (b + 1)
        start = self.offset(b) + self.p.flags[b] * size
        other = self.offset(b) + (1 - self.p.flags[b]) * size
        at = self.full.at[k, pl.ds(pl.multiple_of(start, 16), size)]
        to = self.full.at[k, pl.ds(pl.multiple_of(other if incoming else start, 16), size)]
        return send(at, to, self.back_sem, b * self.n + k, self.p.peers[b])

    def stage(self, j, k):
        col, levels = self.p.col, self.levels
        if j == 0:
            self.crossing(k).wait_recv()
            ref = self.mine(col, k)
            ref[...] = ref[...] + self.over[k]
            self.halving(0, k).start()
        elif j <= levels:
            b = j - 1
            self.halving(b, k).wait_recv()
            size = self.rows >> (b + 1)
            start = self.offset(b + 1)
            ref = self.mine(col, k, start, size)
            total = ref[...] + self.landing[b][k]
            if b + 1 < levels:
                ref[...] = total
                self.halving(b + 1, k).start()
            else:
                self.full[k, pl.ds(pl.multiple_of(start, 16), size)] = total
                self.doubling(b, k, False).start()
        else:
            b = 2 * levels - j
            self.doubling(b, k, True).wait_recv()
            if b:
                self.doubling(b - 1, k, False).start()

    def sum_on(self, t):
        for j in reversed(range(1 + 2 * self.levels)):
            k = t - 2 * j

            @pl.when((k >= 0) & (k < self.n))
            def _(j=j, k=k):
                self.stage(j, k)

    def steps(self):
        return self.n + 4 * self.levels

    def advance(self, t):
        @pl.when((t >= 0) & (t < self.n))
        def _():
            self.pair(0, t)
            self.crossing(t).start()

        @pl.when((t >= 1) & (t < self.n + 1))
        def _():
            self.pair(1, t - 1)

        self.sum_on(t - CROSSING)

    def drain(self, t):
        def body(i, carry):
            self.advance(i)
            return carry

        lax.fori_loop(t, self.steps() + CROSSING, body, 0)

    def result(self, g):
        i, k = self.chunks[g]
        return pltpu.make_async_copy(
            self.full.at[g], self.outs[i].at[:, pl.ds(k * WIDE, WIDE)], self.out_sem.at[g]
        )

    def finish(self):
        for g in range(self.n):
            self.result(g).start()

        def body(k, carry):
            for mine in range(2):
                self.landed(mine, k).wait_send()
            self.crossing(k).wait_send()
            for b in range(self.levels):
                self.halving(b, k).wait_send()
                self.doubling(b, k, False).wait_send()
            return carry

        lax.fori_loop(0, self.n, body, 0)
        for g in range(self.n):
            self.result(g).wait()


class Spread:
    def __init__(self, place, block, whole, to_sequences, chunks, refs):
        self.p, self.block, self.whole, self.forward, self.n = place, block, whole, to_sequences, chunks
        self.keep, self.sems, self.copy_sems = refs
        self.rows = whole.shape[0]
        self.cols = block.shape[1]
        self.step = self.rows // chunks

    @staticmethod
    def scratch(rows, cols, chunks):
        return [
            pltpu.VMEM((rows, cols), BF),
            pltpu.SemaphoreType.DMA((2, 3 * chunks)),
            pltpu.SemaphoreType.DMA((2,)),
        ]

    def ends(self, to_row, to_col, row, col, k=None):
        if self.forward:
            seq, part = 2 * to_row + to_col, 2 * row + col
        else:
            seq, part = 2 * row + col, 2 * to_row + to_col
        start, size = (0, self.rows) if k is None else (k * self.step, self.step)
        narrow = self.block.at[pl.ds(pl.multiple_of(seq * self.rows + start, 16), size)]
        wide = self.whole.at[
            pl.ds(start, size), pl.ds(pl.multiple_of(part * self.cols, 128), self.cols)
        ]
        return (narrow, wide) if self.forward else (wide, narrow)

    def copy(self, which, k, incoming):
        p = self.p
        row, col = ((p.row, 1 - p.col), (1 - p.row, 1 - p.col), (1 - p.row, p.col))[which]
        device = (p.across, p.diagonal, p.beside)[which]
        src, dst = self.ends(row, col, p.row, p.col, k)
        if incoming:
            dst = self.ends(p.row, p.col, row, col, k)[1]
        return send(src, dst, self.sems, 3 * k + which, device)

    def load(self):
        p = self.p
        return pltpu.make_async_copy(self.ends(p.row, p.col, p.row, p.col)[0], self.keep, self.copy_sems.at[0])

    def store(self):
        p = self.p
        return pltpu.make_async_copy(self.keep, self.ends(p.row, p.col, p.row, p.col)[1], self.copy_sems.at[1])

    def start(self):
        self.load().start()

    def issue(self, k):
        for which in range(3):
            self.copy(which, k, False).start()

    def settle(self):
        self.load().wait()
        self.store().start()

    def arrived(self, k):
        for which in range(3):
            self.copy(which, k, True).wait_recv()

    def relayed(self, k):
        pass

    def ended(self, k):
        pass

    def finish(self):
        self.store().wait()
        for k in range(self.n):
            for which in range(3):
                self.copy(which, k, False).wait_send()


ANY = pl.BlockSpec(memory_space=pl.ANY)


FIRST_CHUNKS = 2


def front_kernel(dp_size, tokens, weight, small, x, full, smalls, *refs):
    p = Place(dp_size)
    p.meet([p.across, p.beside, p.diagonal, p.peers[0], p.peers[1]])
    gather = Gather(p, weight, full, 0, FIRST_CHUNKS, refs[:3])
    spread = Spread(p, tokens, x, True, FIRST_CHUNKS, refs[3:6])
    small_sems, keep_sem = refs[6:]
    items = [(gather, k) for k in range(FIRST_CHUNKS)] + [(spread, k) for k in range(FIRST_CHUNKS)]
    mine = 2 * p.row + p.col
    others = (
        (2 * p.row + 1 - p.col, p.across),
        (2 * (1 - p.row) + p.col, p.beside),
        (2 * (1 - p.row) + 1 - p.col, p.diagonal),
    )
    gather.start()
    keep = pltpu.make_async_copy(small, smalls.at[mine], keep_sem)
    keep.start()
    for k, (_, device) in enumerate(others):
        send(small, smalls.at[mine], small_sems, k, device).start()
    spread.start()
    first_moves(items)
    gather.settle()
    spread.settle()
    for t in range(len(items) + 2 * LAG):
        move_on(items, t)
    keep.wait()
    for k, (index, device) in enumerate(others):
        send(small, smalls.at[mine], small_sems, k, device).wait_send()
        send(small, smalls.at[index], small_sems, k, device).wait_recv()
    gather.finish()
    spread.finish()


def front(dp_size, tokens, weight, small):
    rows, width = tokens.shape
    return pl.pallas_call(
        partial(front_kernel, dp_size),
        in_specs=[ANY] * 2 + [pl.BlockSpec(memory_space=pltpu.VMEM)],
        out_specs=[ANY] * 2 + [pl.BlockSpec(memory_space=pltpu.VMEM)],
        out_shape=[
            jax.ShapeDtypeStruct((rows // 4, width * 4), BF),
            jax.ShapeDtypeStruct((2 * weight.shape[0], 2 * weight.shape[1]), BF),
            jax.ShapeDtypeStruct((4,) + small.shape, F32),
        ],
        scratch_shapes=Gather.scratch(weight.shape, FIRST_CHUNKS)
        + Spread.scratch(rows // 4, width, FIRST_CHUNKS)
        + [pltpu.SemaphoreType.DMA((2, 3)), pltpu.SemaphoreType.DMA],
        compiler_params=pltpu.CompilerParams(collective_id=0, has_side_effects=True),
        name="front",
    )(tokens, weight, small)


def tail_kernel(dp_size, part, grads, small, out, spread_out, small_out, *refs):
    p = Place(dp_size)
    p.meet([p.across, p.beside, p.diagonal] + p.peers)
    count = len(refs) - 9
    reduction = Reduce(p, (part,), (out,), refs[:count])
    spread = Spread(p, spread_out, grads, False, 4, refs[count : count + 3])
    four_sem, bit_sem, four, lots, mine_ref, own_sem = refs[count + 3 :]
    reduction.begin()
    spread.start()
    others = (
        (2 * p.row + 1 - p.col, p.across),
        (2 * (1 - p.row) + p.col, p.beside),
        (2 * (1 - p.row) + 1 - p.col, p.diagonal),
    )
    load = pltpu.make_async_copy(small.at[2 * p.row + p.col], mine_ref.at[0], own_sem.at[0])
    load.start()
    for k, (index, device) in enumerate(others):
        send(small.at[index], four.at[k], four_sem, k, device).start()
    for t in range(CROSSING):
        reduction.advance(t)
    spread.settle()
    load.wait()
    for k, (index, device) in enumerate(others):
        send(small.at[index], four.at[k], four_sem, k, device).wait_recv()
    mine_ref[0] = mine_ref[0] + four[0] + (four[1] + four[2])
    for b, peer in enumerate(p.peers):
        copy = send(mine_ref.at[b], lots.at[b], bit_sem, b, peer)
        copy.start()
        reduction.advance(CROSSING + b)
        copy.wait_recv()
        mine_ref[b + 1] = mine_ref[b] + lots[b]
    small_out[...] = mine_ref[len(p.peers)]
    for k in range(4):
        spread.issue(k)
    reduction.drain(CROSSING + len(p.peers))
    for k, (index, device) in enumerate(others):
        send(small.at[index], four.at[k], four_sem, k, device).wait_send()
    for b, peer in enumerate(p.peers):
        send(mine_ref.at[b], lots.at[b], bit_sem, b, peer).wait_send()
    for k in range(4):
        spread.arrived(k)
    spread.finish()
    reduction.finish()


def tail(dp_size, part, grads, small):
    levels = dp_size.bit_length() - 1
    rows, cols = part.shape[0] // 2, part.shape[1] // 2
    shape = small.shape[1:]
    return pl.pallas_call(
        partial(tail_kernel, dp_size),
        in_specs=[ANY] * 3,
        out_specs=[ANY, ANY, pl.BlockSpec(memory_space=pltpu.VMEM)],
        out_shape=[
            jax.ShapeDtypeStruct((rows, cols), BF),
            jax.ShapeDtypeStruct((4 * grads.shape[0], grads.shape[1] // 4), BF),
            jax.ShapeDtypeStruct(shape, F32),
        ],
        scratch_shapes=Reduce.scratch(cols // WIDE, rows, levels)
        + Spread.scratch(grads.shape[0], grads.shape[1] // 4, 4)
        + [
            pltpu.SemaphoreType.DMA((2, 3)),
            pltpu.SemaphoreType.DMA((2, levels)),
            pltpu.VMEM((3,) + shape, F32),
            pltpu.VMEM((levels,) + shape, F32),
            pltpu.VMEM((levels + 1,) + shape, F32),
            pltpu.SemaphoreType.DMA((1,)),
        ],
        compiler_params=pltpu.CompilerParams(
            collective_id=3, has_side_effects=True, vmem_limit_bytes=48 << 20
        ),
        name="tail",
    )(part, grads, small)


GATHERED = ((1, 2), (0, 4), (1, 4))


def attend_kernel(dp_size, slopes, x_ref, *refs):
    blocks, grads, refs = refs[:3], refs[3], refs[4:]
    (o_ref, lse_ref), wholes, og, refs = refs[:2], refs[2:5], refs[5], refs[6:]
    step, last = pl.program_id(0), pl.num_programs(0) - 1
    p = Place(dp_size)
    gathers = [
        Gather(p, block, whole, dim, chunks, refs[3 * i : 3 * i + 3])
        for i, (block, whole, (dim, chunks)) in enumerate(zip(blocks, wholes, GATHERED))
    ]
    spread = Spread(p, grads, og, True, 4, refs[9:12])
    items = [(g, k) for g in gathers + [spread] for k in range(g.n)]

    @pl.when(step == 0)
    def _():
        p.meet([p.across, p.beside, p.diagonal, p.peers[0], p.peers[1]])
        for g in gathers + [spread]:
            g.start()
        first_moves(items)

    attend_step(slopes, x_ref, o_ref, lse_ref)

    @pl.when(step == 1)
    def _():
        for g in gathers + [spread]:
            g.settle()

    marks = [max(0, (7 * (i - 1)) // 5) for i in range(9)]
    for i in range(1, 7):

        @pl.when(step == i)
        def _(i=i):
            for t in range(marks[i], marks[i + 1]):
                move_on(items, t)

    @pl.when(step == last)
    def _():
        for t in range(marks[7], len(items) + 2 * LAG):
            move_on(items, t)
        for g in gathers + [spread]:
            g.finish()


def attend(dp_size, slopes, joined, weights, grads):
    n, width = joined.shape
    pairs = width // (6 * HD)
    rows, cols = grads.shape[0] // 4, grads.shape[1]
    return pl.pallas_call(
        partial(attend_kernel, dp_size),
        grid_spec=pltpu.PrefetchScalarGridSpec(
            num_scalar_prefetch=1,
            grid=(pairs,),
            in_specs=[pl.BlockSpec((n, 6 * HD), lambda h, s: (0, h))] + [ANY] * 4,
            out_specs=[
                pl.BlockSpec((n, 2 * HD), lambda h, s: (0, h)),
                pl.BlockSpec((1, 2, n), lambda h, s: (h, 0, 0)),
            ]
            + [ANY] * 4,
            scratch_shapes=sum((Gather.scratch(w.shape, g[1]) for w, g in zip(weights, GATHERED)), [])
            + Spread.scratch(rows, cols, 4),
        ),
        out_shape=[
            jax.ShapeDtypeStruct((n, pairs * 2 * HD), BF),
            jax.ShapeDtypeStruct((pairs, 2, n), F32),
        ]
        + [jax.ShapeDtypeStruct((2 * w.shape[0], 2 * w.shape[1]), BF) for w in weights]
        + [jax.ShapeDtypeStruct((rows, 4 * cols), BF)],
        compiler_params=pltpu.CompilerParams(
            vmem_limit_bytes=40 << 20, collective_id=1, has_side_effects=True
        ),
        cost_estimate=pl.CostEstimate(
            flops=32 * n * n * HD * pairs, bytes_accessed=n * 512 * pairs * 2, transcendentals=n * n * pairs
        ),
        name="attend",
    )(slopes, joined, *weights, grads)


def attend_back_kernel(dp_size, slopes, x_ref, do_ref, lse_ref, *refs):
    parts, whole, dx_ref, outs, narrow = refs[:2], refs[2], refs[3], refs[4:6], refs[6]
    dk_ref, dv_ref, *refs = refs[7:]
    step, last = pl.program_id(0), pl.num_programs(0) - 1
    p = Place(dp_size)
    reduction = Reduce(p, parts, outs, refs[:-3])
    spread = Spread(p, narrow, whole, False, 4, refs[-3:])

    @pl.when(step == 0)
    def _():
        p.meet([p.across, p.beside, p.diagonal] + p.peers)
        reduction.begin()
        spread.start()

    attend_back_step(slopes, x_ref, do_ref, lse_ref, dx_ref, dk_ref, dv_ref)

    @pl.when(step == 0)
    def _():
        for t in range(CROSSING - 1):
            reduction.advance(t)
        spread.settle()

    @pl.when(step < last)
    def _():
        reduction.advance(step + CROSSING - 1)

    @pl.when(step == last)
    def _():
        reduction.advance(last + CROSSING - 1)
        for k in range(4):
            spread.issue(k)
        reduction.drain(last + CROSSING)
        for k in range(4):
            spread.arrived(k)
        spread.finish()
        reduction.finish()


def attend_back(dp_size, slopes, joined, out_grads, lse, parts, result):
    n, width = joined.shape
    pairs = width // (6 * HD)
    levels = dp_size.bit_length() - 1
    blocks = [(g.shape[0] // 2, g.shape[1] // 2) for g in parts]
    rows, cols = 4 * result.shape[0], result.shape[1] // 4
    return pl.pallas_call(
        partial(attend_back_kernel, dp_size),
        grid_spec=pltpu.PrefetchScalarGridSpec(
            num_scalar_prefetch=1,
            grid=(pairs,),
            in_specs=[
                pl.BlockSpec((n, 6 * HD), lambda h, s: (0, h)),
                pl.BlockSpec((n, 2 * HD), lambda h, s: (0, h)),
                pl.BlockSpec((1, 2, n), lambda h, s: (h, 0, 0)),
            ]
            + [ANY] * 3,
            out_specs=[pl.BlockSpec((n, 6 * HD), lambda h, s: (0, h))] + [ANY] * 3,
            scratch_shapes=[pltpu.VMEM((n, HD), F32)] * 2
            + Reduce.scratch(sum(b[1] // WIDE for b in blocks), blocks[0][0], levels)
            + Spread.scratch(result.shape[0], cols, 4),
        ),
        out_shape=[jax.ShapeDtypeStruct(joined.shape, BF)]
        + [jax.ShapeDtypeStruct(b, BF) for b in blocks]
        + [jax.ShapeDtypeStruct((rows, cols), BF)],
        compiler_params=pltpu.CompilerParams(
            vmem_limit_bytes=60 << 20, collective_id=2, has_side_effects=True
        ),
        cost_estimate=pl.CostEstimate(
            flops=80 * n * n * HD * pairs, bytes_accessed=n * 1024 * pairs * 2, transcendentals=n * n * pairs
        ),
        name="attend_back",
    )(slopes, joined, out_grads, lse, *parts, result)


TILE = 512
ROWS = 256


def hidden_tile(step):
    tiles = FF // TILE
    return lax.rem(step + (tiles // 2) * (1 - lax.axis_index("col")), tiles)


def feed_kernel(
    dp_size, normed, normed_t, grads, grads_t, hidden, up, down, up_bias, down_bias,
    result, back, up_part, bias_grad, out, *refs,
):
    total, act, pre_grad, held, load_sem, *refs = refs
    step, last = pl.program_id(0), pl.num_programs(0) - 1
    p = Place(dp_size)
    reduction = Reduce(p, (None,), (out,), refs, held)
    tiles = FF // TILE
    tile = hidden_tile(step)
    per = TILE // WIDE
    load = pltpu.make_async_copy(hidden, total, load_sem)

    @pl.when(step == 0)
    def _():
        load.start()
        p.meet([p.across, p.beside] + p.peers)
        back[...] = jnp.zeros_like(back)
        load.wait()

    bias = up_bias[:, pl.ds(pl.multiple_of(tile * TILE, TILE), TILE)]
    n = normed.shape[0]
    bias_sum = jnp.zeros((1, TILE), F32)
    a = math.sqrt(2.0 / math.pi)
    b = 0.044715 * a
    for r in range(n // ROWS):
        at = slice(r * ROWS, (r + 1) * ROWS)
        u = bdot(normed[at], up[...], 1, 0) + bias
        act_grad = bdot(grads[at], down[...], 1, 1)
        square = u * u
        half = 0.5 + 0.5 * jnp.tanh(u * (a + b * square))
        value = u * half
        slope = half + 2.0 * value * (1.0 - half) * (a + 3.0 * b * square)
        value = value.astype(BF)
        grad = (act_grad * slope).astype(BF)
        bias_sum = bias_sum + jnp.sum(grad.astype(F32), axis=0, keepdims=True)
        act[at] = value
        pre_grad[at] = grad
        total[at] += bdot(value, down[...], 1, 0)
        back[at] += bdot(grad, up[...], 1, 1)
    bias_grad[:, pl.ds(pl.multiple_of(tile * TILE, TILE), TILE)] = bias_sum
    up_part[...] = bdot(normed_t[...], pre_grad[...], 1, 0).astype(BF)
    part = bdot(grads_t[...], act[...], 1, 0).astype(BF)
    col = tile // (tiles // 2)
    first = lax.rem(tile, tiles // 2) * per
    for k in range(per):
        held[col, first + k] = part[:, k * WIDE : (k + 1) * WIDE]

    half_tiles = tiles // 2
    for s in range(tiles):

        @pl.when(step == s)
        def _(s=s):
            mine, start = s // half_tiles, (s % half_tiles) * per
            for k in range(start, start + per):
                reduction.beside(mine, k).start()
            if s:
                mine, start = (s - 1) // half_tiles, ((s - 1) % half_tiles) * per
                for k in range(start, start + per):
                    reduction.pair(mine, k)
                    if mine:
                        reduction.sum_on(k)
                    else:
                        reduction.crossing(k).start()

    @pl.when(step == last)
    def _():
        result[...] = (total[...] + down_bias[...]).astype(BF)
        start = (half_tiles - 1) * per
        for k in range(start, start + per):
            reduction.pair(1, k)

        def body(i, carry):
            reduction.sum_on(i)
            return carry

        lax.fori_loop(start, reduction.steps(), body, 0)
        reduction.finish()


def feed(dp_size, normed, grads, hidden, up, down, up_bias, down_bias):
    n, width = normed.shape
    levels = dp_size.bit_length() - 1
    rows, cols = width // 2, FF // 2
    whole = lambda shape: pl.BlockSpec(shape, lambda s: (0, 0), pipeline_mode=pl.Buffered(1))
    return pl.pallas_call(
        partial(feed_kernel, dp_size),
        grid=(FF // TILE,),
        in_specs=[
            whole((n, width)),
            whole((width, n)),
            whole((n, width)),
            whole((width, n)),
            ANY,
            pl.BlockSpec((width, TILE), lambda s: (0, hidden_tile(s))),
            pl.BlockSpec((TILE, width), lambda s: (hidden_tile(s), 0)),
            whole((1, FF)),
            whole((1, width)),
        ],
        out_specs=[
            whole((n, width)),
            whole((n, width)),
            pl.BlockSpec((width, TILE), lambda s: (0, hidden_tile(s))),
            whole((1, FF)),
            ANY,
        ],
        out_shape=[
            jax.ShapeDtypeStruct((n, width), BF),
            jax.ShapeDtypeStruct((n, width), F32),
            jax.ShapeDtypeStruct((width, FF), BF),
            jax.ShapeDtypeStruct((1, FF), F32),
            jax.ShapeDtypeStruct((rows, cols), BF),
        ],
        scratch_shapes=[
            pltpu.VMEM((n, width), F32),
            pltpu.VMEM((n, TILE), BF),
            pltpu.VMEM((n, TILE), BF),
            pltpu.VMEM((2, cols // WIDE, width, WIDE), BF),
            pltpu.SemaphoreType.DMA,
        ]
        + Reduce.scratch(cols // WIDE, rows, levels, True),
        compiler_params=pltpu.CompilerParams(
            vmem_limit_bytes=61 << 20, collective_id=4, has_side_effects=True
        ),
        cost_estimate=pl.CostEstimate(
            flops=12 * n * width * FF, bytes_accessed=6 * width * FF, transcendentals=n * FF
        ),
        name="feed",
    )(normed, normed.T, grads, grads.T, hidden, up, down, up_bias.reshape(1, -1), down_bias.reshape(1, -1))


def normed(values, gain, shift):
    average = jnp.mean(values, axis=1, keepdims=True)
    away = values - average
    scale = lax.rsqrt(jnp.mean(away * away, axis=1, keepdims=True) + EPSILON)
    centered = away * scale
    return centered, scale, (centered * gain + shift).astype(BF)


def norm_backward(upstream, centered, scale, gain):
    scaled = upstream * gain
    back = scale * (
        scaled
        - jnp.mean(scaled, axis=1, keepdims=True)
        - centered * jnp.mean(scaled * centered, axis=1, keepdims=True)
    )
    return back, jnp.sum(upstream * centered, axis=0), jnp.sum(upstream, axis=0)


def local(
    dp_size,
    tokens,
    first_gain,
    first_shift,
    joined_weight,
    query_value_bias,
    output_weight,
    output_bias,
    second_gain,
    second_shift,
    up_weight,
    up_bias,
    down_weight,
    down_bias,
    out_grad,
):
    heads = query_value_bias.shape[0] * 4
    w = D // 4
    small = jnp.concatenate(
        [
            first_gain,
            first_shift,
            output_bias,
            second_gain,
            second_shift,
            down_bias,
            up_bias,
            query_value_bias.reshape(-1),
        ]
    ).reshape(-1, 128)
    x, wj, small = front(dp_size, tokens, joined_weight, small)
    small = small.reshape(2, 2, -1)
    g1, s1, ob, g2, s2, db = (small[:, :, w * k : w * (k + 1)].reshape(-1) for k in range(6))

    def hidden_vector(start, size):
        return small[:, :, start : start + size].transpose(1, 0, 2).reshape(-1)

    ub = hidden_vector(6 * w, up_bias.shape[0])
    pair_bias = hidden_vector(6 * w + up_bias.shape[0], query_value_bias.size).reshape(heads, 2, HD)
    qv_bias = jnp.concatenate(
        [pair_bias[:, :1], jnp.zeros((heads, 1, HD), F32), pair_bias[:, 1:]], axis=1
    ).reshape(-1)
    slopes = jnp.exp2(-8.0 * (jnp.arange(heads).astype(F32) + 1.0) / heads)

    inputs = x.astype(F32)
    centered_first, scale_first, normed_first = normed(inputs, g1, s1)
    joined = (jnp.dot(normed_first, wj, preferred_element_type=F32) + qv_bias).astype(BF)
    attended, lse, wo, wu, wd, og = attend(
        dp_size, slopes, joined, (output_weight, up_weight, down_weight), out_grad
    )
    hidden = inputs + jnp.dot(attended, wo, preferred_element_type=F32) + ob
    centered_second, scale_second, normed_second = normed(hidden, g2, s2)
    upstream = og.astype(F32)
    down_bias_grad = jnp.sum(upstream, axis=0)
    result, normed_second_grad, up_part, up_bias_grad, down_weight_grad = feed(
        dp_size, normed_second, og, hidden, wu, wd, ub, db
    )
    back_second, second_gain_grad, second_shift_grad = norm_backward(
        normed_second_grad, centered_second, scale_second, g2
    )
    hidden_grad = upstream + back_second
    output_bias_grad = jnp.sum(hidden_grad, axis=0)
    branch = hidden_grad.astype(BF)
    output_part = bdot(branch, attended, 0, 0).astype(BF)
    attended_grad = bdot(branch, wo, 1, 1).astype(BF)
    joined_grad, up_weight_grad, output_weight_grad, result = attend_back(
        dp_size, slopes, joined, attended_grad, lse, (up_part, output_part), result
    )
    column_sums = jnp.sum(joined_grad.astype(F32), axis=0).reshape(heads, 3, HD)
    query_value_bias_grad = jnp.stack([column_sums[:, 0], column_sums[:, 2]], axis=1).reshape(-1)
    joined_part = bdot(normed_first, joined_grad, 0, 0).astype(BF)
    normed_first_grad = bdot(joined_grad, wj, 1, 1)
    back_first, first_gain_grad, first_shift_grad = norm_backward(
        normed_first_grad, centered_first, scale_first, g1
    )
    tokens_grad = (hidden_grad + back_first).astype(BF)

    features = jnp.stack(
        [
            first_gain_grad,
            first_shift_grad,
            output_bias_grad,
            second_gain_grad,
            second_shift_grad,
            down_bias_grad,
        ]
    ).reshape(6, 4, w)
    features = features.transpose(1, 0, 2).reshape(4, -1)

    def hidden_parts(values):
        return values.reshape(2, 2, -1).transpose(1, 0, 2).reshape(4, -1)

    totals = jnp.concatenate([features, hidden_parts(up_bias_grad), hidden_parts(query_value_bias_grad)], 1)
    joined_weight_grad, tokens_grad, totals = tail(
        dp_size, joined_part, tokens_grad, totals.reshape(4, -1, 128)
    )
    totals = totals.reshape(-1)
    fg, fs, obg, sg, ss, dbg = (totals[w * k : w * (k + 1)] for k in range(6))
    ubg = totals[6 * w : 6 * w + up_bias.shape[0]]
    qvg = totals[6 * w + up_bias.shape[0] :].reshape(query_value_bias.shape)
    return (
        result,
        tokens_grad.astype(F32),
        fg,
        fs,
        joined_weight_grad.astype(F32),
        qvg,
        output_weight_grad.T.astype(F32),
        obg,
        sg,
        ss,
        up_weight_grad.astype(F32),
        ubg,
        down_weight_grad.T.astype(F32),
        dbg,
    )


def solution(mesh):
    feature = P(("row", "col"))
    in_specs = (
        P("dp", ("row", "col")),
        feature,
        feature,
        P("row", "col"),
        P(("col", "row"), None),
        P("col", "row"),
        feature,
        feature,
        feature,
        P("row", "col"),
        P(("col", "row")),
        P("col", "row"),
        feature,
        P("dp", ("row", "col")),
    )
    out_specs = (
        P("dp", ("row", "col")),
        P("dp", ("row", "col")),
        feature,
        feature,
        P("row", "col"),
        P(("col", "row"), None),
        P("col", "row"),
        feature,
        feature,
        feature,
        P("row", "col"),
        P(("col", "row")),
        P("col", "row"),
        feature,
    )
    return jax.shard_map(
        partial(local, mesh.shape["dp"]),
        mesh=mesh,
        in_specs=in_specs,
        out_specs=out_specs,
        check_vma=False,
    )
```

```python
import math
from functools import partial

import jax
import jax.numpy as jnp
from jax import lax
from jax.experimental import pallas as pl
from jax.experimental.pallas import tpu as pltpu
from jax.sharding import PartitionSpec as P

D = 1024
H = 16
HD = 64
FF = 4096
SEQ_LEN = 1024
QB = 256
EPSILON = 1e-05
L2E = math.log2(math.e)
BF = jnp.bfloat16
F32 = jnp.float32
MESH = pl.DeviceIdType.MESH


def bdot(a, b, ca, cb):
    return lax.dot_general(a, b, (((ca,), (cb,)), ((), ())), preferred_element_type=F32)


def bias_cols(slope, n):
    j = lax.broadcasted_iota(jnp.int32, (n, HD), 0).astype(F32)
    lane = lax.broadcasted_iota(jnp.int32, (n, HD), 1)
    full = j * (slope * 8.0)
    hi = full.astype(BF)
    rest = full - hi.astype(F32)
    mid = rest.astype(BF)
    low = (rest - mid.astype(F32)).astype(BF)
    return jnp.where(lane == 0, hi, jnp.where(lane == 1, mid, jnp.where(lane == 2, low, jnp.zeros_like(hi))))


def block_scores(keys, queries, stop, i):
    z = bdot(keys[:stop], queries[i * QB : (i + 1) * QB], 1, 1) * (HD ** (-0.5) * L2E)
    row = lax.broadcasted_iota(jnp.int32, (QB, QB), 0)
    col = lax.broadcasted_iota(jnp.int32, (QB, QB), 1)
    last = jnp.where(row <= col, z[stop - QB :], -1e30)
    return last if stop == QB else jnp.concatenate([z[: stop - QB], last], 0)


def attend_step(slopes, x_ref, o_ref, lse_ref):
    n = x_ref.shape[0]
    pair = pl.program_id(0)
    ones = jnp.ones((n, HD), BF)
    heads = []
    for t in range(2):
        base = 3 * HD * t
        q, k, v = (x_ref[:, base + HD * s : base + HD * (s + 1)] for s in range(3))
        keys = jnp.concatenate([k, bias_cols(slopes[2 * pair + t], n)], 1)
        queries = jnp.concatenate([q, ones], 1)
        pieces = []
        for i in range(n // QB):
            stop = QB * (i + 1)
            z = block_scores(keys, queries, stop, i)
            top = jnp.max(z, 0, keepdims=True)
            p = jnp.exp2(z - top)
            total = jnp.sum(p, 0, keepdims=True)
            pieces.append((bdot(v[:stop], p.astype(BF), 0, 0) / total).T)
            lse_ref[0, t : t + 1, i * QB : stop] = top + jnp.log2(total)
        heads.append(jnp.concatenate(pieces, 0))
    o_ref[...] = jnp.concatenate(heads, 1).astype(BF)


def attend_back_step(slopes, x_ref, do_ref, lse_ref, dx_ref, dk_ref, dv_ref):
    n = x_ref.shape[0]
    pair = pl.program_id(0)
    ones = jnp.ones((n, HD), BF)
    parts = []
    for t in range(2):
        base = 3 * HD * t
        q, k, v = (x_ref[:, base + HD * s : base + HD * (s + 1)] for s in range(3))
        do = do_ref[:, HD * t : HD * (t + 1)]
        keys = jnp.concatenate([k, bias_cols(slopes[2 * pair + t], n)], 1)
        queries = jnp.concatenate([q, ones], 1)
        dq = []
        for i in reversed(range(n // QB)):
            stop = QB * (i + 1)
            rows = slice(i * QB, stop)
            z = block_scores(keys, queries, stop, i)
            p = jnp.exp2(z - lse_ref[0, t : t + 1, rows])
            dp = bdot(v[:stop], do[rows], 1, 1)
            total = jnp.sum(p * dp, 0, keepdims=True)
            ds = (p * (dp - total)).astype(BF)
            dq.append(bdot(k[:stop], ds, 0, 0).T)
            dk = bdot(ds, q[rows], 1, 0)
            dv = bdot(p.astype(BF), do[rows], 1, 0)
            if stop == n:
                dk_ref[...] = dk
                dv_ref[...] = dv
            else:
                dk_ref[:stop] += dk
                dv_ref[:stop] += dv
        scale = HD ** (-0.5)
        parts += [jnp.concatenate(dq[::-1], 0) * scale, dk_ref[...] * scale, dv_ref[...]]
    dx_ref[...] = jnp.concatenate(parts, 1).astype(BF)


def radices(dp_size):
    sizes = []
    while dp_size > 1:
        sizes.append(4 if dp_size % 4 == 0 and dp_size != 8 else 2)
        dp_size //= sizes[-1]
    return sizes


class Ring:
    def __init__(self, dp, size, stride):
        self.dp, self.size, self.stride = dp, size, stride
        self.flag = lax.rem(dp // stride, size)

    def index(self, q):
        return lax.rem(self.flag + q + self.size, self.size)

    def device(self, q):
        return {"dp": self.dp + (self.index(q) - self.flag) * self.stride}

    def devices(self):
        return [self.device(q) for q in range(1, self.size)]


class Place:
    def __init__(self, dp_size):
        self.row = lax.axis_index("row")
        self.col = lax.axis_index("col")
        self.dp = lax.axis_index("dp")
        self.bits = [1 << b for b in range(dp_size.bit_length() - 1)]
        self.across = {"col": 1 - self.col}
        self.beside = {"row": 1 - self.row}
        self.diagonal = {"row": 1 - self.row, "col": 1 - self.col}
        self.rings, stride = [], 1
        for size in radices(dp_size):
            self.rings.append(Ring(self.dp, size, stride))
            stride *= size
        self.flags = [lax.rem(self.dp // bit, 2) for bit in self.bits]
        self.peers = [
            {"dp": self.dp + bit - 2 * bit * flag} for bit, flag in zip(self.bits, self.flags)
        ]

    def all_rings(self):
        return [device for ring in self.rings for device in ring.devices()]

    def meet(self, partners):
        barrier = pltpu.get_barrier_semaphore()
        for partner in partners:
            pl.semaphore_signal(barrier, inc=1, device_id=partner, device_id_type=MESH)
        pl.semaphore_wait(barrier, len(partners))


def send(src, dst, sems, k, device):
    return pltpu.make_async_remote_copy(
        src_ref=src,
        dst_ref=dst,
        send_sem=sems.at[0, k],
        recv_sem=sems.at[1, k],
        device_id=device,
        device_id_type=MESH,
    )


class Gather:
    def __init__(self, place, block, full, row_dim, chunks, refs):
        self.p, self.block, self.full, self.row_dim, self.n = place, block, full, row_dim, chunks
        self.keep, self.sems, self.copy_sems = refs
        self.rows, self.cols = block.shape
        self.part = self.rows // 4
        self.step = self.part // chunks

    @staticmethod
    def scratch(shape, chunks):
        return [
            pltpu.VMEM(shape, BF),
            pltpu.SemaphoreType.DMA((2, 1 + 8 * chunks)),
            pltpu.SemaphoreType.DMA((2,)),
        ]

    def region(self, row, col, part=None, k=0):
        first, second = (row, col) if self.row_dim == 0 else (col, row)
        start = pl.multiple_of(first * self.rows, 16)
        size = self.rows
        if part is not None:
            start = pl.multiple_of(start + part * self.part + k * self.step, 16)
            size = self.step
        return self.full.at[pl.ds(start, size), pl.ds(pl.multiple_of(second * self.cols, 128), self.cols)]

    def quarter(self, first=False, second=False):
        a, b = self.p.flags[0], self.p.flags[1]
        return 2 * (1 - b if second else b) + (1 - a if first else a)

    def load(self):
        return pltpu.make_async_copy(self.block, self.keep, self.copy_sems.at[0])

    def store(self):
        return pltpu.make_async_copy(self.keep, self.region(self.p.row, self.p.col), self.copy_sems.at[1])

    def beside(self, incoming):
        row = 1 - self.p.row if incoming else self.p.row
        return send(self.block, self.region(row, self.p.col), self.sems, 0, self.p.beside)

    def over(self, k, incoming):
        part = self.quarter()
        src = self.block.at[pl.ds(pl.multiple_of(part * self.part + k * self.step, 16), self.step)]
        col = 1 - self.p.col if incoming else self.p.col
        return send(src, self.region(self.p.row, col, part, k), self.sems, 1 + k, self.p.across)

    def relay(self, bit, k, incoming):
        src = self.region(self.p.row, 1 - self.p.col, self.quarter(), k)
        part = self.quarter(bit == 0, bit == 1) if incoming else self.quarter()
        dst = self.region(self.p.row, 1 - self.p.col, part, k)
        return send(src, dst, self.sems, 1 + (1 + bit) * self.n + k, self.p.peers[bit])

    def second(self, k, incoming):
        bit = k % 2
        src = self.region(self.p.row, 1 - self.p.col, self.quarter(bit == 1, bit == 0), k)
        part = self.quarter(True, True) if incoming else self.quarter(bit == 1, bit == 0)
        dst = self.region(self.p.row, 1 - self.p.col, part, k)
        return send(src, dst, self.sems, 1 + 3 * self.n + k, self.p.peers[bit])

    def hand(self, which, k, incoming):
        part = self.quarter(which in (1, 3), which in (2, 3))
        row = 1 - self.p.row if incoming else self.p.row
        src = self.region(self.p.row, 1 - self.p.col, part, k)
        dst = self.region(row, 1 - self.p.col, part, k)
        return send(src, dst, self.sems, 1 + (4 + which) * self.n + k, self.p.beside)

    def start(self):
        self.beside(False).start()
        self.load().start()

    def issue(self, k):
        self.over(k, False).start()

    def arrived(self, k):
        self.over(k, True).wait_recv()
        for bit in range(2):
            self.relay(bit, k, False).start()
        self.hand(0, k, False).start()

    def relayed(self, k):
        for bit in range(2):
            self.relay(bit, k, True).wait_recv()
            self.hand(1 + bit, k, False).start()
        self.second(k, False).start()

    def ended(self, k):
        self.second(k, True).wait_recv()
        self.hand(3, k, False).start()

    def settle(self):
        self.load().wait()
        self.store().start()

    def finish(self):
        self.store().wait()
        self.beside(False).wait_send()
        self.beside(True).wait_recv()
        for k in range(self.n):
            self.over(k, False).wait_send()
            self.second(k, False).wait_send()
            for bit in range(2):
                self.relay(bit, k, False).wait_send()
            for which in range(4):
                self.hand(which, k, False).wait_send()
                self.hand(which, k, True).wait_recv()


AHEAD = 3
LAG = 3


def move_on(items, t):
    for lag, name in ((2 * LAG, "ended"), (LAG, "relayed"), (0, "arrived"), (-AHEAD, "issue")):
        if 0 <= t - lag < len(items):
            item, k = items[t - lag]
            getattr(item, name)(k)


def first_moves(items):
    for item, k in items[:AHEAD]:
        item.issue(k)


WIDE = 256
CROSSING = 3


def split_of(levels):
    down, rest, joined = FF // 2 // WIDE, (FF + D) // 2 // WIDE, 3 * D // 2 // WIDE
    fresh = down + rest + GAP
    ticks = (0, down - 2, fresh - 2, fresh + joined + 4 * levels)

    def first(tick):
        ended = tick - 4 * levels + 2
        return max(k for k in (0, down, 2 * down, down + rest) if k <= max(0, ended))

    return [
        Span(ticks[0], ticks[1], 0, down + EARLY, 0, first(ticks[1]), down + rest),
        Span(ticks[1], ticks[2], down + EARLY, down + rest, first(ticks[1]), first(ticks[2]), down + rest),
        Span(ticks[2], ticks[3], fresh, fresh + joined, first(ticks[2]), fresh + joined, down + rest),
    ]


GAP = 4
EARLY = 2


def weights_done(span):
    down, out, joined = FF // 2 // WIDE, D // 2 // WIDE, 3 * D // 2 // WIDE
    table = ((0, down, True), (down, down, False), (2 * down, out, True), (2 * down + out + GAP, joined, False))
    return [
        (first, count, turned) for first, count, turned in table if span.lo <= first and first + count <= span.done
    ]


def blocks_like(span, rows):
    return [
        jax.ShapeDtypeStruct((count * WIDE, rows) if turned else (rows, count * WIDE), BF)
        for _, count, turned in weights_done(span)
    ]


def turning(span, rows):
    count = sum(count for _, count, turned in weights_done(span) if turned)
    return [pltpu.VMEM((max(1, count), WIDE, rows), BF)]


class Span:
    def __init__(self, start, stop, before, after, lo, done, gap):
        self.start, self.stop, self.before, self.after, self.lo, self.done = start, stop, before, after, lo, done
        self.gap = gap
        self.hole = before - gap if before > gap else 0
        self.count = after - lo - self.hole
        self.fresh = after - before
        self.old = range(lo, min(before, gap))
        self.left = after - done

    def chunks(self):
        return [*self.old, *range(self.before, self.after)]

    def place(self, k):
        return k - self.lo - (self.hole * (k // self.before) if self.hole else 0)


class Reduce:
    def __init__(self, place, span, parts, state, finished, handed, refs, held=None, turn=None):
        self.p, self.span, self.parts, self.held = place, span, parts, held
        self.state, self.finished, self.handed, self.turn = state, finished, handed, turn
        self.rings = place.rings
        levels = self.levels = len(place.rings)
        self.own, self.other, *refs = refs
        self.got, self.over, self.full, *refs = refs
        self.landing = refs[:levels]
        self.load_sem, self.core_sem, self.over_sem, self.half_sem, self.back_sem, self.out_sem = refs[levels:]
        self.rows = self.full.shape[1]

    @staticmethod
    def scratch(span, rows, sizes):
        n, fresh = span.count, span.fresh
        landing, lanes, size = [], 0, rows
        for ring in sizes:
            size //= ring
            landing.append(pltpu.VMEM((ring - 1, n, size, WIDE), BF))
            lanes += ring - 1
        return (
            [
                pltpu.VMEM((n, rows, WIDE), BF),
                pltpu.VMEM((fresh, rows, WIDE), BF),
                pltpu.VMEM((2, fresh, rows, WIDE), BF),
                pltpu.VMEM((fresh, rows, WIDE), BF),
                pltpu.VMEM((n, rows, WIDE), BF),
            ]
            + landing
            + [
                pltpu.SemaphoreType.DMA((n + fresh,)),
                pltpu.SemaphoreType.DMA((2, 2 * fresh)),
                pltpu.SemaphoreType.DMA((2, fresh)),
                pltpu.SemaphoreType.DMA((2, lanes * n)),
                pltpu.SemaphoreType.DMA((2, lanes * n)),
                pltpu.SemaphoreType.DMA((n,)),
            ]
        )

    def lane(self, b, q):
        return sum(ring.size - 1 for ring in self.rings[:b]) + q - 1

    def size(self, b):
        return self.rows // math.prod(ring.size for ring in self.rings[: b + 1])


    def mine(self, k, start=0, size=None):
        size = self.rows if size is None else size
        return self.own.at[self.span.place(k), pl.ds(pl.multiple_of(start, 16), size)]

    def others(self, k):
        return self.other.at[k - self.span.before]

    def kept(self, row, slot):
        return self.held.at[slot, pl.ds(pl.multiple_of(row * self.rows, 16), self.rows)]

    def part(self, row, mine, k):
        ref, start = self.parts[k]
        col = self.p.col if mine else 1 - self.p.col
        start = pl.multiple_of(col * (ref.shape[1] // 2) + start, WIDE)
        return ref.at[pl.ds(pl.multiple_of(row * self.rows, 16), self.rows), pl.ds(start, WIDE)]

    def load(self, mine, k):
        dst = self.mine(k) if mine else self.others(k)
        return pltpu.make_async_copy(self.part(self.p.row, mine, k), dst, self.load_sem.at[self.load_at(mine, k)])

    def load_at(self, mine, k):
        return self.span.place(k) if mine else self.span.count + k - self.span.before

    def beside(self, mine, k, slot=None):
        if slot is None:
            src = self.part(1 - self.p.row, mine, k)
        else:
            src = self.kept(1 - self.p.row, slot)
        r = k - self.span.before
        return send(src, self.got.at[mine, r], self.core_sem, self.span.fresh * mine + r, self.p.beside)

    def landed(self, mine, k):
        r = k - self.span.before
        ref = self.got.at[mine, r]
        return send(ref, ref, self.core_sem, self.span.fresh * mine + r, self.p.beside)

    def crossing(self, k):
        r = k - self.span.before
        return send(self.others(k), self.over.at[r], self.over_sem, r, self.p.across)

    def offset(self, level):
        return sum((self.rings[b].flag * self.size(b) for b in range(level)), 0)

    def halving(self, b, q, k):
        ring, size, i = self.rings[b], self.size(b), self.span.place(k)
        return send(
            self.mine(k, self.offset(b) + ring.index(q) * size, size),
            self.landing[b].at[q - 1, i],
            self.half_sem,
            self.lane(b, q) * self.span.count + i,
            ring.device(q),
        )

    def doubling(self, b, q, k, incoming):
        ring, size, i = self.rings[b], self.size(b), self.span.place(k)
        start = self.offset(b) + ring.flag * size
        other = self.offset(b) + ring.index(-q) * size
        at = self.full.at[i, pl.ds(pl.multiple_of(start, 16), size)]
        to = self.full.at[i, pl.ds(pl.multiple_of(other if incoming else start, 16), size)]
        return send(at, to, self.back_sem, self.lane(b, q) * self.span.count + i, ring.device(q))

    def turns(self, b):
        return range(1, self.rings[b].size)

    def settled(self, j):
        b = 0 if j < self.levels else max(0, 2 * self.levels - j)
        size = self.size(b - 1) if b else self.rows
        return pl.ds(pl.multiple_of(self.offset(b), 16), size)

    def resume(self, k):
        i, j = self.span.place(k), self.pending(self.span.start, k)
        at = self.settled(j)
        dst = (self.own if j < self.levels else self.full).at[i, at]
        return pltpu.make_async_copy(self.state.at[i, at], dst, self.load_sem.at[i])

    @staticmethod
    def pending(tick, k):
        return max(0, (tick - k + 1) // 2)

    def begin(self):
        span = self.span
        for k in span.old:
            self.resume(k).start()
        if self.held is None:
            for mine in range(2):
                for k in range(span.before, span.after):
                    self.beside(mine, k).start()
                    self.load(mine, k).start()

    def resumed(self):
        for k in self.span.old:
            self.resume(k).wait()

    def pair(self, mine, k, slot=None):
        if slot is None:
            ref = self.mine(k) if mine else self.others(k)
            pltpu.make_async_copy(ref, ref, self.load_sem.at[self.load_at(mine, k)]).wait()
        self.landed(mine, k).wait_recv()
        ref = self.mine(k) if mine else self.others(k)
        here = ref if slot is None else self.kept(self.p.row, slot)
        ref[...] = here[...] + self.got[mine, k - self.span.before]
        if slot is not None:
            self.landed(mine, k).wait_send()

    def take(self, j, k):
        levels = self.levels
        i = self.span.place(k)
        if j == 0:
            self.crossing(k).wait_recv()
            ref = self.mine(k)
            ref[...] = ref[...] + self.over[k - self.span.before]
        elif j <= levels:
            b = j - 1
            start, size = self.offset(b + 1), self.size(b)
            ref = self.mine(k, start, size)
            total = ref[...].astype(F32)
            for q in self.turns(b):
                self.halving(b, q, k).wait_recv()
                total = total + self.landing[b][q - 1, i].astype(F32)
            total = total.astype(BF)
            if b + 1 < levels:
                ref[...] = total
            else:
                self.full[i, pl.ds(pl.multiple_of(start, 16), size)] = total
        else:
            b = 2 * levels - j
            for q in self.turns(b):
                self.doubling(b, q, k, True).wait_recv()

    def give(self, j, k):
        levels = self.levels
        if j < levels:
            for q in self.turns(j):
                self.halving(j, q, k).start()
        elif j < 2 * levels:
            b = 2 * levels - 1 - j
            for q in self.turns(b):
                self.doubling(b, q, k, False).start()

    def sum_on(self, t):
        span = self.span
        for j in reversed(range(1 + 2 * self.levels)):
            k = t - 2 * j
            old = (k < span.before) if j == 0 else (k < span.before) & (t < span.start + 2)

            @pl.when((k >= span.lo) & (k < span.after) & ((k < span.gap) | (k >= span.before)))
            def _(j=j, k=k, old=old):
                @pl.when(jnp.logical_not(old))
                def _():
                    self.take(j, k)

                self.give(j, k)

    def advance(self, t):
        span = self.span
        k = t + CROSSING

        @pl.when((k >= span.before) & (k < span.after))
        def _():
            self.pair(0, k)
            self.crossing(k).start()

        @pl.when((k - 1 >= span.before) & (k - 1 < span.after))
        def _():
            self.pair(1, k - 1)

        self.sum_on(t)

    def ahead(self):
        span = self.span
        for k in range(span.before, min(span.after, span.start + CROSSING)):
            self.pair(0, k)
            self.crossing(k).start()
        for k in range(span.before, min(span.after, span.start + CROSSING - 1)):
            self.pair(1, k)

    def run(self, start, stop):
        def body(i, carry):
            self.advance(i)
            return carry

        lax.fori_loop(start, stop, body, 0)

    def finish(self):
        span, levels = self.span, self.levels
        copies, where, turned_count = [], {}, 0
        for out, (first, count, turned) in zip(self.finished, weights_done(span)):
            for k in range(count):
                where[first + k] = (out, k, turned_count if turned else None)
                turned_count += 1 if turned else 0
        for k in span.chunks():
            i = span.place(k)
            j = self.pending(span.stop, k)
            if j <= 2 * levels and not (k < span.before and k >= span.stop):
                self.take(j, k)
            if k < span.done:
                out, place, turned = where[k]
                if turned is None:
                    src, dst = self.full.at[i], out.at[:, pl.ds(place * WIDE, WIDE)]
                else:
                    self.turn[turned] = self.full[i].T
                    src, dst = self.turn.at[turned], out.at[pl.ds(place * WIDE, WIDE)]
            else:
                at = self.settled(j)
                src = (self.own if j < levels else self.full).at[i, at]
                dst = self.handed.at[k - span.done, at]
            copy = pltpu.make_async_copy(src, dst, self.out_sem.at[i])
            copy.start()
            copies.append(copy)
        for r in range(span.before, span.after):
            if self.held is None:
                for mine in range(2):
                    self.landed(mine, r).wait_send()
            self.crossing(r).wait_send()
        for k in span.chunks():
            begun = self.pending(span.start, k) if k < span.before else 0
            ended = self.pending(span.stop, k)
            for j in range(begun, min(ended, 2 * levels)):
                b = j if j < levels else 2 * levels - 1 - j
                for q in self.turns(b):
                    if j < levels:
                        self.halving(b, q, k).wait_send()
                    else:
                        self.doubling(b, q, k, False).wait_send()
        for copy in copies:
            copy.wait()


def chunk_list(span, *arrays):
    places = [(ref, k * WIDE) for ref, first, last in arrays for k in range(first, last)]
    return dict(zip(range(span.before, span.after), places))


def chunks_like(count, rows):
    return jax.ShapeDtypeStruct((count, rows, WIDE), BF)


class Spread:
    def __init__(self, place, block, whole, to_sequences, chunks, refs):
        self.p, self.block, self.whole, self.forward, self.n = place, block, whole, to_sequences, chunks
        *keep, self.sems, self.copy_sems = refs
        self.keep = keep[0] if keep else None
        self.rows = whole.shape[0]
        self.cols = block.shape[1]
        self.step = self.rows // chunks

    @staticmethod
    def scratch(rows, cols, chunks):
        return [
            pltpu.VMEM((rows, cols), BF),
            pltpu.SemaphoreType.DMA((2, 3 * chunks)),
            pltpu.SemaphoreType.DMA((max(2, chunks),)),
        ]

    def ends(self, to_row, to_col, row, col, k=None):
        if self.forward:
            seq, part = 2 * to_row + to_col, 2 * row + col
        else:
            seq, part = 2 * row + col, 2 * to_row + to_col
        start, size = (0, self.rows) if k is None else (k * self.step, self.step)
        narrow = self.block.at[pl.ds(pl.multiple_of(seq * self.rows + start, 16), size)]
        wide = self.whole.at[
            pl.ds(start, size), pl.ds(pl.multiple_of(part * self.cols, 128), self.cols)
        ]
        return (narrow, wide) if self.forward else (wide, narrow)

    def copy(self, which, k, incoming):
        p = self.p
        row, col = ((p.row, 1 - p.col), (1 - p.row, 1 - p.col), (1 - p.row, p.col))[which]
        device = (p.across, p.diagonal, p.beside)[which]
        src, dst = self.ends(row, col, p.row, p.col, k)
        if incoming:
            dst = self.ends(p.row, p.col, row, col, k)[1]
        return send(src, dst, self.sems, 3 * k + which, device)

    def load(self):
        p = self.p
        return pltpu.make_async_copy(self.ends(p.row, p.col, p.row, p.col)[0], self.keep, self.copy_sems.at[0])

    def store(self):
        p = self.p
        return pltpu.make_async_copy(self.keep, self.ends(p.row, p.col, p.row, p.col)[1], self.copy_sems.at[1])

    def start(self):
        self.load().start()

    def straight(self, k):
        p = self.p
        return pltpu.make_async_copy(*self.ends(p.row, p.col, p.row, p.col, k), self.copy_sems.at[k])

    def issue(self, k):
        for which in range(3):
            self.copy(which, k, False).start()
        if self.keep is None:
            self.straight(k).start()

    def settle(self):
        self.load().wait()
        self.store().start()

    def arrived(self, k):
        for which in range(3):
            self.copy(which, k, True).wait_recv()

    def relayed(self, k):
        pass

    def ended(self, k):
        pass

    def finish(self):
        if self.keep is not None:
            self.store().wait()
        for k in range(self.n):
            if self.keep is None:
                self.straight(k).wait()
            for which in range(3):
                self.copy(which, k, False).wait_send()


ANY = pl.BlockSpec(memory_space=pl.ANY)


FIRST_CHUNKS = 2


def front_kernel(dp_size, tokens, weight, small, x, full, smalls, *refs):
    p = Place(dp_size)
    p.meet([p.across, p.beside, p.diagonal, p.peers[0], p.peers[1]])
    gather = Gather(p, weight, full, 0, FIRST_CHUNKS, refs[:3])
    spread = Spread(p, tokens, x, True, FIRST_CHUNKS, refs[3:6])
    small_sems, keep_sem = refs[6:]
    items = [(gather, k) for k in range(FIRST_CHUNKS)] + [(spread, k) for k in range(FIRST_CHUNKS)]
    mine = 2 * p.row + p.col
    others = (
        (2 * p.row + 1 - p.col, p.across),
        (2 * (1 - p.row) + p.col, p.beside),
        (2 * (1 - p.row) + 1 - p.col, p.diagonal),
    )
    gather.start()
    keep = pltpu.make_async_copy(small, smalls.at[mine], keep_sem)
    keep.start()
    for k, (_, device) in enumerate(others):
        send(small, smalls.at[mine], small_sems, k, device).start()
    spread.start()
    for item, k in items:
        item.issue(k)
    gather.settle()
    spread.settle()
    for k in range(FIRST_CHUNKS):
        gather.arrived(k)
    for k in range(FIRST_CHUNKS):
        gather.relayed(k)
    for k in range(FIRST_CHUNKS):
        gather.ended(k)
    for k in range(FIRST_CHUNKS):
        spread.arrived(k)
    keep.wait()
    for k, (index, device) in enumerate(others):
        send(small, smalls.at[mine], small_sems, k, device).wait_send()
        send(small, smalls.at[index], small_sems, k, device).wait_recv()
    gather.finish()
    spread.finish()


def front(dp_size, tokens, weight, small):
    rows, width = tokens.shape
    return pl.pallas_call(
        partial(front_kernel, dp_size),
        in_specs=[ANY] * 2 + [pl.BlockSpec(memory_space=pltpu.VMEM)],
        out_specs=[ANY] * 2 + [pl.BlockSpec(memory_space=pltpu.VMEM)],
        out_shape=[
            jax.ShapeDtypeStruct((rows // 4, width * 4), BF),
            jax.ShapeDtypeStruct((2 * weight.shape[0], 2 * weight.shape[1]), BF),
            jax.ShapeDtypeStruct((4,) + small.shape, F32),
        ],
        scratch_shapes=Gather.scratch(weight.shape, FIRST_CHUNKS)
        + Spread.scratch(rows // 4, width, FIRST_CHUNKS)
        + [pltpu.SemaphoreType.DMA((2, 3)), pltpu.SemaphoreType.DMA],
        compiler_params=pltpu.CompilerParams(collective_id=0, has_side_effects=True),
        name="front",
    )(tokens, weight, small)


SUMS = 16


def tail_kernel(dp_size, span, normed_t, joined_grad, weight, x, hidden_grad, state, gain, small, *refs):
    ends = len(weights_done(span))
    finished, (narrow, small_out), refs = refs[:ends], refs[ends : ends + 2], refs[ends + 2 :]
    normed_v, grad_v, weight_v, x_v, hidden_v, tokens_v, held, load_sems, turn, *refs = refs
    p = Place(dp_size)
    p.meet([p.across, p.beside, p.diagonal] + p.all_rings())
    four = 2 * p.row + p.col
    rounds = [(four, [p.across, p.beside, p.diagonal])] + [(ring.flag, ring.devices()) for ring in p.rings]
    *refs, spread_sems, straight_sems, bit_sem, lots = refs
    reduction = Reduce(p, span, None, state, finished, None, refs, held=held, turn=turn)
    spread = Spread(p, narrow, tokens_v, False, 4, (spread_sems, straight_sems))
    loads = [
        pltpu.make_async_copy(src, dst, load_sems.at[i])
        for i, (src, dst) in enumerate(
            ((joined_grad, grad_v), (normed_t, normed_v), (weight, weight_v), (x, x_v), (hidden_grad, hidden_v))
        )
    ]
    loads[0].start()
    loads[1].start()
    reduction.begin()
    for load in loads[2:]:
        load.start()
    first, n = span.before, span.fresh
    half = joined_grad.shape[1] // 2

    def partial_sum(mine, k):
        col = p.col if mine else 1 - p.col
        columns = pl.ds(pl.multiple_of(col * half + k * WIDE, WIDE), WIDE)
        held[mine * n + k] = bdot(normed_v[...], grad_v[:, columns], 1, 0).astype(BF)
        reduction.beside(mine, first + k, mine * n + k).start()

    def cross(k):
        reduction.pair(0, first + k, k)
        reduction.crossing(first + k).start()

    loads[0].wait()
    loads[1].wait()
    partial_sum(0, 0)
    partial_sum(0, 1)
    cross(0)
    reduction.resumed()
    reduction.sum_on(span.start)
    partial_sum(0, 2)
    cross(1)
    partial_sum(0, 3)
    cross(2)
    partial_sum(0, 4)
    reduction.sum_on(span.start + 1)
    partial_sum(0, 5)
    for k in range(n):
        partial_sum(1, k)
        if k:
            reduction.pair(1, first + k - 1, n + k - 1)
    reduction.pair(1, first + n - 1, 2 * n - 1)
    for load in loads[2:]:
        load.wait()

    tick = first
    size = x.shape[0] // 4
    gain_sum = shift_sum = column_sum = 0.0
    for k in range(4):
        at = slice(k * size, (k + 1) * size)
        rows = grad_v[at]
        column_sum = column_sum + jnp.sum(rows.astype(F32), axis=0, keepdims=True)
        upstream = bdot(rows, weight_v[...], 1, 1)
        centered, scale, _ = normed(x_v[at].astype(F32), 1.0, 0.0)
        back, gains, shifts = norm_backward(upstream, centered, scale, gain[...])
        gain_sum, shift_sum = gain_sum + gains, shift_sum + shifts
        tokens_v[at] = (hidden_v[at] + back).astype(BF)
        if k < n - CROSSING:
            reduction.sum_on(tick)
            tick += 1
            cross(CROSSING + k)
    width = x.shape[1]
    total = jnp.concatenate(
        [gain_sum, shift_sum, small[2:10]]
        + [column_sum[:, k * width : (k + 1) * width] for k in range(3)]
        + [small[13:]],
        0,
    )
    lane, copies = 0, []
    for b, (index, devices) in enumerate(rounds):
        lots[b, index] = total
        for device in devices:
            copies.append(send(lots.at[b, index], lots.at[b, index], bit_sem, lane, device))
            copies[-1].start()
            lane += 1
        for _ in range(2):
            reduction.sum_on(tick)
            tick += 1
            if tick - first - n + CROSSING in range(1, 5):
                spread.issue(tick - first - n + CROSSING - 1)
        for copy in copies[-len(devices) :]:
            copy.wait_recv()
        total = lots[b, 0]
        for k in range(1, len(devices) + 1):
            total = total + lots[b, k]
    small_out[...] = total

    def body(i, carry):
        reduction.sum_on(i)
        return carry

    lax.fori_loop(tick, span.stop, body, 0)
    for copy in copies:
        copy.wait_send()
    for k in range(4):
        spread.arrived(k)
    spread.finish()
    reduction.finish()


def tail(dp_size, normed_t, joined_grad, weight, x, hidden_grad, state, gain, small):
    sizes = radices(dp_size)
    levels = len(sizes)
    n, width = x.shape
    rows = width // 2
    span = split_of(levels)[2]
    return pl.pallas_call(
        partial(tail_kernel, dp_size, span),
        in_specs=[ANY] * 6 + [pl.BlockSpec(memory_space=pltpu.VMEM)] * 2,
        out_specs=[ANY] * (len(weights_done(span)) + 1) + [pl.BlockSpec(memory_space=pltpu.VMEM)],
        out_shape=blocks_like(span, rows)
        + [
            jax.ShapeDtypeStruct((4 * n, width // 4), BF),
            jax.ShapeDtypeStruct(small.shape, F32),
        ],
        scratch_shapes=[
            pltpu.VMEM(normed_t.shape, BF),
            pltpu.VMEM(joined_grad.shape, BF),
            pltpu.VMEM(weight.shape, BF),
            pltpu.VMEM(x.shape, BF),
            pltpu.VMEM(x.shape, F32),
            pltpu.VMEM(x.shape, BF),
            pltpu.VMEM((2 * span.fresh, width, WIDE), BF),
            pltpu.SemaphoreType.DMA((5,)),
        ]
        + turning(span, rows)
        + Reduce.scratch(span, rows, sizes)
        + Spread.scratch(n, width // 4, 4)[1:]
        + [
            pltpu.SemaphoreType.DMA((2, 3 + sum(size - 1 for size in sizes))),
            pltpu.VMEM((levels + 1, 4) + small.shape, F32),
        ],
        compiler_params=pltpu.CompilerParams(
            collective_id=3, has_side_effects=True, vmem_limit_bytes=61 << 20
        ),
        name="tail",
    )(normed_t, joined_grad, weight, x, hidden_grad, state, gain.reshape(1, -1), small)


GATHERED = ((1, 2), (0, 4), (1, 4))
QUARTERS = 4


def attend_kernel(dp_size, slopes, x, weight, bias, gain, shift, out_bias, second_gain, second_shift, *refs):
    blocks, grads, refs = refs[:3], refs[3], refs[4:]
    joined, lse_ref, normed_t, attended, hidden, second, second_t, *refs = refs
    wholes, og, (first, output_v, output_sem), refs = refs[:3], refs[3], refs[4:7], refs[7:]
    output = pltpu.make_async_copy(output_v, wholes[0], output_sem)
    wholes = [output_v, *wholes[1:]]
    step, last = pl.program_id(0), pl.num_programs(0) - 1
    p = Place(dp_size)
    gathers = [
        Gather(p, block, whole, dim, chunks, refs[3 * i : 3 * i + 3])
        for i, (block, whole, (dim, chunks)) in enumerate(zip(blocks, wholes, GATHERED))
    ]
    spread = Spread(p, grads, og, True, 4, refs[9:12])
    items = [(g, k) for g in gathers + [spread] for k in range(g.n)]
    n = x.shape[0]
    size = n // QUARTERS

    @pl.when(step == 0)
    def _():
        p.meet([p.across, p.beside, p.diagonal, p.peers[0], p.peers[1]])
        for g in gathers + [spread]:
            g.start()
        first_moves(items)
        for k in range(QUARTERS):
            at = slice(k * size, (k + 1) * size)
            value = normed(x[at].astype(F32), gain[...], shift[...])[2]
            first[at] = value
            normed_t[:, at] = value.T

    joined[...] = (bdot(first[...], weight[...], 1, 0) + bias[...]).astype(BF)
    out = attended.at[:, pl.ds(pl.multiple_of(step * 2 * HD, 2 * HD), 2 * HD)]
    attend_step(slopes, joined, out, lse_ref)

    @pl.when(step == 1)
    def _():
        for g in gathers + [spread]:
            g.settle()

    marks = [max(0, (7 * (i - 1)) // 5) for i in range(9)]
    for i in range(1, 7):

        @pl.when(step == i)
        def _(i=i):
            for t in range(marks[i], marks[i + 1]):
                move_on(items, t)

    @pl.when(step == last)
    def _():
        t = max(marks[7], GATHERED[0][1] + 2 * LAG)
        for i in range(marks[7], t):
            move_on(items, i)
        gathers[0].finish()
        output.start()
        for k in range(QUARTERS):
            at = slice(k * size, (k + 1) * size)
            value = x[at].astype(F32) + bdot(attended[at], wholes[0][...], 1, 0) + out_bias[...]
            hidden[at] = value
            value = normed(value, second_gain[...], second_shift[...])[2]
            second[at] = value
            second_t[:, at] = value.T
            move_on(items, t)
            t += 1
        for i in range(t, len(items) + 2 * LAG):
            move_on(items, i)
        for g in gathers[1:] + [spread]:
            g.finish()
        output.wait()


def attend(dp_size, slopes, x, weight, bias, vectors, weights, grads):
    n, width = x.shape
    pairs = weight.shape[1] // (6 * HD)
    rows, cols = grads.shape[0] // 4, grads.shape[1]
    whole = lambda shape: pl.BlockSpec(shape, lambda h, s: (0, 0), pipeline_mode=pl.Buffered(1))
    fulls = [jax.ShapeDtypeStruct((2 * w.shape[0], 2 * w.shape[1]), BF) for w in weights]
    return pl.pallas_call(
        partial(attend_kernel, dp_size),
        grid_spec=pltpu.PrefetchScalarGridSpec(
            num_scalar_prefetch=1,
            grid=(pairs,),
            in_specs=[
                whole((n, width)),
                pl.BlockSpec((width, 6 * HD), lambda h, s: (0, h)),
                pl.BlockSpec((1, 6 * HD), lambda h, s: (0, h)),
            ]
            + [whole((1, width))] * 5
            + [ANY] * 4,
            out_specs=[
                pl.BlockSpec((n, 6 * HD), lambda h, s: (0, h)),
                pl.BlockSpec((1, 2, n), lambda h, s: (h, 0, 0)),
            ]
            + [whole((width, n)), whole((n, width)), whole((n, width)), whole((n, width)), whole((width, n))]
            + [ANY] * 4,
            scratch_shapes=[pltpu.VMEM((n, width), BF), pltpu.VMEM(fulls[0].shape, BF), pltpu.SemaphoreType.DMA]
            + sum((Gather.scratch(w.shape, g[1]) for w, g in zip(weights, GATHERED)), [])
            + Spread.scratch(rows, cols, 4),
        ),
        out_shape=[
            jax.ShapeDtypeStruct((n, weight.shape[1]), BF),
            jax.ShapeDtypeStruct((pairs, 2, n), F32),
            jax.ShapeDtypeStruct((width, n), BF),
            jax.ShapeDtypeStruct((n, width), BF),
            jax.ShapeDtypeStruct((n, width), F32),
            jax.ShapeDtypeStruct((n, width), BF),
            jax.ShapeDtypeStruct((width, n), BF),
        ]
        + fulls
        + [jax.ShapeDtypeStruct((rows, 4 * cols), BF)],
        compiler_params=pltpu.CompilerParams(
            vmem_limit_bytes=58 << 20, collective_id=1, has_side_effects=True
        ),
        cost_estimate=pl.CostEstimate(
            flops=40 * n * n * HD * pairs, bytes_accessed=n * 512 * pairs * 2, transcendentals=n * n * pairs
        ),
        name="attend",
    )(slopes, x, weight, bias.reshape(1, -1), *(v.reshape(1, -1) for v in vectors), *weights, grads)


def attend_back_kernel(dp_size, span, slopes, x_ref, do_ref, lse_ref, *refs):
    ends = len(weights_done(span))
    (up, out, state, whole), dx_ref, finished, refs = refs[:4], refs[4], refs[5 : 5 + ends], refs[5 + ends :]
    handed, narrow, dk_ref, dv_ref, turn, *refs = refs
    step, last = pl.program_id(0), pl.num_programs(0) - 1
    p = Place(dp_size)
    parts = chunk_list(span, (up, EARLY, FF // 2 // WIDE), (out, 0, D // 2 // WIDE))
    reduction = Reduce(p, span, parts, state, finished, handed, refs[:-3], turn=turn)
    spread = Spread(p, narrow, whole, False, 4, refs[-3:])

    @pl.when(step == 0)
    def _():
        p.meet([p.across, p.beside, p.diagonal] + p.all_rings())
        reduction.begin()
        spread.start()

    attend_back_step(slopes, x_ref, do_ref, lse_ref, dx_ref, dk_ref, dv_ref)

    @pl.when(step == 0)
    def _():
        reduction.ahead()
        reduction.resumed()
        spread.settle()

    ticks, steps = span.stop - span.start, SEQ_STEPS
    for s in range(steps):

        @pl.when(step == s)
        def _(s=s):
            reduction.run(span.start + ticks * s // steps, span.start + ticks * (s + 1) // steps)
            if s >= steps - 4:
                spread.issue(s - steps + 4)

    @pl.when(step == last)
    def _():
        reduction.finish()
        for k in range(4):
            spread.arrived(k)
        spread.finish()


SEQ_STEPS = H // 2


def attend_back(dp_size, slopes, joined, out_grads, lse, up, out, state, result):
    n, width = joined.shape
    pairs = width // (6 * HD)
    sizes = radices(dp_size)
    levels = len(sizes)
    span = split_of(levels)[1]
    block = up.shape[0] // 2
    rows, cols = 4 * result.shape[0], result.shape[1] // 4
    return pl.pallas_call(
        partial(attend_back_kernel, dp_size, span),
        grid_spec=pltpu.PrefetchScalarGridSpec(
            num_scalar_prefetch=1,
            grid=(pairs,),
            in_specs=[
                pl.BlockSpec((n, 6 * HD), lambda h, s: (0, h)),
                pl.BlockSpec((n, 2 * HD), lambda h, s: (0, h)),
                pl.BlockSpec((1, 2, n), lambda h, s: (h, 0, 0)),
            ]
            + [ANY] * 4,
            out_specs=[pl.BlockSpec((n, 6 * HD), lambda h, s: (0, h))] + [ANY] * (len(weights_done(span)) + 2),
            scratch_shapes=[pltpu.VMEM((n, HD), F32)] * 2
            + turning(span, block)
            + Reduce.scratch(span, block, sizes)
            + Spread.scratch(result.shape[0], cols, 4),
        ),
        out_shape=[jax.ShapeDtypeStruct(joined.shape, BF)]
        + blocks_like(span, block)
        + [
            chunks_like(span.left, block),
            jax.ShapeDtypeStruct((rows, cols), BF),
        ],
        compiler_params=pltpu.CompilerParams(
            vmem_limit_bytes=60 << 20, collective_id=2, has_side_effects=True
        ),
        cost_estimate=pl.CostEstimate(
            flops=80 * n * n * HD * pairs, bytes_accessed=n * 1024 * pairs * 2, transcendentals=n * n * pairs
        ),
        name="attend_back",
    )(slopes, joined, out_grads, lse, up, out, state, result)


TILE = 512
ROWS = 256


def hidden_tile(step):
    tiles = FF // TILE
    return lax.rem(step + (tiles // 2) * (1 - lax.axis_index("col")), tiles)


def feed_kernel(
    dp_size, span, normed_in, normed_t, grads, hidden, up, down, up_bias, down_bias, gain, output, attended,
    result, back, up_part, small, attended_grad, out_part, handed, *refs,
):
    total, pair, grads_t, held, output_v, bias_grad, load_sem, *refs = refs
    act, pre_grad = pair.at[0], pair.at[1]
    step, last = pl.program_id(0), pl.num_programs(0) - 1
    p = Place(dp_size)
    reduction = Reduce(p, span, None, None, (), handed, refs, held=held)
    tiles = FF // TILE
    half_tiles, per = tiles // 2, TILE // WIDE
    downs = half_tiles * per
    tile = hidden_tile(step)
    load = pltpu.make_async_copy(hidden, total, load_sem.at[0])
    loads = [pltpu.make_async_copy(output, output_v, load_sem.at[1])] + [
        pltpu.make_async_copy(attended.at[:, pl.ds(k * TILE, TILE)], pair.at[k], load_sem.at[2 + k])
        for k in range(2)
    ]

    @pl.when(step == 0)
    def _():
        load.start()
        loads[0].start()
        p.meet([p.across, p.beside] + p.all_rings())
        back[...] = jnp.zeros_like(back)
        grads_t[...] = grads[...].T
        load.wait()
        loads[0].wait()

    bias = up_bias[:, pl.ds(pl.multiple_of(tile * TILE, TILE), TILE)]
    n = normed_in.shape[0]
    bias_sum = jnp.zeros((1, TILE), F32)
    a = math.sqrt(2.0 / math.pi)
    b = 0.044715 * a
    for r in range(n // ROWS):
        at = slice(r * ROWS, (r + 1) * ROWS)
        u = bdot(normed_in[at], up[...], 1, 0) + bias
        act_grad = bdot(grads[at], down[...], 1, 1)
        square = u * u
        half = 0.5 + 0.5 * jnp.tanh(u * (a + b * square))
        value = u * half
        slope = half + 2.0 * value * (1.0 - half) * (a + 3.0 * b * square)
        value = value.astype(BF)
        grad = (act_grad * slope).astype(BF)
        bias_sum = bias_sum + jnp.sum(grad.astype(F32), axis=0, keepdims=True)
        act[at] = value
        pre_grad[at] = grad
        total[at] += bdot(value, down[...], 1, 0)
        back[at] += bdot(grad, up[...], 1, 1)
    bias_grad[:, pl.ds(pl.multiple_of(tile * TILE, TILE), TILE)] = bias_sum
    part = bdot(grads_t[...], act[...], 1, 0).astype(BF)
    for k in range(per):
        held[lax.rem(per * step + k, RING)] = part[:, k * WIDE : (k + 1) * WIDE]
    part = bdot(normed_t[...], pre_grad[...], 1, 0).astype(BF)
    up_part[...] = part

    @pl.when(lax.rem(step, half_tiles) == 0)
    def _():
        for k in range(EARLY):
            held[RING + k] = part[:, k * WIDE : (k + 1) * WIDE]

    def chunks_of(s):
        first = (s % half_tiles) * per
        return s // half_tiles, [(first + k, (per * s + k) % RING) for k in range(per)]

    def early_of(s):
        return [(downs + k, RING + k) for k in range(EARLY)] if s % half_tiles == 0 else []

    def added(s):
        mine, chunks = chunks_of(s)
        for k, slot in chunks + early_of(s):
            reduction.pair(mine, k, slot)
        for k, _ in chunks + early_of(s):
            if not mine:
                reduction.crossing(k).start()

    for s in range(tiles):

        @pl.when(step == s)
        def _(s=s):
            mine, chunks = chunks_of(s)
            for k, slot in chunks + early_of(s):
                reduction.beside(mine, k, slot).start()
            if s:
                added(s - 1)
                if (s - 1) // half_tiles:
                    for k, _ in chunks_of(s - 1)[1]:
                        if k < span.stop:
                            reduction.sum_on(k)

    @pl.when(step == last)
    def _():
        for k in range(2):
            loads[1 + k].start()
        result[...] = (total[...] + down_bias[...]).astype(BF)
        load.start()
        load.wait()
        added(tiles - 1)
        sums = [jnp.zeros((1, back.shape[1]), F32)] * 4
        for r in range(n // ROWS):
            at = slice(r * ROWS, (r + 1) * ROWS)
            centered, scale, _ = normed(total[at], 1.0, 0.0)
            upstream = grads[at].astype(F32)
            change, gains, shifts = norm_backward(back[at], centered, scale, gain[...])
            value = upstream + change
            back[at] = value
            grads_t[at] = value.astype(BF)
            attended_grad[at] = bdot(grads_t[at], output_v[...], 1, 1).astype(BF)
            new = (jnp.sum(value, axis=0, keepdims=True), gains, shifts, jnp.sum(upstream, axis=0, keepdims=True))
            sums = [x + y for x, y in zip(sums, new)]
        width = back.shape[1]
        small[...] = jnp.concatenate(
            [jnp.zeros((2, width), F32)]
            + sums
            + [bias_grad[:, k * width : (k + 1) * width] for k in range(FF // width)]
            + [jnp.zeros((SUMS - 6 - FF // width, width), F32)],
            0,
        )
        for k in range(2):
            loads[1 + k].wait()
            out_part[:, k * TILE : (k + 1) * TILE] = bdot(grads_t[...], pair[k], 0, 0).astype(BF)
        reduction.finish()


RING = 6


def feed(dp_size, normed_in, normed_t, grads, hidden, up, down, up_bias, down_bias, gain, output, attended):
    n, width = normed_in.shape
    sizes = radices(dp_size)
    rows, span = width // 2, split_of(len(sizes))[0]
    whole = lambda shape: pl.BlockSpec(shape, lambda s: (0, 0), pipeline_mode=pl.Buffered(1))
    return pl.pallas_call(
        partial(feed_kernel, dp_size, span),
        grid=(FF // TILE,),
        in_specs=[
            whole((n, width)),
            whole((width, n)),
            whole((n, width)),
            ANY,
            pl.BlockSpec((width, TILE), lambda s: (0, hidden_tile(s))),
            pl.BlockSpec((TILE, width), lambda s: (hidden_tile(s), 0)),
            whole((1, FF)),
            whole((1, width)),
            whole((1, width)),
            ANY,
            ANY,
        ],
        out_specs=[
            whole((n, width)),
            whole((n, width)),
            pl.BlockSpec((width, TILE), lambda s: (0, hidden_tile(s))),
            whole((SUMS, width)),
            whole((n, width)),
            whole((width, width)),
            ANY,
        ],
        out_shape=[
            jax.ShapeDtypeStruct((n, width), BF),
            jax.ShapeDtypeStruct((n, width), F32),
            jax.ShapeDtypeStruct((width, FF), BF),
            jax.ShapeDtypeStruct((SUMS, width), F32),
            jax.ShapeDtypeStruct((n, width), BF),
            jax.ShapeDtypeStruct((width, width), BF),
            chunks_like(span.left, rows),
        ],
        scratch_shapes=[
            pltpu.VMEM((n, width), F32),
            pltpu.VMEM((2, n, TILE), BF),
            pltpu.VMEM((width, n), BF),
            pltpu.VMEM((RING + EARLY, width, WIDE), BF),
            pltpu.VMEM((width, width), BF),
            pltpu.VMEM((1, FF), F32),
            pltpu.SemaphoreType.DMA((4,)),
        ]
        + Reduce.scratch(span, rows, sizes),
        compiler_params=pltpu.CompilerParams(
            vmem_limit_bytes=62 << 20, collective_id=4, has_side_effects=True
        ),
        cost_estimate=pl.CostEstimate(
            flops=12 * n * width * FF, bytes_accessed=6 * width * FF, transcendentals=n * FF
        ),
        name="feed",
    )(
        normed_in, normed_t, grads, hidden, up, down,
        up_bias.reshape(1, -1), down_bias.reshape(1, -1), gain.reshape(1, -1), output, attended,
    )


def normed(values, gain, shift):
    average = jnp.mean(values, axis=1, keepdims=True)
    away = values - average
    scale = lax.rsqrt(jnp.mean(away * away, axis=1, keepdims=True) + EPSILON)
    centered = away * scale
    return centered, scale, (centered * gain + shift).astype(BF)


def norm_backward(upstream, centered, scale, gain):
    scaled = upstream * gain
    back = scale * (
        scaled
        - jnp.mean(scaled, axis=1, keepdims=True)
        - centered * jnp.mean(scaled * centered, axis=1, keepdims=True)
    )
    return back, jnp.sum(upstream * centered, axis=0, keepdims=True), jnp.sum(upstream, axis=0, keepdims=True)


def local(
    dp_size,
    tokens,
    first_gain,
    first_shift,
    joined_weight,
    query_value_bias,
    output_weight,
    output_bias,
    second_gain,
    second_shift,
    up_weight,
    up_bias,
    down_weight,
    down_bias,
    out_grad,
):
    heads = query_value_bias.shape[0] * 4
    w = D // 4
    small = jnp.concatenate(
        [
            first_gain,
            first_shift,
            output_bias,
            second_gain,
            second_shift,
            down_bias,
            up_bias,
            query_value_bias.reshape(-1),
        ]
    ).reshape(-1, 128)
    x, wj, small = front(dp_size, tokens, joined_weight, small)
    small = small.reshape(2, 2, -1)
    g1, s1, ob, g2, s2, db = (small[:, :, w * k : w * (k + 1)].reshape(-1) for k in range(6))

    def hidden_vector(start, size):
        return small[:, :, start : start + size].transpose(1, 0, 2).reshape(-1)

    ub = hidden_vector(6 * w, up_bias.shape[0])
    pair_bias = hidden_vector(6 * w + up_bias.shape[0], query_value_bias.size).reshape(heads, 2, HD)
    qv_bias = jnp.concatenate(
        [pair_bias[:, :1], jnp.zeros((heads, 1, HD), F32), pair_bias[:, 1:]], axis=1
    ).reshape(-1)
    slopes = jnp.exp2(-8.0 * (jnp.arange(heads).astype(F32) + 1.0) / heads)

    joined, lse, normed_t, attended, hidden, second, second_t, wo, wu, wd, og = attend(
        dp_size, slopes, x, wj, qv_bias, (g1, s1, ob, g2, s2), (output_weight, up_weight, down_weight), out_grad
    )
    result, hidden_grad, up_part, sums_in, attended_grad, output_part, state = feed(
        dp_size, second, second_t, og, hidden, wu, wd, ub, db, g2, wo, attended
    )
    joined_grad, *sums, state, result = attend_back(
        dp_size, slopes, joined, attended_grad, lse, up_part, output_part, state, result
    )
    *more, tokens_grad, totals = tail(
        dp_size, normed_t, joined_grad, wj, x, hidden_grad, state, g1, sums_in
    )
    down_weight_grad, up_weight_grad, output_weight_grad, joined_weight_grad = (
        total.astype(F32) for total in sums + more
    )
    row, col = lax.axis_index("row"), lax.axis_index("col")
    features = lax.dynamic_slice(totals, (0, (2 * row + col) * w), (6, w))
    fg, fs, obg, sg, ss, dbg = features
    ubg = lax.dynamic_index_in_dim(totals[6:10].reshape(4, -1), 2 * col + row, 0, False)
    columns = lax.dynamic_index_in_dim(totals[10:13].reshape(4, -1), 2 * col + row, 0, False)
    columns = columns.reshape(-1, 3, HD)
    qvg = jnp.concatenate([columns[:, 0], columns[:, 2]], axis=1)
    return (
        result,
        tokens_grad.astype(F32),
        fg,
        fs,
        joined_weight_grad,
        qvg,
        output_weight_grad,
        obg,
        sg,
        ss,
        up_weight_grad,
        ubg,
        down_weight_grad,
        dbg,
    )


def solution(mesh):
    feature = P(("row", "col"))
    in_specs = (
        P("dp", ("row", "col")),
        feature,
        feature,
        P("row", "col"),
        P(("col", "row"), None),
        P("col", "row"),
        feature,
        feature,
        feature,
        P("row", "col"),
        P(("col", "row")),
        P("col", "row"),
        feature,
        P("dp", ("row", "col")),
    )
    out_specs = (
        P("dp", ("row", "col")),
        P("dp", ("row", "col")),
        feature,
        feature,
        P("row", "col"),
        P(("col", "row"), None),
        P("col", "row"),
        feature,
        feature,
        feature,
        P("row", "col"),
        P(("col", "row")),
        P("col", "row"),
        feature,
    )
    return jax.shard_map(
        partial(local, mesh.shape["dp"]),
        mesh=mesh,
        in_specs=in_specs,
        out_specs=out_specs,
        check_vma=False,
    )
```

```python
import math
from functools import partial

import jax
import jax.numpy as jnp
from jax import lax
from jax.experimental import pallas as pl
from jax.experimental.pallas import tpu as pltpu
from jax.sharding import PartitionSpec as P

D = 1024
H = 16
HD = 64
FF = 4096
SEQ_LEN = 1024
QB = 256
EPSILON = 1e-05
L2E = math.log2(math.e)
BF = jnp.bfloat16
F32 = jnp.float32
MESH = pl.DeviceIdType.MESH


def bdot(a, b, ca, cb):
    return lax.dot_general(a, b, (((ca,), (cb,)), ((), ())), preferred_element_type=F32)


def bias_cols(slope, n):
    j = lax.broadcasted_iota(jnp.int32, (n, HD), 0).astype(F32)
    lane = lax.broadcasted_iota(jnp.int32, (n, HD), 1)
    full = j * (slope * 8.0)
    hi = full.astype(BF)
    rest = full - hi.astype(F32)
    mid = rest.astype(BF)
    low = (rest - mid.astype(F32)).astype(BF)
    return jnp.where(lane == 0, hi, jnp.where(lane == 1, mid, jnp.where(lane == 2, low, jnp.zeros_like(hi))))


def block_scores(keys, queries, stop, i):
    z = bdot(keys[:stop], queries[i * QB : (i + 1) * QB], 1, 1) * (HD ** (-0.5) * L2E)
    row = lax.broadcasted_iota(jnp.int32, (QB, QB), 0)
    col = lax.broadcasted_iota(jnp.int32, (QB, QB), 1)
    last = jnp.where(row <= col, z[stop - QB :], -1e30)
    return last if stop == QB else jnp.concatenate([z[: stop - QB], last], 0)


def attend_step(slopes, x_ref, o_ref, lse_ref):
    n = x_ref.shape[0]
    pair = pl.program_id(0)
    ones = jnp.ones((n, HD), BF)
    heads = []
    for t in range(2):
        base = 3 * HD * t
        q, k, v = (x_ref[:, base + HD * s : base + HD * (s + 1)] for s in range(3))
        keys = jnp.concatenate([k, bias_cols(slopes[2 * pair + t], n)], 1)
        queries = jnp.concatenate([q, ones], 1)
        pieces = []
        for i in range(n // QB):
            stop = QB * (i + 1)
            z = block_scores(keys, queries, stop, i)
            top = jnp.max(z, 0, keepdims=True)
            p = jnp.exp2(z - top)
            total = jnp.sum(p, 0, keepdims=True)
            pieces.append((bdot(v[:stop], p.astype(BF), 0, 0) / total).T)
            lse_ref[0, t : t + 1, i * QB : stop] = top + jnp.log2(total)
        heads.append(jnp.concatenate(pieces, 0))
    o_ref[...] = jnp.concatenate(heads, 1).astype(BF)


def attend_back_step(slopes, x_ref, do_ref, lse_ref, dx_ref, dk_ref, dv_ref):
    n = x_ref.shape[0]
    pair = pl.program_id(0)
    ones = jnp.ones((n, HD), BF)
    parts = []
    for t in range(2):
        base = 3 * HD * t
        q, k, v = (x_ref[:, base + HD * s : base + HD * (s + 1)] for s in range(3))
        do = do_ref[:, HD * t : HD * (t + 1)]
        keys = jnp.concatenate([k, bias_cols(slopes[2 * pair + t], n)], 1)
        queries = jnp.concatenate([q, ones], 1)
        dq = []
        for i in reversed(range(n // QB)):
            stop = QB * (i + 1)
            rows = slice(i * QB, stop)
            z = block_scores(keys, queries, stop, i)
            p = jnp.exp2(z - lse_ref[0, t : t + 1, rows])
            dp = bdot(v[:stop], do[rows], 1, 1)
            total = jnp.sum(p * dp, 0, keepdims=True)
            ds = (p * (dp - total)).astype(BF)
            dq.append(bdot(k[:stop], ds, 0, 0).T)
            dk = bdot(ds, q[rows], 1, 0)
            dv = bdot(p.astype(BF), do[rows], 1, 0)
            if stop == n:
                dk_ref[...] = dk
                dv_ref[...] = dv
            else:
                dk_ref[:stop] += dk
                dv_ref[:stop] += dv
        scale = HD ** (-0.5)
        parts += [jnp.concatenate(dq[::-1], 0) * scale, dk_ref[...] * scale, dv_ref[...]]
    dx_ref[...] = jnp.concatenate(parts, 1).astype(BF)


def radices(dp_size):
    sizes = []
    while dp_size > 1:
        sizes.append(4 if dp_size % 4 == 0 and dp_size != 8 else 2)
        dp_size //= sizes[-1]
    return sizes


class Ring:
    def __init__(self, dp, size, stride):
        self.dp, self.size, self.stride = dp, size, stride
        self.flag = lax.rem(dp // stride, size)

    def index(self, q):
        return lax.rem(self.flag + q + self.size, self.size)

    def device(self, q):
        return {"dp": self.dp + (self.index(q) - self.flag) * self.stride}

    def devices(self):
        return [self.device(q) for q in range(1, self.size)]


class Place:
    def __init__(self, dp_size):
        self.row = lax.axis_index("row")
        self.col = lax.axis_index("col")
        self.dp = lax.axis_index("dp")
        self.bits = [1 << b for b in range(dp_size.bit_length() - 1)]
        self.across = {"col": 1 - self.col}
        self.beside = {"row": 1 - self.row}
        self.diagonal = {"row": 1 - self.row, "col": 1 - self.col}
        self.rings, stride = [], 1
        for size in radices(dp_size):
            self.rings.append(Ring(self.dp, size, stride))
            stride *= size
        self.flags = [lax.rem(self.dp // bit, 2) for bit in self.bits]
        self.peers = [
            {"dp": self.dp + bit - 2 * bit * flag} for bit, flag in zip(self.bits, self.flags)
        ]

    def all_rings(self):
        return [device for ring in self.rings for device in ring.devices()]

    def meet(self, partners):
        barrier = pltpu.get_barrier_semaphore()
        for partner in partners:
            pl.semaphore_signal(barrier, inc=1, device_id=partner, device_id_type=MESH)
        pl.semaphore_wait(barrier, len(partners))


def send(src, dst, sems, k, device):
    return pltpu.make_async_remote_copy(
        src_ref=src,
        dst_ref=dst,
        send_sem=sems.at[0, k],
        recv_sem=sems.at[1, k],
        device_id=device,
        device_id_type=MESH,
    )


class Gather:
    def __init__(self, place, block, full, row_dim, chunks, refs):
        self.p, self.block, self.full, self.row_dim, self.n = place, block, full, row_dim, chunks
        self.keep, self.sems, self.copy_sems = refs
        self.rows, self.cols = block.shape
        self.part = self.rows // 4
        self.step = self.part // chunks

    @staticmethod
    def scratch(shape, chunks):
        return [
            pltpu.VMEM(shape, BF),
            pltpu.SemaphoreType.DMA((2, 1 + 8 * chunks)),
            pltpu.SemaphoreType.DMA((2,)),
        ]

    def region(self, row, col, part=None, k=0):
        first, second = (row, col) if self.row_dim == 0 else (col, row)
        start = pl.multiple_of(first * self.rows, 16)
        size = self.rows
        if part is not None:
            start = pl.multiple_of(start + part * self.part + k * self.step, 16)
            size = self.step
        return self.full.at[pl.ds(start, size), pl.ds(pl.multiple_of(second * self.cols, 128), self.cols)]

    def quarter(self, first=False, second=False):
        a, b = self.p.flags[0], self.p.flags[1]
        return 2 * (1 - b if second else b) + (1 - a if first else a)

    def load(self):
        return pltpu.make_async_copy(self.block, self.keep, self.copy_sems.at[0])

    def store(self):
        return pltpu.make_async_copy(self.keep, self.region(self.p.row, self.p.col), self.copy_sems.at[1])

    def beside(self, incoming):
        row = 1 - self.p.row if incoming else self.p.row
        return send(self.block, self.region(row, self.p.col), self.sems, 0, self.p.beside)

    def over(self, k, incoming):
        part = self.quarter()
        src = self.block.at[pl.ds(pl.multiple_of(part * self.part + k * self.step, 16), self.step)]
        col = 1 - self.p.col if incoming else self.p.col
        return send(src, self.region(self.p.row, col, part, k), self.sems, 1 + k, self.p.across)

    def relay(self, bit, k, incoming):
        src = self.region(self.p.row, 1 - self.p.col, self.quarter(), k)
        part = self.quarter(bit == 0, bit == 1) if incoming else self.quarter()
        dst = self.region(self.p.row, 1 - self.p.col, part, k)
        return send(src, dst, self.sems, 1 + (1 + bit) * self.n + k, self.p.peers[bit])

    def second(self, k, incoming):
        bit = k % 2
        src = self.region(self.p.row, 1 - self.p.col, self.quarter(bit == 1, bit == 0), k)
        part = self.quarter(True, True) if incoming else self.quarter(bit == 1, bit == 0)
        dst = self.region(self.p.row, 1 - self.p.col, part, k)
        return send(src, dst, self.sems, 1 + 3 * self.n + k, self.p.peers[bit])

    def hand(self, which, k, incoming):
        part = self.quarter(which in (1, 3), which in (2, 3))
        row = 1 - self.p.row if incoming else self.p.row
        src = self.region(self.p.row, 1 - self.p.col, part, k)
        dst = self.region(row, 1 - self.p.col, part, k)
        return send(src, dst, self.sems, 1 + (4 + which) * self.n + k, self.p.beside)

    def start(self):
        self.beside(False).start()
        self.load().start()

    def issue(self, k):
        self.over(k, False).start()

    def arrived(self, k):
        self.over(k, True).wait_recv()
        for bit in range(2):
            self.relay(bit, k, False).start()
        self.hand(0, k, False).start()

    def relayed(self, k):
        for bit in range(2):
            self.relay(bit, k, True).wait_recv()
            self.hand(1 + bit, k, False).start()
        self.second(k, False).start()

    def ended(self, k):
        self.second(k, True).wait_recv()
        self.hand(3, k, False).start()

    def settle(self):
        self.load().wait()
        self.store().start()

    def finish(self):
        self.store().wait()
        self.beside(False).wait_send()
        self.beside(True).wait_recv()
        for k in range(self.n):
            self.over(k, False).wait_send()
            self.second(k, False).wait_send()
            for bit in range(2):
                self.relay(bit, k, False).wait_send()
            for which in range(4):
                self.hand(which, k, False).wait_send()
                self.hand(which, k, True).wait_recv()


AHEAD = 4
LAG = 3


def move_on(items, t):
    for lag, name in ((2 * LAG, "ended"), (LAG, "relayed"), (0, "arrived"), (-AHEAD, "issue")):
        if 0 <= t - lag < len(items):
            item, k = items[t - lag]
            getattr(item, name)(k)


def first_moves(items):
    for item, k in items[:AHEAD]:
        item.issue(k)


WIDE = 256
CROSSING = 3


def split_of(levels):
    down, rest, joined = FF // 2 // WIDE, (FF + D) // 2 // WIDE, 3 * D // 2 // WIDE
    fresh = down + rest + GAP
    ticks = (0, FEED_TICKS, fresh - 3, fresh + joined + 4 * levels)
    ended = min(max(0, ticks[2] - 4 * levels + 2), 2 * down)
    return [
        Span(ticks[0], ticks[1], 0, down + EARLY, 0, 0, down + rest),
        Span(ticks[1], ticks[2], down + EARLY, down + rest, 0, ended, down + rest),
        Span(ticks[2], ticks[3], fresh, fresh + joined, ended, fresh + joined, down + rest),
    ]


FEED_TICKS = 10
GAP = 4
EARLY = 4


def numbering():
    down, out, joined = FF // 2 // WIDE, D // 2 // WIDE, 3 * D // 2 // WIDE
    order, per = [], TILE // WIDE
    for first in range(0, down, per):
        order += [("down", first + k) for k in range(per)]
        order += [("up", first + k) for k in range(per) if first + k < EARLY]
    order += [("up", k) for k in range(EARLY, down)] + [("out", k) for k in range(out)]
    numbers = {name: number for number, name in enumerate(order)}
    numbers.update({("joined", k): len(order) + GAP + k for k in range(joined)})
    return numbers


TURNED = ("down", "out")


def blocks_like(names, rows):
    count = {"down": FF, "up": FF, "out": D, "joined": 3 * D}
    return [
        jax.ShapeDtypeStruct((count[name] // 2, rows) if name in TURNED else (rows, count[name] // 2), BF)
        for name in names
    ]


def ending(span):
    return {number: name for name, number in numbering().items() if number in span.chunks() and number < span.done}


def turning(span, rows):
    count = sum(name in TURNED for name, _ in ending(span).values())
    return [pltpu.VMEM((max(1, count), WIDE, rows), BF)]


class Span:
    def __init__(self, start, stop, before, after, lo, done, gap):
        self.start, self.stop, self.before, self.after, self.lo, self.done = start, stop, before, after, lo, done
        self.gap = gap
        self.lead = before - start + 2
        self.hole = before - gap if before > gap else 0
        self.count = after - lo - self.hole
        self.fresh = after - before
        self.old = range(lo, min(before, gap))
        self.left = after - done

    def chunks(self):
        return [*self.old, *range(self.before, self.after)]

    def summed(self, levels):
        return max(1, sum(Reduce.pending(self.stop, k) >= levels for k in self.chunks()))

    def place(self, k):
        return k - self.lo - (self.hole * (k // self.before) if self.hole else 0)


class Reduce:
    def __init__(self, place, span, parts, state, finished, handed, refs, held=None, turn=None):
        self.p, self.span, self.parts, self.held = place, span, parts, held
        self.state, self.finished, self.handed, self.turn = state, finished, handed, turn
        self.rings = place.rings
        levels = self.levels = len(place.rings)
        self.own, self.other, *refs = refs
        self.got, self.over, self.full, *refs = refs
        self.landing = refs[:levels]
        self.load_sem, self.core_sem, self.over_sem, self.half_sem, self.back_sem, self.out_sem = refs[levels:]
        self.rows = self.full.shape[1]

    @staticmethod
    def scratch(span, rows, sizes):
        n, fresh = span.count, span.fresh
        landing, lanes, size = [], 0, rows
        for ring in sizes:
            size //= ring
            landing.append(pltpu.VMEM((ring - 1, n, size, WIDE), BF))
            lanes += ring - 1
        return (
            [
                pltpu.VMEM((n, rows, WIDE), BF),
                pltpu.VMEM((fresh, rows, WIDE), BF),
                pltpu.VMEM((2, fresh, rows, WIDE), BF),
                pltpu.VMEM((fresh, rows, WIDE), BF),
                pltpu.VMEM((span.summed(len(sizes)), rows, WIDE), BF),
            ]
            + landing
            + [
                pltpu.SemaphoreType.DMA((n + fresh,)),
                pltpu.SemaphoreType.DMA((2, 2 * fresh)),
                pltpu.SemaphoreType.DMA((2, fresh)),
                pltpu.SemaphoreType.DMA((2, lanes * n)),
                pltpu.SemaphoreType.DMA((2, lanes * n)),
                pltpu.SemaphoreType.DMA((n,)),
            ]
        )

    def lane(self, b, q):
        return sum(ring.size - 1 for ring in self.rings[:b]) + q - 1

    def size(self, b):
        return self.rows // math.prod(ring.size for ring in self.rings[: b + 1])


    def mine(self, k, start=0, size=None):
        size = self.rows if size is None else size
        return self.own.at[self.span.place(k), pl.ds(pl.multiple_of(start, 16), size)]

    def others(self, k):
        return self.other.at[k - self.span.before]

    def kept(self, row, slot):
        return self.held.at[slot, pl.ds(pl.multiple_of(row * self.rows, 16), self.rows)]

    def part(self, row, mine, k):
        ref, start = self.parts[k]
        col = self.p.col if mine else 1 - self.p.col
        start = pl.multiple_of(col * (ref.shape[1] // 2) + start, WIDE)
        return ref.at[pl.ds(pl.multiple_of(row * self.rows, 16), self.rows), pl.ds(start, WIDE)]

    def load(self, mine, k):
        dst = self.mine(k) if mine else self.others(k)
        return pltpu.make_async_copy(self.part(self.p.row, mine, k), dst, self.load_sem.at[self.load_at(mine, k)])

    def load_at(self, mine, k):
        return self.span.place(k) if mine else self.span.count + k - self.span.before

    def beside(self, mine, k, slot=None):
        if slot is None:
            src = self.part(1 - self.p.row, mine, k)
        else:
            src = self.kept(1 - self.p.row, slot)
        r = k - self.span.before
        return send(src, self.got.at[mine, r], self.core_sem, self.span.fresh * mine + r, self.p.beside)

    def landed(self, mine, k):
        r = k - self.span.before
        ref = self.got.at[mine, r]
        return send(ref, ref, self.core_sem, self.span.fresh * mine + r, self.p.beside)

    def crossing(self, k):
        r = k - self.span.before
        return send(self.others(k), self.over.at[r], self.over_sem, r, self.p.across)

    def offset(self, level):
        return sum((self.rings[b].flag * self.size(b) for b in range(level)), 0)

    def halving(self, b, q, k):
        ring, size, i = self.rings[b], self.size(b), self.span.place(k)
        return send(
            self.mine(k, self.offset(b) + ring.index(q) * size, size),
            self.landing[b].at[q - 1, i],
            self.half_sem,
            self.lane(b, q) * self.span.count + i,
            ring.device(q),
        )

    def doubling(self, b, q, k, incoming):
        ring, size, i = self.rings[b], self.size(b), self.span.place(k)
        start = self.offset(b) + ring.flag * size
        other = self.offset(b) + ring.index(-q) * size
        at = self.full.at[i, pl.ds(pl.multiple_of(start, 16), size)]
        to = self.full.at[i, pl.ds(pl.multiple_of(other if incoming else start, 16), size)]
        return send(at, to, self.back_sem, self.lane(b, q) * self.span.count + i, ring.device(q))

    def turns(self, b):
        return range(1, self.rings[b].size)

    def settled(self, j):
        b = 0 if j < self.levels else max(0, 2 * self.levels - j)
        size = self.size(b - 1) if b else self.rows
        return pl.ds(pl.multiple_of(self.offset(b), 16), size)

    def resume(self, k):
        i, j = self.span.place(k), self.pending(self.span.start, k)
        at = self.settled(j)
        dst = (self.own if j < self.levels else self.full).at[i, at]
        return pltpu.make_async_copy(self.state.at[i, at], dst, self.load_sem.at[i])

    @staticmethod
    def pending(tick, k):
        return max(0, (tick - k + 1) // 2)

    def begin(self):
        span = self.span
        for k in span.old:
            self.resume(k).start()
        if self.held is None:
            for mine in range(2):
                for k in range(span.before, span.after):
                    self.beside(mine, k).start()
                    self.load(mine, k).start()

    def resumed(self):
        for k in self.span.old:
            self.resume(k).wait()

    def pair(self, mine, k, slot=None):
        if slot is None:
            ref = self.mine(k) if mine else self.others(k)
            pltpu.make_async_copy(ref, ref, self.load_sem.at[self.load_at(mine, k)]).wait()
        self.landed(mine, k).wait_recv()
        ref = self.mine(k) if mine else self.others(k)
        here = ref if slot is None else self.kept(self.p.row, slot)
        ref[...] = here[...] + self.got[mine, k - self.span.before]
        if slot is not None:
            self.landed(mine, k).wait_send()

    def take(self, j, k):
        levels = self.levels
        i = self.span.place(k)
        if j == 0:
            self.crossing(k).wait_recv()
            ref = self.mine(k)
            ref[...] = ref[...] + self.over[k - self.span.before]
        elif j <= levels:
            b = j - 1
            start, size = self.offset(b + 1), self.size(b)
            ref = self.mine(k, start, size)
            total = ref[...].astype(F32)
            for q in self.turns(b):
                self.halving(b, q, k).wait_recv()
                total = total + self.landing[b][q - 1, i].astype(F32)
            total = total.astype(BF)
            if b + 1 < levels:
                ref[...] = total
            else:
                self.full[i, pl.ds(pl.multiple_of(start, 16), size)] = total
        else:
            b = 2 * levels - j
            for q in self.turns(b):
                self.doubling(b, q, k, True).wait_recv()

    def give(self, j, k):
        levels = self.levels
        if j < levels:
            for q in self.turns(j):
                self.halving(j, q, k).start()
        elif j < 2 * levels:
            b = 2 * levels - 1 - j
            for q in self.turns(b):
                self.doubling(b, q, k, False).start()

    def sum_on(self, t):
        span = self.span
        for j in reversed(range(1 + 2 * self.levels)):
            k = t - 2 * j
            old = (k < span.before) if j == 0 else (k < span.before) & (t < span.start + 2)

            @pl.when((k >= span.lo) & (k < span.after) & ((k < span.gap) | (k >= span.before)))
            def _(j=j, k=k, old=old):
                @pl.when(jnp.logical_not(old))
                def _():
                    self.take(j, k)

                self.give(j, k)

    def advance(self, t):
        span = self.span
        k = t + span.lead

        @pl.when((k >= span.before) & (k < span.after))
        def _():
            self.pair(0, k)
            self.crossing(k).start()

        @pl.when((k - 1 >= span.before) & (k - 1 < span.after))
        def _():
            self.pair(1, k - 1)

        self.sum_on(t)

    def ahead(self):
        span = self.span
        for k in range(span.before, min(span.after, span.start + span.lead)):
            self.pair(0, k)
            self.crossing(k).start()
        for k in range(span.before, min(span.after, span.start + span.lead - 1)):
            self.pair(1, k)

    def run(self, start, stop):
        def body(i, carry):
            self.advance(i)
            return carry

        lax.fori_loop(start, stop, body, 0)

    def finish(self):
        span, levels = self.span, self.levels
        copies, names, turned = [], ending(span), 0
        for k in span.chunks():
            i = span.place(k)
            j = self.pending(span.stop, k)
            if j <= 2 * levels and not (k < span.before and k >= span.stop):
                self.take(j, k)
            if k < span.done:
                name, place = names[k]
                out = self.finished[name]
                if name in TURNED:
                    self.turn[turned] = self.full[i].T
                    src, dst = self.turn.at[turned], out.at[pl.ds(place * WIDE, WIDE)]
                    turned += 1
                else:
                    src, dst = self.full.at[i], out.at[:, pl.ds(place * WIDE, WIDE)]
            else:
                at = self.settled(j)
                src = (self.own if j < levels else self.full).at[i, at]
                dst = self.handed.at[k - span.done, at]
            copy = pltpu.make_async_copy(src, dst, self.out_sem.at[i])
            copy.start()
            copies.append(copy)
        for r in range(span.before, span.after):
            if self.held is None:
                for mine in range(2):
                    self.landed(mine, r).wait_send()
            self.crossing(r).wait_send()
        for k in span.chunks():
            begun = self.pending(span.start, k) if k < span.before else 0
            ended = self.pending(span.stop, k)
            for j in range(begun, min(ended, 2 * levels)):
                b = j if j < levels else 2 * levels - 1 - j
                for q in self.turns(b):
                    if j < levels:
                        self.halving(b, q, k).wait_send()
                    else:
                        self.doubling(b, q, k, False).wait_send()
        for copy in copies:
            copy.wait()


def chunk_list(span, *arrays):
    places = [(ref, k * WIDE) for ref, first, last in arrays for k in range(first, last)]
    return dict(zip(range(span.before, span.after), places))


def chunks_like(count, rows):
    return jax.ShapeDtypeStruct((count, rows, WIDE), BF)


class Spread:
    def __init__(self, place, block, whole, to_sequences, chunks, refs):
        self.p, self.block, self.whole, self.forward, self.n = place, block, whole, to_sequences, chunks
        *keep, self.sems, self.copy_sems = refs
        self.keep = keep[0] if keep else None
        self.rows = whole.shape[0]
        self.cols = block.shape[1]
        self.step = self.rows // chunks

    @staticmethod
    def scratch(rows, cols, chunks):
        return [
            pltpu.VMEM((rows, cols), BF),
            pltpu.SemaphoreType.DMA((2, 3 * chunks)),
            pltpu.SemaphoreType.DMA((max(2, chunks),)),
        ]

    def ends(self, to_row, to_col, row, col, k=None):
        if self.forward:
            seq, part = 2 * to_row + to_col, 2 * row + col
        else:
            seq, part = 2 * row + col, 2 * to_row + to_col
        start, size = (0, self.rows) if k is None else (k * self.step, self.step)
        narrow = self.block.at[pl.ds(pl.multiple_of(seq * self.rows + start, 16), size)]
        wide = self.whole.at[
            pl.ds(start, size), pl.ds(pl.multiple_of(part * self.cols, 128), self.cols)
        ]
        return (narrow, wide) if self.forward else (wide, narrow)

    def copy(self, which, k, incoming):
        p = self.p
        row, col = ((p.row, 1 - p.col), (1 - p.row, 1 - p.col), (1 - p.row, p.col))[which]
        device = (p.across, p.diagonal, p.beside)[which]
        src, dst = self.ends(row, col, p.row, p.col, k)
        if incoming:
            dst = self.ends(p.row, p.col, row, col, k)[1]
        return send(src, dst, self.sems, 3 * k + which, device)

    def load(self):
        p = self.p
        return pltpu.make_async_copy(self.ends(p.row, p.col, p.row, p.col)[0], self.keep, self.copy_sems.at[0])

    def store(self):
        p = self.p
        return pltpu.make_async_copy(self.keep, self.ends(p.row, p.col, p.row, p.col)[1], self.copy_sems.at[1])

    def start(self):
        self.load().start()

    def straight(self, k):
        p = self.p
        return pltpu.make_async_copy(*self.ends(p.row, p.col, p.row, p.col, k), self.copy_sems.at[k])

    def issue(self, k):
        for which in range(3):
            self.copy(which, k, False).start()
        if self.keep is None:
            self.straight(k).start()

    def settle(self):
        self.load().wait()
        self.store().start()

    def arrived(self, k):
        for which in range(3):
            self.copy(which, k, True).wait_recv()

    def relayed(self, k):
        pass

    def ended(self, k):
        pass

    def finish(self):
        if self.keep is not None:
            self.store().wait()
        for k in range(self.n):
            if self.keep is None:
                self.straight(k).wait()
            for which in range(3):
                self.copy(which, k, False).wait_send()


ANY = pl.BlockSpec(memory_space=pl.ANY)


FIRST_CHUNKS = 2


def front_kernel(dp_size, tokens, weight, small, x, full, smalls, *refs):
    p = Place(dp_size)
    p.meet([p.across, p.beside, p.diagonal, p.peers[0], p.peers[1]])
    gather = Gather(p, weight, full, 0, FIRST_CHUNKS, refs[:3])
    spread = Spread(p, tokens, x, True, FIRST_CHUNKS, refs[3:6])
    small_sems, keep_sem = refs[6:]
    items = [(gather, k) for k in range(FIRST_CHUNKS)] + [(spread, k) for k in range(FIRST_CHUNKS)]
    mine = 2 * p.row + p.col
    others = (
        (2 * p.row + 1 - p.col, p.across),
        (2 * (1 - p.row) + p.col, p.beside),
        (2 * (1 - p.row) + 1 - p.col, p.diagonal),
    )
    gather.start()
    keep = pltpu.make_async_copy(small, smalls.at[mine], keep_sem)
    keep.start()
    for k, (_, device) in enumerate(others):
        send(small, smalls.at[mine], small_sems, k, device).start()
    spread.start()
    for item, k in items:
        item.issue(k)
    gather.settle()
    spread.settle()
    for k in range(FIRST_CHUNKS):
        gather.arrived(k)
    for k in range(FIRST_CHUNKS):
        gather.relayed(k)
    for k in range(FIRST_CHUNKS):
        gather.ended(k)
    for k in range(FIRST_CHUNKS):
        spread.arrived(k)
    keep.wait()
    for k, (index, device) in enumerate(others):
        send(small, smalls.at[mine], small_sems, k, device).wait_send()
        send(small, smalls.at[index], small_sems, k, device).wait_recv()
    gather.finish()
    spread.finish()


def front(dp_size, tokens, weight, small):
    rows, width = tokens.shape
    return pl.pallas_call(
        partial(front_kernel, dp_size),
        in_specs=[ANY] * 2 + [pl.BlockSpec(memory_space=pltpu.VMEM)],
        out_specs=[ANY] * 2 + [pl.BlockSpec(memory_space=pltpu.VMEM)],
        out_shape=[
            jax.ShapeDtypeStruct((rows // 4, width * 4), BF),
            jax.ShapeDtypeStruct((2 * weight.shape[0], 2 * weight.shape[1]), BF),
            jax.ShapeDtypeStruct((4,) + small.shape, F32),
        ],
        scratch_shapes=Gather.scratch(weight.shape, FIRST_CHUNKS)
        + Spread.scratch(rows // 4, width, FIRST_CHUNKS)
        + [pltpu.SemaphoreType.DMA((2, 3)), pltpu.SemaphoreType.DMA],
        compiler_params=pltpu.CompilerParams(collective_id=0, has_side_effects=True),
        name="front",
    )(tokens, weight, small)


SUMS = 16


def tail_kernel(dp_size, span, normed_t, joined_grad, weight, x, hidden_grad, state, vectors, small, *refs):
    _, _, *refs = refs
    finished, (narrow, small_out), refs = dict(zip(WEIGHTS, refs[:4])), refs[4:6], refs[6:]
    normed_v, grad_v, weight_v, x_v, hidden_v, tokens_v, held, load_sems, turn, *refs = refs
    p = Place(dp_size)
    p.meet([p.across, p.beside, p.diagonal] + p.all_rings())
    four = 2 * p.row + p.col
    rounds = [(four, [p.across, p.beside, p.diagonal])] + [(ring.flag, ring.devices()) for ring in p.rings]
    *refs, spread_sems, straight_sems, bit_sem, lots = refs
    reduction = Reduce(p, span, None, state, finished, None, refs, held=held, turn=turn)
    spread = Spread(p, narrow, tokens_v, False, 4, (spread_sems, straight_sems))
    loads = [
        pltpu.make_async_copy(src, dst, load_sems.at[i])
        for i, (src, dst) in enumerate(
            ((joined_grad, grad_v), (normed_t, normed_v), (weight, weight_v), (x, x_v), (hidden_grad, hidden_v))
        )
    ]
    loads[0].start()
    loads[1].start()
    reduction.begin()
    for load in loads[2:]:
        load.start()
    first, n = span.before, span.fresh
    half = joined_grad.shape[1] // 2

    def partial_sum(mine, k):
        col = p.col if mine else 1 - p.col
        columns = pl.ds(pl.multiple_of(col * half + k * WIDE, WIDE), WIDE)
        held[mine * n + k] = bdot(normed_v[...], grad_v[:, columns], 1, 0).astype(BF)
        reduction.beside(mine, first + k, mine * n + k).start()

    def cross(k):
        reduction.pair(0, first + k, k)
        reduction.crossing(first + k).start()

    loads[0].wait()
    loads[1].wait()
    partial_sum(0, 0)
    partial_sum(0, 1)
    cross(0)
    reduction.resumed()
    early = list(range(span.start, first))
    reduction.sum_on(early.pop(0))
    partial_sum(0, 2)
    cross(1)
    partial_sum(0, 3)
    cross(2)
    partial_sum(0, 4)
    reduction.sum_on(early.pop(0))
    partial_sum(0, 5)
    for k in range(n):
        partial_sum(1, k)
        if k:
            reduction.pair(1, first + k - 1, n + k - 1)
        if k % 2 and early:
            reduction.sum_on(early.pop(0))
    reduction.pair(1, first + n - 1, 2 * n - 1)
    for load in loads[2:]:
        load.wait()
    for t in early:
        reduction.sum_on(t)

    tick = first
    size = x.shape[0] // 4
    gain_sum = shift_sum = column_sum = 0.0
    for k in range(4):
        at = slice(k * size, (k + 1) * size)
        rows = grad_v[at]
        column_sum = column_sum + jnp.sum(rows.astype(F32), axis=0, keepdims=True)
        upstream = bdot(rows, weight_v[...], 1, 1)
        centered, scale, _ = normed(x_v[at].astype(F32), 1.0, 0.0)
        back, gains, shifts = norm_backward(upstream, centered, scale, vectors[0:1])
        gain_sum, shift_sum = gain_sum + gains, shift_sum + shifts
        tokens_v[at] = (hidden_v[at] + back).astype(BF)
        if k < n - CROSSING:
            reduction.sum_on(tick)
            tick += 1
            cross(CROSSING + k)
    width = x.shape[1]
    total = jnp.concatenate(
        [gain_sum, shift_sum, small[2:10]]
        + [column_sum[:, k * width : (k + 1) * width] for k in range(3)]
        + [small[13:]],
        0,
    )
    lane, copies = 0, []
    for b, (index, devices) in enumerate(rounds):
        lots[b, index] = total
        for device in devices:
            copies.append(send(lots.at[b, index], lots.at[b, index], bit_sem, lane, device))
            copies[-1].start()
            lane += 1
        for _ in range(2):
            reduction.sum_on(tick)
            tick += 1
            if tick - first - n in (0, 1):
                for k in range(2):
                    spread.issue(2 * (tick - first - n) + k)
        for copy in copies[-len(devices) :]:
            copy.wait_recv()
        total = lots[b, 0]
        for k in range(1, len(devices) + 1):
            total = total + lots[b, k]
    small_out[...] = total

    def body(i, carry):
        reduction.sum_on(i)
        return carry

    lax.fori_loop(tick, span.stop, body, 0)
    for copy in copies:
        copy.wait_send()
    for k in range(4):
        spread.arrived(k)
    spread.finish()
    reduction.finish()


def tail(dp_size, normed_t, joined_grad, weight, x, hidden_grad, state, vectors, small, begun):
    sizes = radices(dp_size)
    levels = len(sizes)
    n, width = x.shape
    rows = width // 2
    span = split_of(levels)[2]
    return pl.pallas_call(
        partial(tail_kernel, dp_size, span),
        in_specs=[ANY] * 6 + [pl.BlockSpec(memory_space=pltpu.VMEM)] * 2 + [ANY] * 2,
        out_specs=[ANY] * 5 + [pl.BlockSpec(memory_space=pltpu.VMEM)],
        input_output_aliases={8: 0, 9: 1},
        out_shape=blocks_like(WEIGHTS, rows)
        + [
            jax.ShapeDtypeStruct((4 * n, width // 4), BF),
            jax.ShapeDtypeStruct(small.shape, F32),
        ],
        scratch_shapes=[
            pltpu.VMEM(normed_t.shape, BF),
            pltpu.VMEM(joined_grad.shape, BF),
            pltpu.VMEM(weight.shape, BF),
            pltpu.VMEM(x.shape, BF),
            pltpu.VMEM(x.shape, F32),
            pltpu.VMEM(x.shape, BF),
            pltpu.VMEM((2 * span.fresh, width, WIDE), BF),
            pltpu.SemaphoreType.DMA((5,)),
        ]
        + turning(span, rows)
        + Reduce.scratch(span, rows, sizes)
        + Spread.scratch(n, width // 4, 4)[1:]
        + [
            pltpu.SemaphoreType.DMA((2, 3 + sum(size - 1 for size in sizes))),
            pltpu.VMEM((levels + 1, 4) + small.shape, F32),
        ],
        compiler_params=pltpu.CompilerParams(
            collective_id=3, has_side_effects=True, vmem_limit_bytes=61 << 20
        ),
        name="tail",
    )(normed_t, joined_grad, weight, x, hidden_grad, state, vectors, small, *begun)


WEIGHTS = ("down", "up", "out", "joined")


GATHERED = ((1, 2), (0, 4), (1, 4))
MARKS = (0, 1, 3, 5, 7, 9, 10, 11)
QUARTERS = 4


def attend_kernel(dp_size, slopes, x, weight, vectors, *refs):
    blocks, grads, refs = refs[:3], refs[3], refs[4:]
    joined, lse_ref, normed_t, attended, hidden, second, second_t, *refs = refs
    wholes, og, (first, bias_v, output_v, output_sem), refs = refs[:3], refs[3], refs[4:8], refs[8:]
    output = pltpu.make_async_copy(output_v, wholes[0], output_sem)
    wholes = [output_v, *wholes[1:]]
    step, last = pl.program_id(0), pl.num_programs(0) - 1
    p = Place(dp_size)
    gathers = [
        Gather(p, block, whole, dim, chunks, refs[3 * i : 3 * i + 3])
        for i, (block, whole, (dim, chunks)) in enumerate(zip(blocks, wholes, GATHERED))
    ]
    spread = Spread(p, grads, og, True, 4, refs[9:12])
    items = [(g, k) for g in gathers + [spread] for k in range(g.n)]
    n = x.shape[0]
    size = n // QUARTERS

    @pl.when(step == 0)
    def _():
        p.meet([p.across, p.beside, p.diagonal, p.peers[0], p.peers[1]])
        for g in gathers + [spread]:
            g.start()
        first_moves(items)
        for k in range(3):
            bias_v[:, k * D : (k + 1) * D] = vectors[10 + k : 11 + k]
        for k in range(QUARTERS):
            at = slice(k * size, (k + 1) * size)
            value = normed(x[at].astype(F32), vectors[0:1], vectors[1:2])[2]
            first[at] = value
            normed_t[:, at] = value.T

    bias = bias_v[:, pl.ds(pl.multiple_of(step * 6 * HD, 6 * HD), 6 * HD)]
    joined[...] = (bdot(first[...], weight[...], 1, 0) + bias).astype(BF)
    out = attended.at[:, pl.ds(pl.multiple_of(step * 2 * HD, 2 * HD), 2 * HD)]
    attend_step(slopes, joined, out, lse_ref)

    @pl.when(step == 1)
    def _():
        for g in gathers + [spread]:
            g.settle()

    marks = MARKS
    for i in range(len(marks) - 1):

        @pl.when(step == i)
        def _(i=i):
            for t in range(marks[i], marks[i + 1]):
                move_on(items, t)

    @pl.when(step == last)
    def _():
        t = max(marks[-1], GATHERED[0][1] + 2 * LAG)
        for i in range(marks[-1], t):
            move_on(items, i)
        gathers[0].finish()
        output.start()
        for k in range(QUARTERS):
            at = slice(k * size, (k + 1) * size)
            value = x[at].astype(F32) + bdot(attended[at], wholes[0][...], 1, 0) + vectors[2:3]
            hidden[at] = value
            value = normed(value, vectors[3:4], vectors[4:5])[2]
            second[at] = value
            second_t[:, at] = value.T
            move_on(items, t)
            t += 1
        for i in range(t, len(items) + 2 * LAG):
            move_on(items, i)
        for g in gathers[1:] + [spread]:
            g.finish()
        output.wait()


def attend(dp_size, slopes, x, weight, vectors, weights, grads):
    n, width = x.shape
    pairs = weight.shape[1] // (6 * HD)
    rows, cols = grads.shape[0] // 4, grads.shape[1]
    whole = lambda shape: pl.BlockSpec(shape, lambda h, s: (0, 0), pipeline_mode=pl.Buffered(1))
    fulls = [jax.ShapeDtypeStruct((2 * w.shape[0], 2 * w.shape[1]), BF) for w in weights]
    return pl.pallas_call(
        partial(attend_kernel, dp_size),
        grid_spec=pltpu.PrefetchScalarGridSpec(
            num_scalar_prefetch=1,
            grid=(pairs,),
            in_specs=[
                whole((n, width)),
                pl.BlockSpec((width, 6 * HD), lambda h, s: (0, h)),
                whole(vectors.shape),
            ]
            + [ANY] * 4,
            out_specs=[
                pl.BlockSpec((n, 6 * HD), lambda h, s: (0, h)),
                pl.BlockSpec((1, 2, n), lambda h, s: (h, 0, 0)),
            ]
            + [whole((width, n)), whole((n, width)), whole((n, width)), whole((n, width)), whole((width, n))]
            + [ANY] * 4,
            scratch_shapes=[
                pltpu.VMEM((n, width), BF),
                pltpu.VMEM((1, weight.shape[1]), F32),
                pltpu.VMEM(fulls[0].shape, BF),
                pltpu.SemaphoreType.DMA,
            ]
            + sum((Gather.scratch(w.shape, g[1]) for w, g in zip(weights, GATHERED)), [])
            + Spread.scratch(rows, cols, 4),
        ),
        out_shape=[
            jax.ShapeDtypeStruct((n, weight.shape[1]), BF),
            jax.ShapeDtypeStruct((pairs, 2, n), F32),
            jax.ShapeDtypeStruct((width, n), BF),
            jax.ShapeDtypeStruct((n, width), BF),
            jax.ShapeDtypeStruct((n, width), F32),
            jax.ShapeDtypeStruct((n, width), BF),
            jax.ShapeDtypeStruct((width, n), BF),
        ]
        + fulls
        + [jax.ShapeDtypeStruct((rows, 4 * cols), BF)],
        compiler_params=pltpu.CompilerParams(
            vmem_limit_bytes=58 << 20, collective_id=1, has_side_effects=True
        ),
        cost_estimate=pl.CostEstimate(
            flops=40 * n * n * HD * pairs, bytes_accessed=n * 512 * pairs * 2, transcendentals=n * n * pairs
        ),
        name="attend",
    )(slopes, x, weight, vectors, *weights, grads)


def attend_back_kernel(dp_size, span, slopes, x_ref, do_ref, lse_ref, *refs):
    (up, out, state, whole), dx_ref, finished, refs = refs[:4], refs[4], dict(zip(WEIGHTS, refs[5:7])), refs[7:]
    handed, narrow, dk_ref, dv_ref, turn, *refs = refs
    step, last = pl.program_id(0), pl.num_programs(0) - 1
    p = Place(dp_size)
    parts = chunk_list(span, (up, EARLY, FF // 2 // WIDE), (out, 0, D // 2 // WIDE))
    reduction = Reduce(p, span, parts, state, finished, handed, refs[:-3], turn=turn)
    spread = Spread(p, narrow, whole, False, 4, refs[-3:])

    @pl.when(step == 0)
    def _():
        p.meet([p.across, p.beside, p.diagonal] + p.all_rings())
        reduction.begin()
        spread.start()

    attend_back_step(slopes, x_ref, do_ref, lse_ref, dx_ref, dk_ref, dv_ref)

    @pl.when(step == 0)
    def _():
        reduction.ahead()
        reduction.resumed()
        spread.settle()

    ticks, steps = span.stop - span.start, SEQ_STEPS
    for s in range(steps):

        @pl.when(step == s)
        def _(s=s):
            reduction.run(span.start + ticks * s // steps, span.start + ticks * (s + 1) // steps)
            if s >= steps - 4:
                spread.issue(s - steps + 4)

    @pl.when(step == last)
    def _():
        reduction.finish()
        for k in range(4):
            spread.arrived(k)
        spread.finish()


SEQ_STEPS = H // 2


def attend_back(dp_size, slopes, joined, out_grads, lse, up, out, state, result):
    n, width = joined.shape
    pairs = width // (6 * HD)
    sizes = radices(dp_size)
    levels = len(sizes)
    span = split_of(levels)[1]
    block = up.shape[0] // 2
    rows, cols = 4 * result.shape[0], result.shape[1] // 4
    return pl.pallas_call(
        partial(attend_back_kernel, dp_size, span),
        grid_spec=pltpu.PrefetchScalarGridSpec(
            num_scalar_prefetch=1,
            grid=(pairs,),
            in_specs=[
                pl.BlockSpec((n, 6 * HD), lambda h, s: (0, h)),
                pl.BlockSpec((n, 2 * HD), lambda h, s: (0, h)),
                pl.BlockSpec((1, 2, n), lambda h, s: (h, 0, 0)),
            ]
            + [ANY] * 4,
            out_specs=[pl.BlockSpec((n, 6 * HD), lambda h, s: (0, h))] + [ANY] * 4,
            scratch_shapes=[pltpu.VMEM((n, HD), F32)] * 2
            + turning(span, block)
            + Reduce.scratch(span, block, sizes)
            + Spread.scratch(result.shape[0], cols, 4),
        ),
        out_shape=[jax.ShapeDtypeStruct(joined.shape, BF)]
        + blocks_like(WEIGHTS[:2], block)
        + [
            chunks_like(span.left, block),
            jax.ShapeDtypeStruct((rows, cols), BF),
        ],
        compiler_params=pltpu.CompilerParams(
            vmem_limit_bytes=60 << 20, collective_id=2, has_side_effects=True
        ),
        cost_estimate=pl.CostEstimate(
            flops=80 * n * n * HD * pairs, bytes_accessed=n * 1024 * pairs * 2, transcendentals=n * n * pairs
        ),
        name="attend_back",
    )(slopes, joined, out_grads, lse, up, out, state, result)


TILE = 512
ROWS = 256


def hidden_tile(step):
    return lax.rem(lax.axis_index("col") + 1 + lax.rem(step, 2), 2) * (FF // TILE // 2) + step // 2


def feed_kernel(
    dp_size, span, normed_in, normed_t, grads, hidden, up, down, vectors, output, attended,
    result, back, up_part, small, attended_grad, out_part, handed, *refs,
):
    total, pair, grads_t, held, output_v, bias_grad, up_bias, load_sem, *refs = refs
    act, pre_grad = pair.at[0], pair.at[1]
    step, last = pl.program_id(0), pl.num_programs(0) - 1
    p = Place(dp_size)
    reduction = Reduce(p, span, None, None, (), handed, refs, held=held)
    tiles = FF // TILE
    per, numbers = TILE // WIDE, numbering()
    tile = hidden_tile(step)
    load = pltpu.make_async_copy(hidden, total, load_sem.at[0])
    loads = [pltpu.make_async_copy(output, output_v, load_sem.at[1])] + [
        pltpu.make_async_copy(attended.at[:, pl.ds(k * TILE, TILE)], pair.at[k], load_sem.at[2 + k])
        for k in range(2)
    ]

    @pl.when(step == 0)
    def _():
        load.start()
        loads[0].start()
        p.meet([p.across, p.beside] + p.all_rings())
        back[...] = jnp.zeros_like(back)
        for k in range(FF // D):
            up_bias[:, k * D : (k + 1) * D] = vectors[6 + k : 7 + k]
        grads_t[...] = grads[...].T
        load.wait()
        loads[0].wait()

    bias = up_bias[:, pl.ds(pl.multiple_of(tile * TILE, TILE), TILE)]
    n = normed_in.shape[0]
    bias_sum = jnp.zeros((1, TILE), F32)
    a = math.sqrt(2.0 / math.pi)
    b = 0.044715 * a
    for r in range(n // ROWS):
        at = slice(r * ROWS, (r + 1) * ROWS)
        u = bdot(normed_in[at], up[...], 1, 0) + bias
        act_grad = bdot(grads[at], down[...], 1, 1)
        square = u * u
        half = 0.5 + 0.5 * jnp.tanh(u * (a + b * square))
        value = u * half
        slope = half + 2.0 * value * (1.0 - half) * (a + 3.0 * b * square)
        value = value.astype(BF)
        grad = (act_grad * slope).astype(BF)
        bias_sum = bias_sum + jnp.sum(grad.astype(F32), axis=0, keepdims=True)
        act[at] = value
        pre_grad[at] = grad
        total[at] += bdot(value, down[...], 1, 0)
        back[at] += bdot(grad, up[...], 1, 1)
    bias_grad[:, pl.ds(pl.multiple_of(tile * TILE, TILE), TILE)] = bias_sum
    part = bdot(grads_t[...], act[...], 1, 0).astype(BF)
    for k in range(per):
        held[lax.rem(per * step + k, RING)] = part[:, k * WIDE : (k + 1) * WIDE]
    part = bdot(normed_t[...], pre_grad[...], 1, 0).astype(BF)
    up_part[...] = part

    @pl.when(step < 2 * (EARLY // per))
    def _():
        for k in range(per):
            held[RING + lax.rem(step, 2) * per + k] = part[:, k * WIDE : (k + 1) * WIDE]

    def chunks_of(s):
        first = s // 2 * per
        chunks = [(numbers["down", first + k], (per * s + k) % RING) for k in range(per)]
        chunks += [(numbers["up", first + k], RING + s % 2 * per + k) for k in range(per) if first + k < EARLY]
        return s % 2, chunks

    def added(s):
        mine, chunks = chunks_of(s)
        for k, slot in chunks:
            reduction.pair(mine, k, slot)
            if not mine:
                reduction.crossing(k).start()

    for s in range(tiles):

        @pl.when(step == s)
        def _(s=s):
            mine, chunks = chunks_of(s)
            for k, slot in chunks:
                reduction.beside(mine, k, slot).start()
            if s:
                added(s - 1)
            for t in range(2 * (s - 4), 2 * (s - 3)):
                if t >= 0:
                    reduction.sum_on(t)

    @pl.when(step == last)
    def _():
        for k in range(2):
            loads[1 + k].start()
        result[...] = (total[...] + vectors[5:6]).astype(BF)
        load.start()
        load.wait()
        added(tiles - 1)
        sums = [jnp.zeros((1, back.shape[1]), F32)] * 4
        for r in range(n // ROWS):
            at = slice(r * ROWS, (r + 1) * ROWS)
            centered, scale, _ = normed(total[at], 1.0, 0.0)
            upstream = grads[at].astype(F32)
            change, gains, shifts = norm_backward(back[at], centered, scale, vectors[3:4])
            value = upstream + change
            back[at] = value
            grads_t[at] = value.astype(BF)
            attended_grad[at] = bdot(grads_t[at], output_v[...], 1, 1).astype(BF)
            new = (jnp.sum(value, axis=0, keepdims=True), gains, shifts, jnp.sum(upstream, axis=0, keepdims=True))
            sums = [x + y for x, y in zip(sums, new)]
        width = back.shape[1]
        small[...] = jnp.concatenate(
            [jnp.zeros((2, width), F32)]
            + sums
            + [bias_grad[:, k * width : (k + 1) * width] for k in range(FF // width)]
            + [jnp.zeros((SUMS - 6 - FF // width, width), F32)],
            0,
        )
        for k in range(2):
            loads[1 + k].wait()
            out_part[:, k * TILE : (k + 1) * TILE] = bdot(grads_t[...], pair[k], 0, 0).astype(BF)
        for t in range(2 * (tiles - 4), span.stop):
            reduction.sum_on(t)
        reduction.finish()


RING = 6


def feed(dp_size, normed_in, normed_t, grads, hidden, up, down, vectors, output, attended):
    n, width = normed_in.shape
    sizes = radices(dp_size)
    rows, span = width // 2, split_of(len(sizes))[0]
    whole = lambda shape: pl.BlockSpec(shape, lambda s: (0, 0), pipeline_mode=pl.Buffered(1))
    return pl.pallas_call(
        partial(feed_kernel, dp_size, span),
        grid=(FF // TILE,),
        in_specs=[
            whole((n, width)),
            whole((width, n)),
            whole((n, width)),
            ANY,
            pl.BlockSpec((width, TILE), lambda s: (0, hidden_tile(s))),
            pl.BlockSpec((TILE, width), lambda s: (hidden_tile(s), 0)),
            whole(vectors.shape),
            ANY,
            ANY,
        ],
        out_specs=[
            whole((n, width)),
            whole((n, width)),
            pl.BlockSpec((width, TILE), lambda s: (0, hidden_tile(s))),
            whole((SUMS, width)),
            whole((n, width)),
            whole((width, width)),
            ANY,
        ],
        out_shape=[
            jax.ShapeDtypeStruct((n, width), BF),
            jax.ShapeDtypeStruct((n, width), F32),
            jax.ShapeDtypeStruct((width, FF), BF),
            jax.ShapeDtypeStruct((SUMS, width), F32),
            jax.ShapeDtypeStruct((n, width), BF),
            jax.ShapeDtypeStruct((width, width), BF),
            chunks_like(span.left, rows),
        ],
        scratch_shapes=[
            pltpu.VMEM((n, width), F32),
            pltpu.VMEM((2, n, TILE), BF),
            pltpu.VMEM((width, n), BF),
            pltpu.VMEM((RING + EARLY, width, WIDE), BF),
            pltpu.VMEM((width, width), BF),
            pltpu.VMEM((1, FF), F32),
            pltpu.VMEM((1, FF), F32),
            pltpu.SemaphoreType.DMA((4,)),
        ]
        + Reduce.scratch(span, rows, sizes),
        compiler_params=pltpu.CompilerParams(
            vmem_limit_bytes=62 << 20, collective_id=4, has_side_effects=True
        ),
        cost_estimate=pl.CostEstimate(
            flops=12 * n * width * FF, bytes_accessed=6 * width * FF, transcendentals=n * FF
        ),
        name="feed",
    )(normed_in, normed_t, grads, hidden, up, down, vectors, output, attended)


def normed(values, gain, shift):
    average = jnp.mean(values, axis=1, keepdims=True)
    away = values - average
    scale = lax.rsqrt(jnp.mean(away * away, axis=1, keepdims=True) + EPSILON)
    centered = away * scale
    return centered, scale, (centered * gain + shift).astype(BF)


def norm_backward(upstream, centered, scale, gain):
    scaled = upstream * gain
    back = scale * (
        scaled
        - jnp.mean(scaled, axis=1, keepdims=True)
        - centered * jnp.mean(scaled * centered, axis=1, keepdims=True)
    )
    return back, jnp.sum(upstream * centered, axis=0, keepdims=True), jnp.sum(upstream, axis=0, keepdims=True)


def local(
    dp_size,
    tokens,
    first_gain,
    first_shift,
    joined_weight,
    query_value_bias,
    output_weight,
    output_bias,
    second_gain,
    second_shift,
    up_weight,
    up_bias,
    down_weight,
    down_bias,
    out_grad,
):
    heads = query_value_bias.shape[0] * 4
    w = D // 4
    small = jnp.concatenate(
        [
            first_gain,
            first_shift,
            output_bias,
            second_gain,
            second_shift,
            down_bias,
            up_bias,
            query_value_bias.reshape(-1),
        ]
    ).reshape(-1, 128)
    x, wj, small = front(dp_size, tokens, joined_weight, small)
    small = small.reshape(2, 2, -1)
    pair_bias = small[:, :, 10 * w :].transpose(1, 0, 2).reshape(heads, 2, HD)
    qv_bias = jnp.concatenate([pair_bias[:, :1], jnp.zeros((heads, 1, HD), F32), pair_bias[:, 1:]], axis=1)
    vectors = jnp.concatenate(
        [
            small[:, :, : 6 * w].reshape(4, 6, w).transpose(1, 0, 2).reshape(6, D),
            small[:, :, 6 * w : 10 * w].transpose(1, 0, 2).reshape(4, D),
            qv_bias.reshape(3, D),
            jnp.zeros((3, D), F32),
        ]
    )
    slopes = jnp.exp2(-8.0 * (jnp.arange(heads).astype(F32) + 1.0) / heads)

    joined, lse, normed_t, attended, hidden, second, second_t, wo, wu, wd, og = attend(
        dp_size, slopes, x, wj, vectors, (output_weight, up_weight, down_weight), out_grad
    )
    result, hidden_grad, up_part, sums_in, attended_grad, output_part, state = feed(
        dp_size, second, second_t, og, hidden, wu, wd, vectors, wo, attended
    )
    joined_grad, *begun, state, result = attend_back(
        dp_size, slopes, joined, attended_grad, lse, up_part, output_part, state, result
    )
    *sums, tokens_grad, totals = tail(
        dp_size, normed_t, joined_grad, wj, x, hidden_grad, state, vectors, sums_in, begun
    )
    down_weight_grad, up_weight_grad, output_weight_grad, joined_weight_grad = (
        total.astype(F32) for total in sums
    )
    row, col = lax.axis_index("row"), lax.axis_index("col")
    features = lax.dynamic_slice(totals, (0, (2 * row + col) * w), (6, w))
    fg, fs, obg, sg, ss, dbg = features
    ubg = lax.dynamic_index_in_dim(totals[6:10].reshape(4, -1), 2 * col + row, 0, False)
    columns = lax.dynamic_index_in_dim(totals[10:13].reshape(4, -1), 2 * col + row, 0, False)
    columns = columns.reshape(-1, 3, HD)
    qvg = jnp.concatenate([columns[:, 0], columns[:, 2]], axis=1)
    return (
        result,
        tokens_grad.astype(F32),
        fg,
        fs,
        joined_weight_grad,
        qvg,
        output_weight_grad,
        obg,
        sg,
        ss,
        up_weight_grad,
        ubg,
        down_weight_grad,
        dbg,
    )


def solution(mesh):
    feature = P(("row", "col"))
    in_specs = (
        P("dp", ("row", "col")),
        feature,
        feature,
        P("row", "col"),
        P(("col", "row"), None),
        P("col", "row"),
        feature,
        feature,
        feature,
        P("row", "col"),
        P(("col", "row")),
        P("col", "row"),
        feature,
        P("dp", ("row", "col")),
    )
    out_specs = (
        P("dp", ("row", "col")),
        P("dp", ("row", "col")),
        feature,
        feature,
        P("row", "col"),
        P(("col", "row"), None),
        P("col", "row"),
        feature,
        feature,
        feature,
        P("row", "col"),
        P(("col", "row")),
        P("col", "row"),
        feature,
    )
    return jax.shard_map(
        partial(local, mesh.shape["dp"]),
        mesh=mesh,
        in_specs=in_specs,
        out_specs=out_specs,
        check_vma=False,
    )
```
